32 devices in a mesh: rep: 4 (over y, x), fsdp: 8 (over z, core).
Axes of the slice: x: 2, y: 2, z: 4, core: 2. Of those that a mesh axis runs over, the one named last changes fastest.
Arguments:
- embed: bfloat16 [16384, 512], replicated, may hold values from -6 to 6
- first_tokens: int32 [32, 512], P(('rep', 'fsdp')), may hold values from 0 to 16383
- sample_tokens: int32 [32, 512], P(('rep', 'fsdp')), may hold values from 0 to 16383
- seq_len: int32 [32], P(('rep', 'fsdp')), may hold values from 64 to 512, as said below
- mem_len: int32 [32], P(('rep', 'fsdp')), may hold values from 192 to 1536, as said below
- memory: bfloat16 [32, 1536, 512], P(('rep', 'fsdp')), may hold values from -6 to 6
- cotangent: bfloat16 [2, 32, 512, 512], P(None, ('rep', 'fsdp')), may hold values from -6 to 6
- params: float32 [8192, 512], P('fsdp'), as said below
- vecs: float32 [11, 512], P(None, 'fsdp'), as said below
- inner_state: float32 [4, 2, 8192, 512], P('rep', None, 'fsdp'), as said below
- inner_vecs: float32 [4, 2, 11, 512], P('rep', None, None, 'fsdp'), as said below
- outer_mom: float32 [8192, 512], P('fsdp'), may hold values from -0.5 to 0.5
- outer_vecs: float32 [11, 512], P(None, 'fsdp'), may hold values from -0.5 to 0.5
Outputs:
- outputs: bfloat16 [2, 32, 512, 512], P(None, ('rep', 'fsdp'))
- grad_inputs: float32 [2, 32, 512, 512], P(None, ('rep', 'fsdp'))
- grad_memory: float32 [32, 1536, 512], P(('rep', 'fsdp'))
- param_results: float32 [3, 8192, 512], P(None, 'fsdp')
- vec_results: float32 [3, 11, 512], P(None, None, 'fsdp')
- inner_new: float32 [4, 2, 8192, 512], P('rep', None, 'fsdp')
- inner_vecs_new: float32 [4, 2, 11, 512], P('rep', None, None, 'fsdp')
The draws below stay inside these ranges and needn't reach their ends.
Inputs may be any that keep to these rules, and one draw needn't show every extreme that they name: `seq_len`: some sequence has exactly 512 tokens. `mem_len`: some sequence has exactly 1536 valid memory slots. `params`: finite values. `vecs`: finite values. `inner_state`: second moments (index 1 of the second dimension) are positive. `inner_vecs`: second moments (index 1 of the second dimension) are positive.
All inputs are finite; a program needn't handle non-finite values.
Results may differ from the reference program's by a relative error of at most 0.024.
The reference program's roundings to bfloat16 on the way count: a program that leaves them out, or rounds other values in their place, can miss the bound.
Values may be sent and summed in bfloat16 or wider, within the bound.
No kernel may reach another device: no remote copies, remote signals or barrier semaphores. Data moves between devices by JAX's collectives and lax.ppermute only.
A program may use at most 320 MiB of HBM per device.

```python
import math
import jax
import jax.numpy as jnp
import numpy as np
from jax import lax

D = 512
HEADS = 8
HSIZE = 64
FF = 2048
VOCAB = 16384
LEN = 512
MEM = 1536
STEP = 8
REPS = 4
GROUP_SEQS = 8
SEQS = 32
GROUP_TOK = 4096
ROWS = 8192
NVEC = 11
N_REP = 4


def draw_lengths(key, how_many, longest):
    first_key, second_key = jax.random.split(key)
    lengths = jax.random.randint(first_key, (how_many,), longest // 8, longest + 1)
    chosen = jax.random.randint(second_key, (), 0, how_many)
    return lengths.at[chosen].set(longest).astype(jnp.int32)


def draw_seq_len(key, part):
    return draw_lengths(jax.random.fold_in(key, 101), SEQS, LEN)


def draw_mem_len(key, part):
    return draw_lengths(jax.random.fold_in(key, 202), SEQS, MEM)


def row_scales(factors, tail_up, tail_down):
    pieces = [jnp.full((D,), factor_item, jnp.float32) for factor_item in factors]
    pieces.append(jnp.full((FF,), tail_up, jnp.float32))
    pieces.append(jnp.full((FF,), tail_down, jnp.float32))
    return jnp.concatenate(pieces)


def weight_scales():
    inverse = 1.0 / math.sqrt(D)
    factors = [inverse, inverse, inverse, math.sqrt(LEN / (6.0 * D)), inverse, inverse, inverse, math.sqrt(MEM / (6.0 * D))]
    return row_scales(factors, inverse, 1.0 / math.sqrt(FF))


def gradient_scales():
    base_size = math.sqrt(1.2 * GROUP_TOK)
    factors = [0.3, 0.3, 1.0, math.sqrt(6.0 / LEN), 0.3, 0.2, 0.6, math.sqrt(6.0 / MEM)]
    return base_size * row_scales(factors, 0.35, 0.7)


def draw_params(key, part):
    noise = jnp.clip(jax.random.normal(jax.random.fold_in(key, 303), (ROWS, D), jnp.float32), -5.0, 5.0)
    return noise * weight_scales()[:, None]


def draw_vecs(key, part):
    noise = jnp.clip(jax.random.normal(jax.random.fold_in(key, 404), (NVEC, D), jnp.float32), -4.0, 4.0)
    spread_rows = jnp.concatenate([jnp.full((3,), 0.1, jnp.float32), jnp.full((NVEC - 3,), 0.3, jnp.float32)])
    offset_rows = jnp.concatenate([jnp.ones((3,), jnp.float32), jnp.zeros((NVEC - 3,), jnp.float32)])
    return offset_rows[:, None] + spread_rows[:, None] * noise


def moment_pair(key, shape, scales):
    first_key, second_key = jax.random.split(key)
    moment_one = jnp.clip(jax.random.normal(first_key, shape, jnp.float32), -5.0, 5.0) * (scales / 9.0)
    factor = jnp.exp(jax.random.uniform(second_key, shape, jnp.float32, math.log(0.5), math.log(2.0)))
    second = 0.001 * 2.0 * factor * scales * scales
    return jnp.stack([moment_one, second], axis=1)


def draw_inner_state(key, part):
    scales = gradient_scales()[None, :, None]
    return moment_pair(jax.random.fold_in(key, 505), (REPS, ROWS, D), scales)


def draw_inner_vecs(key, part):
    scales = 0.5 * math.sqrt(1.2 * GROUP_TOK)
    return moment_pair(jax.random.fold_in(key, 606), (REPS, NVEC, D), scales)


def set_ends(entries, key, least, high):
    extent = entries.shape
    spot = [jax.random.randint(jax.random.fold_in(key, axis), (), 0, extent[axis]) for axis in range(len(extent))]
    entries = entries.at[tuple(spot)].set(least)
    longest = extent.index(max(extent))
    spot[longest] = (spot[longest] + 1) % extent[longest]
    return entries.at[tuple(spot)].set(high)


def steps_of(key, shape, shards, least, largest):
    level = 1.0
    for dim, parts in shards:
        steps = jax.random.uniform(jax.random.fold_in(jax.random.fold_in(key, 6), dim), (parts,), jnp.float32, least / len(shards), largest / len(shards))
        level = level * jnp.repeat(jnp.exp(steps), shape[dim] // parts).reshape((-1,) + (1,) * (len(shape) - 1 - dim))
    return level


def rank_bounds(number_of, skew):
    loads = [(1 << 20) // math.isqrt(standing ** skew) + 1 for standing in range(1, number_of + 1)]
    scale = 1 + sum(loads) // (1 << 30)
    return np.cumsum(np.array([max(1, weight // scale) for weight in loads]))


def ranked_ids(key, shape, count, skew):
    listing = rank_bounds(count, skew)
    lot = jax.random.randint(jax.random.fold_in(key, 1), shape, 0, int(listing[count - 1]))
    rank = jnp.searchsorted(jnp.asarray(listing, jnp.int32), lot, side="right")
    return jax.random.permutation(jax.random.fold_in(key, 2), count)[rank].astype(jnp.int32)


def scatter_about(key, dims, scale, limit, cuts=(), dtype=jnp.bfloat16):
    values = jax.random.normal(key, dims, jnp.float32) * scale
    if len(cuts) > 0:
        values = steps_of(key, dims, cuts, -0.22, 0.18) * values
    return jnp.clip(values, min=-limit, max=limit).astype(dtype)


def setup_inputs(seed: int = 0) -> dict:
    key_of = jax.random.split(jax.random.key(seed), 14)
    return {
        "embed": scatter_about(key_of[0], (VOCAB, D), 1.0, 6.0),
        "first_tokens": set_ends(ranked_ids(key_of[1], (SEQS, LEN), VOCAB, 2), jax.random.fold_in(key_of[1], 3), 0, VOCAB - 1).astype(jnp.int32),
        "sample_tokens": set_ends(ranked_ids(key_of[2], (SEQS, LEN), VOCAB, 2), jax.random.fold_in(key_of[2], 3), 0, VOCAB - 1).astype(jnp.int32),
        "seq_len": draw_seq_len(jax.random.fold_in(key_of[13], 71), 0),
        "mem_len": draw_mem_len(jax.random.fold_in(key_of[13], 71), 0),
        "memory": scatter_about(key_of[5], (SEQS, MEM, D), 1.0, 6.0, ((0, 32),)),
        "cotangent": scatter_about(key_of[6], (2, SEQS, LEN, D), 1.0, 6.0, ((1, 32),)),
        "params": draw_params(jax.random.fold_in(key_of[13], 71), 0),
        "vecs": draw_vecs(jax.random.fold_in(key_of[13], 71), 0),
        "inner_state": draw_inner_state(jax.random.fold_in(key_of[13], 71), 0),
        "inner_vecs": draw_inner_vecs(jax.random.fold_in(key_of[13], 71), 0),
        "outer_mom": scatter_about(key_of[11], (ROWS, D), 0.035, 0.5, ((0, 8),), jnp.float32),
        "outer_vecs": scatter_about(key_of[12], (NVEC, D), 0.035, 0.5, ((1, 8),), jnp.float32),
    }


@jax.custom_vjp
def low(v):
    return lax.optimization_barrier(v.astype(jnp.bfloat16)).astype(jnp.float32)

@jax.custom_vjp
def low_back(v):
    return v

def low_keep(v):
    return (low(v), None)

def low_pass(kept, grad):
    return (grad,)

def back_keep(v):
    return (v, None)

def back_low(kept, grad):
    return (low(grad),)
low.defvjp(low_keep, low_pass)
low_back.defvjp(back_keep, back_low)
norm_epsilon = 1e-05
beta_first = 0.9
beta_second = 0.999
adam_epsilon = 1e-08
rate_inner = 0.1
rate_outer = 0.7
outer_push = 0.9
decay_rate = 0.01
highest = lax.Precision.HIGHEST

def matmul(left, right):
    return jnp.dot(left, right, precision=highest, preferred_element_type=jnp.float32)

def layer_norm(values_in, gain_row, bias_row):
    centre = values_in - lax.optimization_barrier(jnp.mean(values_in, axis=-1, keepdims=True))
    spread = lax.optimization_barrier(jnp.mean(centre * centre, axis=-1, keepdims=True))
    return centre * lax.rsqrt(spread + norm_epsilon) * gain_row + bias_row

def attend(queries, key_rows, values, key_mask):
    row_count = queries.shape[0]
    split_query = queries.reshape(row_count, HEADS, HSIZE)
    split_keys = key_rows.reshape(key_rows.shape[0], HEADS, HSIZE)
    split_values = values.reshape(values.shape[0], HEADS, HSIZE)
    scores = jnp.einsum('qhd,khd->hqk', split_query, split_keys, precision=highest) / math.sqrt(HSIZE)
    scores = low_back(scores)
    scores = jnp.where(key_mask[None, None, :], scores, -1e+30)
    row_peak = lax.optimization_barrier(jnp.max(scores, axis=-1, keepdims=True))
    exponent = jnp.exp(scores - row_peak)
    probabilities = low(exponent / lax.optimization_barrier(jnp.sum(exponent, axis=-1, keepdims=True)))
    mixture = jnp.einsum('hqk,khd->qhd', probabilities, split_values, precision=highest)
    return mixture.reshape(row_count, HEADS * HSIZE)

def forward(params_f, vecs_f, inputs, memory_f, length, mem_length):
    weights = low(params_f)
    vectors = low(vecs_f)
    blocks = [weights[slot_index * D:(slot_index + 1) * D] for slot_index in range(8)]
    weight_up = weights[8 * D:8 * D + FF].reshape(D, FF)
    weight_down = weights[8 * D + FF:]
    hidden_bias = vectors[7:].reshape(FF)
    key_mask = jnp.arange(LEN) < length
    mem_mask = jnp.arange(MEM) < mem_length
    normed = low(layer_norm(inputs, vectors[0], vectors[3]))
    queries = low(low_back(matmul(normed, blocks[0])))
    key_rows = low(low_back(matmul(normed, blocks[1])))
    values = low(low_back(matmul(normed, blocks[2])))
    mixture = low(low_back(attend(queries, key_rows, values, key_mask)))
    after = inputs + low_back(matmul(mixture, blocks[3]))
    cross_in = low(layer_norm(after, vectors[1], vectors[4]))
    query_two = low(low_back(matmul(cross_in, blocks[4])))
    keys_two = low(low_back(matmul(memory_f, blocks[5])))
    values_two = low(low_back(matmul(memory_f, blocks[6])))
    mixture_two = low(low_back(attend(query_two, keys_two, values_two, mem_mask)))
    middle = after + low_back(matmul(mixture_two, blocks[7]))
    feed_in = low(layer_norm(middle, vectors[2], vectors[5]))
    pre_act = low_back(matmul(feed_in, weight_up) + hidden_bias)
    active = low(jnp.maximum(pre_act, 0.0))
    return middle + low_back(matmul(active, weight_down) + vectors[6])

def inner_update(weight, gradient, moment_one, second, shrink):
    moment_new = beta_first * moment_one + (1.0 - beta_first) * gradient
    second_new = beta_second * second + (1.0 - beta_second) * gradient * gradient
    moment_hat = moment_new / (1.0 - beta_first ** STEP)
    second_hat = second_new / (1.0 - beta_second ** STEP)
    local_weight = weight - rate_inner * (moment_hat / (jnp.sqrt(second_hat) + adam_epsilon) + shrink * weight)
    return (moment_new, second_new, weight - local_weight)

def reference(embed, first_tokens, sample_tokens, seq_len, mem_len, memory, cotangent, params, vecs, inner_state, inner_vecs, outer_mom, outer_vecs):

    def one_sequence(carried, seq_index):
        weight_sum, vector_sum = carried
        memory_f = memory[seq_index].astype(jnp.float32)
        length = seq_len[seq_index]
        mem_length = mem_len[seq_index]
        row_mask = (jnp.arange(LEN) < length).astype(jnp.float32)
        results = []
        input_grads = []
        memory_grad = jnp.zeros((MEM, D), jnp.float32)
        for pass_index, tokens in enumerate((first_tokens, sample_tokens)):
            inputs = embed[tokens[seq_index]].astype(jnp.float32)

            def closed(weights_in, vectors_in, inputs_in, memory_in):
                return forward(weights_in, vectors_in, inputs_in, memory_in, length, mem_length)
            result, pullback = jax.vjp(closed, params, vecs, inputs, memory_f)
            back_rows = cotangent[pass_index, seq_index].astype(jnp.float32) * row_mask[:, None]
            grad_weights, grad_vectors, grad_in, grad_mem = pullback(back_rows)
            weight_sum = weight_sum + grad_weights
            vector_sum = vector_sum + grad_vectors
            memory_grad = memory_grad + grad_mem
            results.append(result.astype(jnp.bfloat16))
            input_grads.append(grad_in)
        return ((weight_sum, vector_sum), (jnp.stack(results), jnp.stack(input_grads), memory_grad))
    out_list = []
    grad_list = []
    memory_list = []
    moments = []
    vector_moments = []
    delta_sum = jnp.zeros((ROWS, D), jnp.float32)
    delta_vec_sum = jnp.zeros((NVEC, D), jnp.float32)
    for replica in range(N_REP):
        indices = (jnp.arange(GROUP_SEQS) + replica * GROUP_SEQS).astype(jnp.int32)
        start = (jnp.zeros((ROWS, D), jnp.float32), jnp.zeros((NVEC, D), jnp.float32))
        (weight_sum, vector_sum), (stacked_out, stacked_grad, stacked_memory) = lax.scan(one_sequence, start, indices)
        out_list.append(stacked_out)
        grad_list.append(stacked_grad)
        memory_list.append(stacked_memory)
        moment_w, second_w, delta_w = inner_update(params, weight_sum, inner_state[replica, 0], inner_state[replica, 1], decay_rate)
        moment_v, second_v, delta_v = inner_update(vecs, vector_sum, inner_vecs[replica, 0], inner_vecs[replica, 1], 0.0)
        moments.append(jnp.stack([moment_w, second_w]))
        vector_moments.append(jnp.stack([moment_v, second_v]))
        delta_sum = delta_sum + delta_w
        delta_vec_sum = delta_vec_sum + delta_v
    mean_w = delta_sum / N_REP
    mean_v = delta_vec_sum / N_REP
    momentum_w = outer_push * outer_mom + mean_w
    momentum_v = outer_push * outer_vecs + mean_v
    new_w = params - rate_outer * (mean_w + outer_push * momentum_w)
    new_v = vecs - rate_outer * (mean_v + outer_push * momentum_v)
    outputs = jnp.transpose(jnp.concatenate(out_list, axis=0), (1, 0, 2, 3))
    grad_inputs = jnp.transpose(jnp.concatenate(grad_list, axis=0), (1, 0, 2, 3))
    grad_memory = jnp.concatenate(memory_list, axis=0)
    return (outputs, grad_inputs, grad_memory, jnp.stack([new_w, mean_w, momentum_w]), jnp.stack([new_v, mean_v, momentum_v]), jnp.stack(moments), jnp.stack(vector_moments))
```

```python
import functools
import math

import jax
import jax.numpy as jnp
from jax import lax
from jax.experimental import pallas as pl
from jax.experimental.pallas import tpu as pltpu
from jax.sharding import PartitionSpec as P

HEADS = 8
STEP = 8
PASSES = 2
AUG = 80
norm_epsilon = 1e-05
beta_first = 0.9
beta_second = 0.999
adam_epsilon = 1e-08
rate_inner = 0.1
rate_outer = 0.7
outer_push = 0.9
decay_rate = 0.01

BF = jnp.bfloat16
F32 = jnp.float32
NN = (((1,), (0,)), ((), ()))
NT = (((1,), (1,)), ((), ()))
TN = (((0,), (0,)), ((), ()))
VMEM_LIMIT = 60 << 20


def dot(left, right, dims):
    return lax.dot_general(left, right, dims, preferred_element_type=F32)


def normalise(values):
    centre = values - jnp.mean(values, axis=-1, keepdims=True)
    spread = jnp.mean(centre * centre, axis=-1, keepdims=True)
    inverse = lax.rsqrt(spread + norm_epsilon)
    return centre * inverse, inverse


def norm_back(grad_out, gain_row, normal, inverse):
    grad_normal = grad_out * gain_row
    mean_grad = jnp.mean(grad_normal, axis=-1, keepdims=True)
    mean_proj = jnp.mean(grad_normal * normal, axis=-1, keepdims=True)
    grad_in = inverse * (grad_normal - mean_grad - normal * mean_proj)
    return grad_in, jnp.sum(grad_out * normal, axis=0, keepdims=True), jnp.sum(grad_out, axis=0, keepdims=True)


def thirds(row):
    high = row.astype(BF)
    rest = row - high.astype(F32)
    middle = rest.astype(BF)
    low = (rest - middle.astype(F32)).astype(BF)
    return high.astype(F32), middle.astype(F32), low.astype(F32)


def tail_rows(width, rows):
    place = lax.broadcasted_iota(jnp.int32, (AUG - 64, width), 0)
    tail = jnp.zeros((AUG - 64, width), F32)
    for number, row in enumerate(rows):
        tail = jnp.where(place == number, row, tail)
    return tail.astype(BF)


def put_heads(target, matrix_t, scale, tail):
    low = matrix_t.astype(BF)
    if scale != 1.0:
        low = low * BF(scale)
    size = low.shape[0] // HEADS
    for head in range(HEADS):
        target[head, :size, :] = low[head * size : (head + 1) * size]
        target[head, size:, :] = tail


def key_tail(width, count, period):
    spot = lax.broadcasted_iota(jnp.int32, (1, width), 1) % period
    bias = jnp.where(spot < count, 0.0, -1e30)
    return tail_rows(width, [bias, 1.0, 1.0, 1.0])


def attend_forward(units, where_of, block, q_ref, k_ref, v_ref, o_ref, s_a, s_b, m_a, m_b):
    keys = s_a.shape[0]

    def scores(step, store, peak):
        head, first, key_first = where_of(jnp.minimum(step, units - 1))
        value = dot(k_ref[head, :, pl.ds(key_first, keys)], q_ref[head, :, pl.ds(first, block)], TN)
        store[...] = value
        peak[...] = jnp.broadcast_to(jnp.max(value, axis=0, keepdims=True), peak.shape)

    def finish(step, store, peak):
        head, first, key_first = where_of(step)
        top = peak[0:1, :]
        weight = jnp.exp(store[...] - top).astype(BF)
        mixed = dot(v_ref[head, :, pl.ds(key_first, keys)], weight, NN)
        total = mixed[64:65, :]
        o_ref[pl.ds(pl.multiple_of(head * 64, 64), 64), pl.ds(first, block)] = (mixed[:64] * (1.0 / total)).astype(BF)
        high, middle, low = thirds(top + jnp.log(total))
        q_ref[head, 64:, pl.ds(first, block)] = tail_rows(block, [1.0, -high, -middle, -low])

    scores(0, s_a, m_a)

    def body(pair, carry):
        step = 2 * pair
        scores(step + 1, s_b, m_b)
        finish(step, s_a, m_a)
        scores(step + 2, s_a, m_a)
        finish(step + 1, s_b, m_b)
        return carry

    lax.fori_loop(0, units // 2 - 1, body, 0)
    step = units - 2
    scores(step + 1, s_b, m_b)
    finish(step, s_a, m_a)
    finish(step + 1, s_b, m_b)


def attend_backward(head, first, block, key_first, keys, q_ref, k_ref, v_ref, d_ref):
    here = pl.ds(first, block)
    there = pl.ds(key_first, keys)
    query = q_ref[head, :, here]
    grad = d_ref[head, :, here]
    key_t = k_ref[head, :, there]
    weight = jnp.exp(dot(query, key_t, TN))
    grad_scores = (weight * dot(grad, v_ref[head, :, there], TN)).astype(BF)
    grad_value = dot(grad[:64], weight.astype(BF), NN)
    grad_key = dot(query[:64], grad_scores, NN)
    grad_query = dot(key_t[:64], grad_scores, NT) * 0.125
    return grad_query.astype(BF), grad_key, grad_value


def put_grads(d_ref, grad_t, o_ref):
    low = grad_t.astype(BF)
    for head in range(HEADS):
        part = low[head * 64 : (head + 1) * 64]
        both = part.astype(F32) * o_ref[head * 64 : (head + 1) * 64, :].astype(F32)
        high, middle, rest = thirds(jnp.sum(both, axis=0, keepdims=True))
        d_ref[head, :64, :] = part
        d_ref[head, 64:, :] = tail_rows(low.shape[1], [-high, -middle, -rest])


def self_forward(lens, x_ref, w_ref, vec_ref, q_ref, k_ref, v_ref, o_ref, h_ref, s_a, s_b, m_a, m_b):
    width = x_ref.shape[1]
    rows = x_ref.shape[0]
    length = rows // PASSES
    x = x_ref[...].astype(F32)
    normal, _ = normalise(x)
    low = (normal * vec_ref[0:1, :] + vec_ref[3:4, :]).astype(BF)
    ones = tail_rows(rows, [1.0, 1.0, 1.0])
    first = tail_rows(rows, [1.0])
    put_heads(q_ref, dot(w_ref[0:width, :], low, (((0,), (1,)), ((), ()))), 0.125, first)
    put_heads(k_ref, dot(w_ref[width : 2 * width, :], low, (((0,), (1,)), ((), ()))), 1.0, key_tail(rows, lens[0], length))
    put_heads(v_ref, dot(w_ref[2 * width : 3 * width, :], low, (((0,), (1,)), ((), ()))), 1.0, ones)

    def where_of(step):
        place = pl.multiple_of((step % PASSES) * length, length)
        return step // PASSES, place, place

    attend_forward(HEADS * PASSES, where_of, length, q_ref, k_ref, v_ref, o_ref, s_a, s_b, m_a, m_b)
    h_ref[...] = x_ref[...].astype(F32) + dot(o_ref[...], w_ref[3 * width : 4 * width, :], TN)


def cross_forward(lens, h_ref, w_ref, mem_ref, vec_ref, q_ref, k_ref, v_ref, o_ref, out_ref, s_a, s_b, m_a, m_b):
    width = h_ref.shape[1]
    rows = h_ref.shape[0]
    slots = mem_ref.shape[0]
    block = s_a.shape[1]
    normal, _ = normalise(h_ref[...])
    low = (normal * vec_ref[1:2, :] + vec_ref[4:5, :]).astype(BF)
    memory = mem_ref[...]
    put_heads(q_ref, dot(w_ref[0:width, :], low, (((0,), (1,)), ((), ()))), 0.125, tail_rows(rows, [1.0]))
    put_heads(k_ref, dot(w_ref[width : 2 * width, :], memory, (((0,), (1,)), ((), ()))), 1.0, key_tail(slots, lens[1], slots))
    put_heads(v_ref, dot(w_ref[2 * width : 3 * width, :], memory, (((0,), (1,)), ((), ()))), 1.0, tail_rows(slots, [1.0, 1.0, 1.0]))
    pieces = rows // block

    def where_of(step):
        return step // pieces, pl.multiple_of((step % pieces) * block, block), 0

    attend_forward(HEADS * pieces, where_of, block, q_ref, k_ref, v_ref, o_ref, s_a, s_b, m_a, m_b)
    out_ref[...] = h_ref[...] + dot(o_ref[...], w_ref[3 * width : 4 * width, :], TN)


def feed(shards, lens, h_ref, up_ref, down_ref, vec_ref, cot_ref, y_ref, dh_ref, gup_ref, gdown_ref, gv_ref, up_s, e_s, n_s, y_s, de_s):
    width = h_ref.shape[1]
    rows = h_ref.shape[0]
    hidden = down_ref.shape[0]
    parts = hidden // width
    piece = hidden // shards // parts
    for shard in range(shards):
        for part in range(parts):
            begin = (shard * parts + part) * piece
            up_s[part, shard * piece : (shard + 1) * piece, :] = up_ref[begin : begin + piece, :]
    normal, inverse = normalise(h_ref[...])
    n_s[...] = normal
    e_s[...] = (normal * vec_ref[2:3, :] + vec_ref[5:6, :]).astype(BF)
    spot = lax.broadcasted_iota(jnp.int32, (rows, 1), 0) % (rows // PASSES)
    cot = jnp.where(spot < lens[0], cot_ref[...].astype(F32), 0.0)
    df = cot.astype(BF)
    y_s[...] = h_ref[...] + vec_ref[6:7, :]
    de_s[...] = jnp.zeros_like(de_s)
    gv_ref[...] = jnp.zeros_like(gv_ref)

    def body(part, carry):
        place = pl.multiple_of(part * width, width)
        down = down_ref[pl.ds(place, width), :]
        up = up_s[part]
        pre = dot(e_s[...], up, NN) + vec_ref[pl.ds(7 + part, 1), :]
        active = jnp.maximum(pre, 0.0).astype(BF)
        y_s[...] += dot(active, down, NN)
        gdown_ref[pl.ds(place, width), :] = dot(active, df, TN).astype(BF)
        du = jnp.where(pre > 0, dot(df, down, NT), 0.0).astype(BF)
        gv_ref[pl.ds(7 + part, 1), :] = jnp.sum(du.astype(F32), axis=0, keepdims=True)
        gup = dot(e_s[...], du, TN).astype(BF)
        for shard in range(shards):
            begin = pl.multiple_of((shard * parts + part) * piece, piece)
            gup_ref[pl.ds(begin, piece), :] = gup[shard * piece : (shard + 1) * piece, :]
        de_s[...] += dot(du, up, NT)
        return carry

    lax.fori_loop(0, parts, body, 0)
    y_ref[...] = y_s[...].astype(BF)
    gv_ref[6:7, :] = jnp.sum(cot, axis=0, keepdims=True)
    back, gain, shift = norm_back(de_s[...], vec_ref[2:3, :], n_s[...], inverse)
    gv_ref[2:3, :] = gain
    gv_ref[5:6, :] = shift
    dh_ref[...] = cot + back


def cross_backward(dh2_ref, w_ref, q_ref, k_ref, v_ref, o_ref, h_ref, mem_ref, vec_ref, g_ref, gmem_ref, dh_ref, gv_ref, d_s, dq_s, dk_s, dv_s, sk, sv):
    width = h_ref.shape[1]
    rows = h_ref.shape[0]
    slots = mem_ref.shape[0]
    block = rows // PASSES
    dz = dh2_ref[...].astype(BF)
    g_ref[3 * width : 4 * width, :] = dot(o_ref[...], dz, NN).astype(BF)
    put_grads(d_s, dot(w_ref[3 * width : 4 * width, :], dz, NT), o_ref)

    def body(head, carry):
        place = pl.ds(pl.multiple_of(head * 64, 64), 64)
        for piece in range(rows // block):
            dq, dk, dv = attend_backward(head, piece * block, block, 0, slots, q_ref, k_ref, v_ref, d_s)
            dq_s[place, piece * block : (piece + 1) * block] = dq
            if piece == 0:
                sk[...] = dk
                sv[...] = dv
            else:
                dk_s[place, :] = (sk[...] + dk).astype(BF)
                dv_s[place, :] = (sv[...] + dv).astype(BF)
        return carry

    lax.fori_loop(0, HEADS, body, 0)
    memory = mem_ref[...]
    dk = dk_s[...].T
    g_ref[width : 2 * width, :] = dot(memory, dk, TN).astype(BF)
    gmem_ref[...] = dot(dk, w_ref[width : 2 * width, :], NT)
    dv = dv_s[...].T
    g_ref[2 * width : 3 * width, :] = dot(memory, dv, TN).astype(BF)
    gmem_ref[...] += dot(dv, w_ref[2 * width : 3 * width, :], NT)
    normal, inverse = normalise(h_ref[...])
    low = (normal * vec_ref[1:2, :] + vec_ref[4:5, :]).astype(BF)
    dq = dq_s[...].T
    g_ref[0:width, :] = dot(low, dq, TN).astype(BF)
    back, gain, shift = norm_back(dot(dq, w_ref[0:width, :], NT), vec_ref[1:2, :], normal, inverse)
    gv_ref[...] = jnp.zeros_like(gv_ref)
    gv_ref[1:2, :] = gain
    gv_ref[4:5, :] = shift
    dh_ref[...] = dh2_ref[...] + back


def self_backward(dh_ref, w_ref, q_ref, k_ref, v_ref, o_ref, x_ref, vec_ref, g_ref, gin_ref, gv_ref, d_s, dq_s, dk_s, dv_s):
    width = x_ref.shape[1]
    rows = x_ref.shape[0]
    length = rows // PASSES
    dz = dh_ref[...].astype(BF)
    g_ref[3 * width : 4 * width, :] = dot(o_ref[...], dz, NN).astype(BF)
    put_grads(d_s, dot(w_ref[3 * width : 4 * width, :], dz, NT), o_ref)

    def body(head, carry):
        place = pl.ds(pl.multiple_of(head * 64, 64), 64)
        for number in range(PASSES):
            begin = number * length
            dq, dk, dv = attend_backward(head, begin, length, begin, length, q_ref, k_ref, v_ref, d_s)
            dq_s[place, begin : begin + length] = dq
            dk_s[place, begin : begin + length] = dk.astype(BF)
            dv_s[place, begin : begin + length] = dv.astype(BF)
        return carry

    lax.fori_loop(0, HEADS, body, 0)
    normal, inverse = normalise(x_ref[...].astype(F32))
    low = (normal * vec_ref[0:1, :] + vec_ref[3:4, :]).astype(BF)
    total = None
    for number, store in enumerate((dq_s, dk_s, dv_s)):
        grad = store[...].T
        g_ref[number * width : (number + 1) * width, :] = dot(low, grad, TN).astype(BF)
        part = dot(grad, w_ref[number * width : (number + 1) * width, :], NT)
        total = part if total is None else total + part
    back, gain, shift = norm_back(total, vec_ref[0:1, :], normal, inverse)
    gv_ref[...] = jnp.zeros_like(gv_ref)
    gv_ref[0:1, :] = gain
    gv_ref[3:4, :] = shift
    gin_ref[...] = dh_ref[...] + back


VM = pl.BlockSpec(memory_space=pltpu.VMEM)
SM = pl.BlockSpec(memory_space=pltpu.SMEM)


def call(body, name, ins, outs, scratch):
    shapes = tuple(jax.ShapeDtypeStruct(shape, kind) for shape, kind in outs)
    return pl.pallas_call(
        body,
        name=name,
        out_shape=shapes,
        in_specs=ins,
        out_specs=tuple(VM for _ in outs),
        scratch_shapes=[pltpu.VMEM(shape, kind) for shape, kind in scratch],
        compiler_params=pltpu.CompilerParams(vmem_limit_bytes=VMEM_LIMIT),
    )


def local_work(blocks, vectors, shards, x, memory, cot, lens):
    rows, width = x.shape
    slots = memory.shape[0]
    length = rows // PASSES
    heads_n = ((HEADS, AUG, rows), BF)
    heads_m = ((HEADS, AUG, slots), BF)
    flat_n = ((width, rows), BF)
    full = ((rows, width), F32)
    block_g = (blocks[0].shape, BF)
    vec_g = (vectors.shape, F32)
    peak = ((8, length), F32)
    qs, ks, vs, o_self, h = call(
        self_forward, "self_forward", [SM] + [VM] * 3,
        [heads_n, heads_n, heads_n, flat_n, full],
        [((length, length), F32)] * 2 + [peak] * 2,
    )(lens, x, blocks[0], vectors)
    qc, kc, vc, o_cross, h2 = call(
        cross_forward, "cross_forward", [SM] + [VM] * 4,
        [heads_n, heads_m, heads_m, flat_n, full],
        [((slots, length), F32)] * 2 + [peak] * 2,
    )(lens, h, blocks[1], memory, vectors)
    parts = blocks[3].shape[0] // width
    y, dh2, g_up, g_down, gv3 = call(
        functools.partial(feed, shards), "feed", [SM] + [VM] * 5,
        [((rows, width), BF), full, block_g, block_g, vec_g],
        [((parts, width, width), BF), ((rows, width), BF), full, full, full],
    )(lens, h2, blocks[2], blocks[3], vectors, cot)
    g_cross, g_mem, dh, gv2 = call(
        cross_backward, "cross_backward", [VM] * 9,
        [block_g, (memory.shape, F32), full, vec_g],
        [heads_n, flat_n, ((width, slots), BF), ((width, slots), BF), ((64, slots), F32), ((64, slots), F32)],
    )(dh2, blocks[1], qc, kc, vc, o_cross, h, memory, vectors)
    g_self, g_in, gv1 = call(
        self_backward, "self_backward", [VM] * 8,
        [block_g, full, vec_g],
        [heads_n, flat_n, flat_n, flat_n],
    )(dh, blocks[0], qs, ks, vs, o_self, x, vectors)
    return y, g_in, g_mem, (g_self, g_cross, g_up, g_down), gv1 + gv2 + gv3


def inner_update(weight, gradient, moment_one, second, shrink):
    moment_new = beta_first * moment_one + (1.0 - beta_first) * gradient
    second_new = beta_second * second + (1.0 - beta_second) * gradient * gradient
    moment_hat = moment_new / (1.0 - beta_first**STEP)
    second_hat = second_new / (1.0 - beta_second**STEP)
    local_weight = weight - rate_inner * (
        moment_hat / (jnp.sqrt(second_hat) + adam_epsilon) + shrink * weight
    )
    return (moment_new, second_new, weight - local_weight)


def per_device(embed, first_tokens, sample_tokens, seq_len, mem_len, memory, cotangent, params, vecs, inner_state, inner_vecs, outer_mom, outer_vecs):
    groups = lax.axis_size("fsdp")
    share, width = params.shape
    hidden = 4 * width
    me = lax.axis_index("fsdp")
    shards = hidden // share
    own_up = (me >= 2 * hidden // share) & (me < 3 * hidden // share)

    def part_first(rows):
        return rows.reshape(share // 4, 4, width).transpose(1, 0, 2).reshape(share, width)

    def part_last(rows):
        return rows.reshape(4, share // 4, width).transpose(1, 0, 2).reshape(share, width)

    low = params.astype(BF)
    low = jnp.where(own_up, part_first(low), low)
    gathered = lax.all_gather(low, "fsdp", axis=0, tiled=True)
    vectors = lax.all_gather(vecs.astype(BF), "fsdp", axis=1, tiled=True).astype(F32)
    vectors = jnp.pad(vectors, ((0, 16 - vectors.shape[0]), (0, 0)))
    blocks = [gathered[i * hidden : (i + 1) * hidden] for i in range(4)]
    x = embed[jnp.concatenate([first_tokens[0], sample_tokens[0]])]
    lens = jnp.stack([seq_len[0], mem_len[0]])
    length = first_tokens.shape[1]
    cot = cotangent.reshape(PASSES * length, width)
    y, g_in, g_mem, grads, gv = local_work(blocks, vectors, shards, x, memory[0], cot, lens)
    grad_w = lax.psum_scatter(jnp.concatenate(grads, axis=0), "fsdp", scatter_dimension=0, tiled=True).astype(F32)
    grad_w = jnp.where(own_up, part_last(grad_w), grad_w)
    grad_v = lax.psum_scatter(gv[: vecs.shape[0]], "fsdp", scatter_dimension=1, tiled=True)
    moment_w, second_w, delta_w = inner_update(params, grad_w, inner_state[0, 0], inner_state[0, 1], decay_rate)
    moment_v, second_v, delta_v = inner_update(vecs, grad_v, inner_vecs[0, 0], inner_vecs[0, 1], 0.0)
    replicas = lax.axis_size("rep")
    mean_w = lax.psum(delta_w.astype(BF), "rep").astype(F32) / replicas
    mean_v = lax.psum(delta_v.astype(BF), "rep").astype(F32) / replicas
    momentum_w = outer_push * outer_mom + mean_w
    momentum_v = outer_push * outer_vecs + mean_v
    new_w = params - rate_outer * (mean_w + outer_push * momentum_w)
    new_v = vecs - rate_outer * (mean_v + outer_push * momentum_v)
    return (
        y.reshape(PASSES, 1, length, width),
        g_in.reshape(PASSES, 1, length, width),
        g_mem[None],
        jnp.stack([new_w, mean_w, momentum_w]),
        jnp.stack([new_v, mean_v, momentum_v]),
        jnp.stack([moment_w, second_w])[None],
        jnp.stack([moment_v, second_v])[None],
    )


def solution(mesh):
    both = ("rep", "fsdp")
    return jax.shard_map(
        per_device,
        mesh=mesh,
        in_specs=(
            P(),
            P(both, None),
            P(both, None),
            P(both),
            P(both),
            P(both, None, None),
            P(None, both, None, None),
            P("fsdp", None),
            P(None, "fsdp"),
            P("rep", None, "fsdp", None),
            P("rep", None, None, "fsdp"),
            P("fsdp", None),
            P(None, "fsdp"),
        ),
        out_specs=(
            P(None, both, None, None),
            P(None, both, None, None),
            P(both, None, None),
            P(None, "fsdp", None),
            P(None, None, "fsdp"),
            P("rep", None, "fsdp", None),
            P("rep", None, None, "fsdp"),
        ),
        check_vma=False,
    )
```

```python
import functools
import math

import jax
import jax.numpy as jnp
from jax import lax
from jax.experimental import pallas as pl
from jax.experimental.pallas import tpu as pltpu
from jax.sharding import PartitionSpec as P

HEADS = 8
STEP = 8
PASSES = 2
AUG = 80
norm_epsilon = 1e-05
beta_first = 0.9
beta_second = 0.999
adam_epsilon = 1e-08
rate_inner = 0.1
rate_outer = 0.7
outer_push = 0.9
decay_rate = 0.01

BF = jnp.bfloat16
F32 = jnp.float32
NN = (((1,), (0,)), ((), ()))
NT = (((1,), (1,)), ((), ()))
TN = (((0,), (0,)), ((), ()))
VMEM_LIMIT = 60 << 20


def dot(left, right, dims):
    return lax.dot_general(left, right, dims, preferred_element_type=F32)


def normalise(values):
    centre = values - jnp.mean(values, axis=-1, keepdims=True)
    spread = jnp.mean(centre * centre, axis=-1, keepdims=True)
    inverse = lax.rsqrt(spread + norm_epsilon)
    return centre * inverse, inverse


def norm_back(grad_out, gain_row, normal, inverse):
    grad_normal = grad_out * gain_row
    mean_grad = jnp.mean(grad_normal, axis=-1, keepdims=True)
    mean_proj = jnp.mean(grad_normal * normal, axis=-1, keepdims=True)
    grad_in = inverse * (grad_normal - mean_grad - normal * mean_proj)
    return grad_in, jnp.sum(grad_out * normal, axis=0, keepdims=True), jnp.sum(grad_out, axis=0, keepdims=True)


def thirds(row):
    high = row.astype(BF)
    rest = row - high.astype(F32)
    middle = rest.astype(BF)
    low = (rest - middle.astype(F32)).astype(BF)
    return high.astype(F32), middle.astype(F32), low.astype(F32)


def tail_rows(width, rows):
    place = lax.broadcasted_iota(jnp.int32, (AUG - 64, width), 0)
    tail = jnp.zeros((AUG - 64, width), F32)
    for number, row in enumerate(rows):
        tail = jnp.where(place == number, row, tail)
    return tail.astype(BF)


def put_heads(target, matrix_t, scale, tail):
    low = matrix_t.astype(BF)
    if scale != 1.0:
        low = low * BF(scale)
    size = low.shape[0] // HEADS
    for head in range(HEADS):
        target[head, :size, :] = low[head * size : (head + 1) * size]
        target[head, size:, :] = tail


def key_tail(width, count, period):
    spot = lax.broadcasted_iota(jnp.int32, (1, width), 1) % period
    bias = jnp.where(spot < count, 0.0, -1e30)
    return tail_rows(width, [bias, 1.0, 1.0, 1.0])


def attend_forward(units, where_of, block, q_ref, k_ref, v_ref, o_ref, s_a, s_b, m_a, m_b):
    keys = s_a.shape[0]

    def scores(step, store, peak):
        head, first, key_first = where_of(jnp.minimum(step, units - 1))
        value = dot(k_ref[head, :, pl.ds(key_first, keys)], q_ref[head, :, pl.ds(first, block)], TN)
        store[...] = value
        peak[...] = jnp.broadcast_to(jnp.max(value, axis=0, keepdims=True), peak.shape)

    def finish(step, store, peak):
        head, first, key_first = where_of(step)
        top = peak[0:1, :]
        weight = jnp.exp(store[...] - top).astype(BF)
        mixed = dot(v_ref[head, :, pl.ds(key_first, keys)], weight, NN)
        total = mixed[64:65, :]
        o_ref[pl.ds(pl.multiple_of(head * 64, 64), 64), pl.ds(first, block)] = (mixed[:64] * (1.0 / total)).astype(BF)
        high, middle, low = thirds(top + jnp.log(total))
        q_ref[head, 64:, pl.ds(first, block)] = tail_rows(block, [1.0, -high, -middle, -low])

    scores(0, s_a, m_a)

    def body(pair, carry):
        step = 2 * pair
        scores(step + 1, s_b, m_b)
        finish(step, s_a, m_a)
        scores(step + 2, s_a, m_a)
        finish(step + 1, s_b, m_b)
        return carry

    lax.fori_loop(0, units // 2 - 1, body, 0)
    step = units - 2
    scores(step + 1, s_b, m_b)
    finish(step, s_a, m_a)
    finish(step + 1, s_b, m_b)


def attend_backward(head, first, block, key_first, keys, q_ref, k_ref, v_ref, d_ref):
    here = pl.ds(first, block)
    there = pl.ds(key_first, keys)
    query = q_ref[head, :, here]
    grad = d_ref[head, :, here]
    key_t = k_ref[head, :, there]
    weight = jnp.exp(dot(query, key_t, TN))
    grad_scores = (weight * dot(grad, v_ref[head, :, there], TN)).astype(BF)
    grad_value = dot(grad[:64], weight.astype(BF), NN)
    grad_key = dot(query[:64], grad_scores, NN)
    grad_query = dot(key_t[:64], grad_scores, NT) * 0.125
    return grad_query.astype(BF), grad_key, grad_value


def put_grads(d_ref, grad_t, o_ref):
    low = grad_t.astype(BF)
    for head in range(HEADS):
        part = low[head * 64 : (head + 1) * 64]
        both = part.astype(F32) * o_ref[head * 64 : (head + 1) * 64, :].astype(F32)
        high, middle, rest = thirds(jnp.sum(both, axis=0, keepdims=True))
        d_ref[head, :64, :] = part
        d_ref[head, 64:, :] = tail_rows(low.shape[1], [-high, -middle, -rest])


def fetch(core, near, far, target, sems):
    half = near.shape[0]
    first = pltpu.make_async_copy(near, target.at[pl.ds(pl.multiple_of(core * half, half), half)], sems.at[0])
    second = pltpu.make_async_copy(far, target.at[pl.ds(pl.multiple_of((1 - core) * half, half), half)], sems.at[1])
    first.start()
    second.start()
    return first, second


def deliver(core, source, near, far, sems):
    first = pltpu.make_async_copy(source.at[core], near, sems.at[0])
    second = pltpu.make_async_copy(source.at[1 - core], far, sems.at[1])
    first.start()
    second.start()
    return first, second


def wait(copies):
    for copy in copies:
        copy.wait()


def self_forward(lens, x_ref, near, far, vec_ref, q_ref, k_ref, v_ref, o_ref, h_ref, s_a, s_b, m_a, m_b, w_ref, sems):
    width = x_ref.shape[1]
    rows = x_ref.shape[0]
    length = rows // PASSES
    copies = fetch(lens[2], near, far, w_ref, sems)
    x = x_ref[...].astype(F32)
    normal, _ = normalise(x)
    low = (normal * vec_ref[0:1, :] + vec_ref[3:4, :]).astype(BF)
    wait(copies)
    ones = tail_rows(rows, [1.0, 1.0, 1.0])
    first = tail_rows(rows, [1.0])
    put_heads(q_ref, dot(w_ref[0:width, :], low, (((0,), (1,)), ((), ()))), 0.125, first)
    put_heads(k_ref, dot(w_ref[width : 2 * width, :], low, (((0,), (1,)), ((), ()))), 1.0, key_tail(rows, lens[0], length))
    put_heads(v_ref, dot(w_ref[2 * width : 3 * width, :], low, (((0,), (1,)), ((), ()))), 1.0, ones)

    def where_of(step):
        place = pl.multiple_of((step % PASSES) * length, length)
        return step // PASSES, place, place

    attend_forward(HEADS * PASSES, where_of, length, q_ref, k_ref, v_ref, o_ref, s_a, s_b, m_a, m_b)
    h_ref[...] = x_ref[...].astype(F32) + dot(o_ref[...], w_ref[3 * width : 4 * width, :], TN)


def cross_forward(lens, h_ref, near, far, mem_ref, vec_ref, q_ref, k_ref, v_ref, o_ref, out_ref, s_a, s_b, m_a, m_b, w_ref, sems):
    width = h_ref.shape[1]
    rows = h_ref.shape[0]
    slots = mem_ref.shape[0]
    block = s_a.shape[1]
    copies = fetch(lens[2], near, far, w_ref, sems)
    normal, _ = normalise(h_ref[...])
    low = (normal * vec_ref[1:2, :] + vec_ref[4:5, :]).astype(BF)
    wait(copies)
    memory = mem_ref[...]
    put_heads(q_ref, dot(w_ref[0:width, :], low, (((0,), (1,)), ((), ()))), 0.125, tail_rows(rows, [1.0]))
    put_heads(k_ref, dot(w_ref[width : 2 * width, :], memory, (((0,), (1,)), ((), ()))), 1.0, key_tail(slots, lens[1], slots))
    put_heads(v_ref, dot(w_ref[2 * width : 3 * width, :], memory, (((0,), (1,)), ((), ()))), 1.0, tail_rows(slots, [1.0, 1.0, 1.0]))
    pieces = rows // block

    def where_of(step):
        return step // pieces, pl.multiple_of((step % pieces) * block, block), 0

    attend_forward(HEADS * pieces, where_of, block, q_ref, k_ref, v_ref, o_ref, s_a, s_b, m_a, m_b)
    out_ref[...] = h_ref[...] + dot(o_ref[...], w_ref[3 * width : 4 * width, :], TN)


def feed(shards, lens, h_ref, up_near, up_far, down_near, down_far, vec_ref, cot_ref, y_ref, dh_ref, gup_near, gup_far, gdown_near, gdown_far, gv_ref, up_s, e_s, n_s, y_s, de_s, up_ref, down_ref, gup_ref, gdown_ref, sems):
    width = h_ref.shape[1]
    rows = h_ref.shape[0]
    hidden = down_ref.shape[0]
    parts = hidden // width
    piece = hidden // shards // parts
    core = lens[2]
    copies = fetch(core, up_near, up_far, up_ref, sems.at[0]) + fetch(core, down_near, down_far, down_ref, sems.at[1])
    normal, inverse = normalise(h_ref[...])
    n_s[...] = normal
    e_s[...] = (normal * vec_ref[2:3, :] + vec_ref[5:6, :]).astype(BF)
    spot = lax.broadcasted_iota(jnp.int32, (rows, 1), 0) % (rows // PASSES)
    cot = jnp.where(spot < lens[0], cot_ref[...].astype(F32), 0.0)
    df = cot.astype(BF)
    y_s[...] = h_ref[...] + vec_ref[6:7, :]
    de_s[...] = jnp.zeros_like(de_s)
    gv_ref[...] = jnp.zeros_like(gv_ref)
    wait(copies)
    for shard in range(shards):
        for part in range(parts):
            begin = (shard * parts + part) * piece
            up_s[part, shard * piece : (shard + 1) * piece, :] = up_ref[begin : begin + piece, :]

    def body(part, carry):
        place = pl.multiple_of(part * width, width)
        down = down_ref[pl.ds(place, width), :]
        up = up_s[part]
        pre = dot(e_s[...], up, NN) + vec_ref[pl.ds(7 + part, 1), :]
        active = jnp.maximum(pre, 0.0).astype(BF)
        y_s[...] += dot(active, down, NN)
        half = gdown_ref.shape[1]
        gdown_ref[place // half, pl.ds(pl.multiple_of(place % half, width), width), :] = dot(active, df, TN).astype(BF)
        du = jnp.where(pre > 0, dot(df, down, NT), 0.0).astype(BF)
        gv_ref[pl.ds(7 + part, 1), :] = jnp.sum(du.astype(F32), axis=0, keepdims=True)
        gup = dot(e_s[...], du, TN).astype(BF)
        for shard in range(shards):
            begin = (shard * parts + part) * piece
            gup_ref[begin // half, pl.ds(pl.multiple_of(begin % half, piece), piece), :] = gup[shard * piece : (shard + 1) * piece, :]
        de_s[...] += dot(du, up, NT)
        return carry

    lax.fori_loop(0, parts, body, 0)
    copies = deliver(core, gup_ref, gup_near, gup_far, sems.at[0]) + deliver(core, gdown_ref, gdown_near, gdown_far, sems.at[1])
    y_ref[...] = y_s[...].astype(BF)
    gv_ref[6:7, :] = jnp.sum(cot, axis=0, keepdims=True)
    back, gain, shift = norm_back(de_s[...], vec_ref[2:3, :], n_s[...], inverse)
    gv_ref[2:3, :] = gain
    gv_ref[5:6, :] = shift
    dh_ref[...] = cot + back
    wait(copies)


def cross_backward(lens, dh2_ref, near, far, q_ref, k_ref, v_ref, o_ref, h_ref, mem_ref, vec_ref, g_near, g_far, gmem_ref, dh_ref, gv_ref, d_s, dq_s, dk_s, dv_s, sk, sv, w_ref, g_ref, sems):
    width = h_ref.shape[1]
    rows = h_ref.shape[0]
    slots = mem_ref.shape[0]
    block = rows // PASSES
    core = lens[2]
    copies = fetch(core, near, far, w_ref, sems)
    dz = dh2_ref[...].astype(BF)
    wait(copies)
    g_ref[1, width:, :] = dot(o_ref[...], dz, NN).astype(BF)
    put_grads(d_s, dot(w_ref[3 * width : 4 * width, :], dz, NT), o_ref)

    def body(head, carry):
        place = pl.ds(pl.multiple_of(head * 64, 64), 64)
        for piece in range(rows // block):
            dq, dk, dv = attend_backward(head, piece * block, block, 0, slots, q_ref, k_ref, v_ref, d_s)
            dq_s[place, piece * block : (piece + 1) * block] = dq
            if piece == 0:
                sk[...] = dk
                sv[...] = dv
            else:
                dk_s[place, :] = (sk[...] + dk).astype(BF)
                dv_s[place, :] = (sv[...] + dv).astype(BF)
        return carry

    lax.fori_loop(0, HEADS, body, 0)
    memory = mem_ref[...]
    dk = dk_s[...].T
    g_ref[0, width:, :] = dot(memory, dk, TN).astype(BF)
    gmem_ref[...] = dot(dk, w_ref[width : 2 * width, :], NT)
    dv = dv_s[...].T
    g_ref[1, :width, :] = dot(memory, dv, TN).astype(BF)
    gmem_ref[...] += dot(dv, w_ref[2 * width : 3 * width, :], NT)
    normal, inverse = normalise(h_ref[...])
    low = (normal * vec_ref[1:2, :] + vec_ref[4:5, :]).astype(BF)
    dq = dq_s[...].T
    g_ref[0, :width, :] = dot(low, dq, TN).astype(BF)
    copies = deliver(core, g_ref, g_near, g_far, sems)
    back, gain, shift = norm_back(dot(dq, w_ref[0:width, :], NT), vec_ref[1:2, :], normal, inverse)
    gv_ref[...] = jnp.zeros_like(gv_ref)
    gv_ref[1:2, :] = gain
    gv_ref[4:5, :] = shift
    dh_ref[...] = dh2_ref[...] + back
    wait(copies)


def self_backward(lens, dh_ref, near, far, q_ref, k_ref, v_ref, o_ref, x_ref, vec_ref, g_near, g_far, gin_ref, gv_ref, d_s, dq_s, dk_s, dv_s, w_ref, g_ref, sems):
    width = x_ref.shape[1]
    rows = x_ref.shape[0]
    length = rows // PASSES
    core = lens[2]
    copies = fetch(core, near, far, w_ref, sems)
    dz = dh_ref[...].astype(BF)
    wait(copies)
    g_ref[1, width:, :] = dot(o_ref[...], dz, NN).astype(BF)
    put_grads(d_s, dot(w_ref[3 * width : 4 * width, :], dz, NT), o_ref)

    def body(head, carry):
        place = pl.ds(pl.multiple_of(head * 64, 64), 64)
        for number in range(PASSES):
            begin = number * length
            dq, dk, dv = attend_backward(head, begin, length, begin, length, q_ref, k_ref, v_ref, d_s)
            dq_s[place, begin : begin + length] = dq
            dk_s[place, begin : begin + length] = dk.astype(BF)
            dv_s[place, begin : begin + length] = dv.astype(BF)
        return carry

    lax.fori_loop(0, HEADS, body, 0)
    normal, inverse = normalise(x_ref[...].astype(F32))
    low = (normal * vec_ref[0:1, :] + vec_ref[3:4, :]).astype(BF)
    total = None
    for number, store in enumerate((dq_s, dk_s, dv_s)):
        grad = store[...].T
        g_ref[number // 2, (number % 2) * width : (number % 2 + 1) * width, :] = dot(low, grad, TN).astype(BF)
        part = dot(grad, w_ref[number * width : (number + 1) * width, :], NT)
        total = part if total is None else total + part
    copies = deliver(core, g_ref, g_near, g_far, sems)
    back, gain, shift = norm_back(total, vec_ref[0:1, :], normal, inverse)
    gv_ref[...] = jnp.zeros_like(gv_ref)
    gv_ref[0:1, :] = gain
    gv_ref[3:4, :] = shift
    gin_ref[...] = dh_ref[...] + back
    wait(copies)


def adam(flags, g0, g1, g2, rest, w_ref, state_ref, new_ref, delta_ref, g_s, order_s):
    share = w_ref.shape[0]
    part = share // 4
    g_s[...] = jnp.where(flags[0] == 1, g0[...].astype(F32) + g1[...].astype(F32) + g2[...].astype(F32), rest[...])

    @pl.when(flags[1] == 1)
    def _():
        for lane in range(order_s.shape[0]):
            lanes = slice(lane * 128, (lane + 1) * 128)
            for number in range(4):
                order_s[lane, pl.ds(number, part, stride=4), :] = g_s[number * part : (number + 1) * part, lanes]
            g_s[:, lanes] = order_s[lane]

    moment, second, delta = inner_update(w_ref[...], g_s[...], state_ref[0, 0], state_ref[0, 1], decay_rate)
    new_ref[0, 0] = moment
    new_ref[0, 1] = second
    delta_ref[...] = delta.astype(BF)


def outer(replicas, *refs):
    halves = (len(refs) - 3) // 2
    w_ref, mom_ref, out_ref = refs[-3:]
    share = w_ref.shape[0] // halves
    for half in range(halves):
        rows = slice(half * share, (half + 1) * share)
        mean = (refs[half][...].astype(F32) + refs[halves + half][...].astype(F32)) / replicas
        momentum = outer_push * mom_ref[rows, :] + mean
        out_ref[0, rows, :] = w_ref[rows, :] - rate_outer * (mean + outer_push * momentum)
        out_ref[1, rows, :] = mean
        out_ref[2, rows, :] = momentum


def place(spot, *refs):
    whole = refs[-1]
    half = whole.shape[0] // 8
    for distance in range(4):
        upper, lower = refs[2 * distance : 2 * distance + 2]
        begin = (spot[0] ^ distance) * 2 * half
        whole[pl.ds(pl.multiple_of(begin, half), half), :] = upper[...]
        whole[pl.ds(pl.multiple_of(begin + half, half), half), :] = lower[...]


VM = pl.BlockSpec(memory_space=pltpu.VMEM)
SM = pl.BlockSpec(memory_space=pltpu.SMEM)
HB = pl.BlockSpec(memory_space=pl.ANY)


def call(body, name, ins, outs, scratch=(), places=None):
    shapes = tuple(jax.ShapeDtypeStruct(shape, kind) for shape, kind in outs)
    return pl.pallas_call(
        body,
        name=name,
        out_shape=shapes,
        in_specs=ins,
        out_specs=tuple(places or [VM] * len(outs)),
        scratch_shapes=[item if not isinstance(item, tuple) else pltpu.VMEM(*item) for item in scratch],
        compiler_params=pltpu.CompilerParams(vmem_limit_bytes=VMEM_LIMIT),
    )


def inner_update(weight, gradient, moment_one, second, shrink):
    moment_new = beta_first * moment_one + (1.0 - beta_first) * gradient
    second_new = beta_second * second + (1.0 - beta_second) * gradient * gradient
    moment_hat = moment_new / (1.0 - beta_first**STEP)
    second_hat = second_new / (1.0 - beta_second**STEP)
    local_weight = weight - rate_inner * (
        moment_hat / (jnp.sqrt(second_hat) + adam_epsilon) + shrink * weight
    )
    return (moment_new, second_new, weight - local_weight)


def swap(values, axis, bit):
    count = lax.axis_size(axis)
    return lax.ppermute(values, axis, [(i, i ^ bit) for i in range(count)])


def total_over(values, axis):
    count = lax.axis_size(axis)
    if count & (count - 1):
        return lax.psum(values, axis)
    bit = 1
    while bit < count:
        values = values + swap(values, axis, bit)
        bit *= 2
    return values


def send(values, source, target):
    return lax.ppermute(values, "fsdp", [(2 * source + core, 2 * target + core) for core in range(2)])


def gather_blocks(low):
    rank = lax.axis_index("rep")
    chip = lax.axis_index("fsdp") // 2
    share, width = low.shape
    quarter = share // 4
    half = quarter // 2
    piece = lax.dynamic_slice(low, (rank * quarter, 0), (quarter, width))
    spot = jnp.reshape(rank, (1,)).astype(jnp.int32)
    pairs = []
    for block in range(4):
        got = [send(piece, block, chip_to) for chip_to in range(4) if chip_to != block]
        own = jnp.where(chip == block, piece, got[0] + got[1] + got[2])
        upper, lower = own[:half], own[half:]
        upper_x = swap(upper, "rep", 1)
        lower_y = swap(lower, "rep", 2)
        upper_y = swap(upper, "rep", 2)
        lower_x = swap(lower, "rep", 1)
        upper_xy = swap(upper_x, "rep", 2)
        lower_xy = swap(lower_y, "rep", 1)
        parts = (upper, lower, upper_x, lower_x, upper_y, lower_y, upper_xy, lower_xy)
        (near,) = call(place, "place", [SM] + [VM] * 8, [((share, width), BF)])(spot, *parts)
        pairs.append((near, swap(near, "fsdp", 1)))
    return pairs


def add_low(one, two):
    return (one.astype(F32) + two.astype(F32)).astype(BF)


def per_device(embed, first_tokens, sample_tokens, seq_len, mem_len, memory, cotangent, params, vecs, inner_state, inner_vecs, outer_mom, outer_vecs):
    groups = lax.axis_size("fsdp")
    replicas = lax.axis_size("rep")
    direct = groups == 8 and replicas == 4
    share, width = params.shape
    hidden = 4 * width
    me = lax.axis_index("fsdp")
    chip = me // 2
    own_up = (me >= 2 * hidden // share) & (me < 3 * hidden // share)
    low = params.astype(BF)
    low = jnp.where(own_up, low.reshape(share // 4, 4, width).transpose(1, 0, 2).reshape(share, width), low)
    count, columns = vecs.shape
    vectors = lax.dynamic_update_slice(jnp.zeros((16, width), BF), vecs.astype(BF), (0, me * columns))
    vectors = total_over(vectors, "fsdp").astype(F32)
    if direct:
        pairs = gather_blocks(low)
        core = me % 2
    else:
        gathered = lax.all_gather(low, "fsdp", axis=0, tiled=True)
        halves = [gathered[i * hidden // 2 : (i + 1) * hidden // 2] for i in range(8)]
        pairs = [(halves[2 * i], halves[2 * i + 1]) for i in range(4)]
        core = jnp.zeros((), jnp.int32)

    x = embed[jnp.concatenate([first_tokens[0], sample_tokens[0]])]
    lens = jnp.stack([seq_len[0], mem_len[0], core]).astype(jnp.int32)
    length = first_tokens.shape[1]
    rows = PASSES * length
    cot = cotangent.reshape(rows, width)
    memory = memory[0]
    slots = memory.shape[0]

    heads_n = ((HEADS, AUG, rows), BF)
    heads_m = ((HEADS, AUG, slots), BF)
    flat_n = ((width, rows), BF)
    flat_m = ((width, slots), BF)
    full = ((rows, width), F32)
    half_g = ((hidden // 2, width), BF)
    block_w = ((hidden, width), BF)
    block_g = ((2, hidden // 2, width), BF)
    vec_g = ((16, width), F32)
    peak = ((8, length), F32)
    sems = pltpu.SemaphoreType.DMA
    qs, ks, vs, o_self, h = call(
        self_forward, "self_forward", [SM, VM, HB, HB, VM],
        [heads_n, heads_n, heads_n, flat_n, full],
        [((length, length), F32)] * 2 + [peak] * 2 + [block_w, sems((2,))],
    )(lens, x, *pairs[0], vectors)
    qc, kc, vc, o_cross, h2 = call(
        cross_forward, "cross_forward", [SM, VM, HB, HB, VM, VM],
        [heads_n, heads_m, heads_m, flat_n, full],
        [((slots, length), F32)] * 2 + [peak] * 2 + [block_w, sems((2,))],
    )(lens, h, *pairs[1], memory, vectors)
    y, dh2, up_near, up_far, down_near, down_far, gv3 = call(
        functools.partial(feed, hidden // min(share, hidden)), "feed", [SM, VM, HB, HB, HB, HB, VM, VM],
        [((rows, width), BF), full, half_g, half_g, half_g, half_g, vec_g],
        [((4, width, width), BF), ((rows, width), BF), full, full, full, block_w, block_w, block_g, block_g, sems((2, 2))],
        [VM, VM, HB, HB, HB, HB, VM],
    )(lens, h2, *pairs[2], *pairs[3], vectors, cot)
    cross_near, cross_far, g_mem, dh, gv2 = call(
        cross_backward, "cross_backward", [SM, VM, HB, HB] + [VM] * 7,
        [half_g, half_g, (memory.shape, F32), full, vec_g],
        [heads_n, flat_n, flat_m, flat_m, ((64, slots), F32), ((64, slots), F32), block_w, block_g, sems((2,))],
        [HB, HB, VM, VM, VM],
    )(lens, dh2, *pairs[1], qc, kc, vc, o_cross, h, memory, vectors)
    self_near, self_far, g_in, gv1 = call(
        self_backward, "self_backward", [SM, VM, HB, HB] + [VM] * 6,
        [half_g, half_g, full, vec_g],
        [heads_n, flat_n, flat_n, flat_n, block_w, block_g, sems((2,))],
        [HB, HB, VM, VM],
    )(lens, dh, *pairs[0], qs, ks, vs, o_self, x, vectors)

    gv = total_over(gv1 + gv2 + gv3, "fsdp")
    grad_v = lax.dynamic_slice(gv, (0, me * columns), (count, columns))
    if direct:
        sums = []
        for near, far in ((self_near, self_far), (cross_near, cross_far), (up_near, up_far), (down_near, down_far)):
            sums.append(add_low(near, swap(far, "fsdp", 1)))
        routes = (((1, 0), (3, 2), (2, 0)), ((0, 1), (3, 2), (2, 1)), ((0, 1), (3, 2), (1, 2)), ((0, 1), (2, 3), (1, 3)))
        finals = []
        for value, (one, two, last) in zip(sums, routes):
            pairs_of = [(2 * a + core_, 2 * b + core_) for a, b in (one, two) for core_ in range(2)]
            got = lax.ppermute(value, "fsdp", pairs_of)
            late = send(add_low(value, got), *last)
            finals.append((value, got, late))
        rest = None
        for block in (1, 2, 3):
            part = sum(item.astype(F32) for item in finals[block])
            rest = part if rest is None else jnp.where(chip == block, part, rest)
        first = finals[0]
        flag = chip == 0
    else:
        whole = jnp.concatenate([self_near, self_far, cross_near, cross_far, up_near, up_far, down_near, down_far])
        rest = lax.psum_scatter(whole, "fsdp", scatter_dimension=0, tiled=True).astype(F32)
        first = [jnp.zeros((share, width), BF)] * 3
        flag = False
    flags = jnp.stack([jnp.asarray(flag), own_up]).astype(jnp.int32)
    inner_new, delta = call(
        adam, "adam", [SM] + [VM] * 6,
        [(inner_state.shape, F32), ((share, width), BF)],
        [((share, width), F32), ((width // 128, share, 128), F32)],
    )(flags, *first, rest, params, inner_state)
    if replicas == 4:
        upper, lower = delta[: share // 2], delta[share // 2 :]
        upper = add_low(upper, swap(upper, "rep", 1))
        lower = add_low(lower, swap(lower, "rep", 2))
        ones = [upper, lower]
        twos = [swap(upper, "rep", 2), swap(lower, "rep", 1)]
    else:
        ones = [lax.psum(delta, "rep")]
        twos = [jnp.zeros_like(delta)]
    (param_results,) = call(
        functools.partial(outer, replicas), "outer", [VM] * (2 * len(ones) + 2),
        [((3, share, width), F32)],
    )(*ones, *twos, params, outer_mom)
    moment_v, second_v, delta_v = inner_update(vecs, grad_v, inner_vecs[0, 0], inner_vecs[0, 1], 0.0)
    mean_v = total_over(delta_v.astype(BF), "rep").astype(F32) / replicas
    momentum_v = outer_push * outer_vecs + mean_v
    new_v = vecs - rate_outer * (mean_v + outer_push * momentum_v)
    return (
        y.reshape(PASSES, 1, length, width),
        g_in.reshape(PASSES, 1, length, width),
        g_mem[None],
        param_results,
        jnp.stack([new_v, mean_v, momentum_v]),
        inner_new,
        jnp.stack([moment_v, second_v])[None],
    )


def solution(mesh):
    both = ("rep", "fsdp")
    return jax.shard_map(
        per_device,
        mesh=mesh,
        in_specs=(
            P(),
            P(both, None),
            P(both, None),
            P(both),
            P(both),
            P(both, None, None),
            P(None, both, None, None),
            P("fsdp", None),
            P(None, "fsdp"),
            P("rep", None, "fsdp", None),
            P("rep", None, None, "fsdp"),
            P("fsdp", None),
            P(None, "fsdp"),
        ),
        out_specs=(
            P(None, both, None, None),
            P(None, both, None, None),
            P(both, None, None),
            P(None, "fsdp", None),
            P(None, None, "fsdp"),
            P("rep", None, "fsdp", None),
            P("rep", None, None, "fsdp"),
        ),
        check_vma=False,
    )
```

```python
import functools
import math

import jax
import jax.numpy as jnp
from jax import lax
from jax.experimental import pallas as pl
from jax.experimental.pallas import tpu as pltpu
from jax.sharding import PartitionSpec as P

HEADS = 8
STEP = 8
PASSES = 2
AUG = 80
norm_epsilon = 1e-05
beta_first = 0.9
beta_second = 0.999
adam_epsilon = 1e-08
rate_inner = 0.1
rate_outer = 0.7
outer_push = 0.9
decay_rate = 0.01

BF = jnp.bfloat16
F32 = jnp.float32
NN = (((1,), (0,)), ((), ()))
NT = (((1,), (1,)), ((), ()))
TN = (((0,), (0,)), ((), ()))
TT = (((0,), (1,)), ((), ()))
VMEM_LIMIT = 60 << 20


def dot(left, right, dims):
    return lax.dot_general(left, right, dims, preferred_element_type=F32)


def normalise(values):
    centre = values - jnp.mean(values, axis=-1, keepdims=True)
    spread = jnp.mean(centre * centre, axis=-1, keepdims=True)
    inverse = lax.rsqrt(spread + norm_epsilon)
    return centre * inverse, inverse


def norm_back(grad_out, gain_row, normal, inverse):
    grad_normal = grad_out * gain_row
    mean_grad = jnp.mean(grad_normal, axis=-1, keepdims=True)
    mean_proj = jnp.mean(grad_normal * normal, axis=-1, keepdims=True)
    grad_in = inverse * (grad_normal - mean_grad - normal * mean_proj)
    return grad_in, jnp.sum(grad_out * normal, axis=0, keepdims=True), jnp.sum(grad_out, axis=0, keepdims=True)


def thirds(row):
    high = row.astype(BF)
    rest = row - high.astype(F32)
    middle = rest.astype(BF)
    low = (rest - middle.astype(F32)).astype(BF)
    return high.astype(F32), middle.astype(F32), low.astype(F32)


def tail_rows(width, rows):
    place = lax.broadcasted_iota(jnp.int32, (AUG - 64, width), 0)
    tail = jnp.zeros((AUG - 64, width), F32)
    for number, row in enumerate(rows):
        tail = jnp.where(place == number, row, tail)
    return tail.astype(BF)


def put_heads(target, matrix_t, scale, tail):
    low = matrix_t.astype(BF)
    if scale != 1.0:
        low = low * BF(scale)
    size = low.shape[0] // HEADS
    for head in range(HEADS):
        target[head, :size, :] = low[head * size : (head + 1) * size]
        target[head, size:, :] = tail


def key_tail(width, count, period):
    spot = lax.broadcasted_iota(jnp.int32, (1, width), 1) % period
    bias = jnp.where(spot < count, 0.0, -1e30)
    return tail_rows(width, [bias, 1.0, 1.0, 1.0])


def attend_forward(units, where_of, block, q_ref, k_ref, v_ref, o_ref, s_a, s_b, m_a, m_b):
    keys = s_a.shape[0]

    def scores(step, store, peak):
        head, first, key_first = where_of(jnp.minimum(step, units - 1))
        value = dot(k_ref[head, :, pl.ds(key_first, keys)], q_ref[head, :, pl.ds(first, block)], TN)
        store[...] = value
        peak[...] = jnp.broadcast_to(jnp.max(value, axis=0, keepdims=True), peak.shape)

    def finish(step, store, peak):
        head, first, key_first = where_of(step)
        top = peak[0:1, :]
        weight = jnp.exp(store[...] - top).astype(BF)
        mixed = dot(v_ref[head, :, pl.ds(key_first, keys)], weight, NN)
        total = mixed[64:65, :]
        o_ref[pl.ds(pl.multiple_of(head * 64, 64), 64), pl.ds(first, block)] = (mixed[:64] * (1.0 / total)).astype(BF)
        high, middle, low = thirds(top + jnp.log(total))
        q_ref[head, 64:, pl.ds(first, block)] = tail_rows(block, [1.0, -high, -middle, -low])

    scores(0, s_a, m_a)

    def body(pair, carry):
        step = 2 * pair
        scores(step + 1, s_b, m_b)
        finish(step, s_a, m_a)
        scores(step + 2, s_a, m_a)
        finish(step + 1, s_b, m_b)
        return carry

    lax.fori_loop(0, units // 2 - 1, body, 0)
    step = units - 2
    scores(step + 1, s_b, m_b)
    finish(step, s_a, m_a)
    finish(step + 1, s_b, m_b)


def attend_backward(head, first, block, key_first, keys, q_ref, k_ref, v_ref, d_ref, skip=0):
    here = pl.ds(first, block)
    there = pl.ds(key_first, keys)
    grad = d_ref[head, :, here]
    head = head + skip
    query = q_ref[head, :, here]
    key_t = k_ref[head, :, there]
    weight = jnp.exp(dot(query, key_t, TN))
    grad_scores = (weight * dot(grad, v_ref[head, :, there], TN)).astype(BF)
    grad_value = dot(grad[:64], weight.astype(BF), NN)
    grad_key = dot(query[:64], grad_scores, NN)
    grad_query = dot(key_t[:64], grad_scores, NT) * 0.125
    return grad_query.astype(BF), grad_key, grad_value


def put_grads(d_ref, grad_t, o_ref, skip, heads):
    low = grad_t.astype(BF)
    for head in range(heads):
        part = low[head * 64 : (head + 1) * 64]
        both = part.astype(F32) * o_ref[(skip + head) * 64 : (skip + head + 1) * 64, :].astype(F32)
        high, middle, rest = thirds(jnp.sum(both, axis=0, keepdims=True))
        d_ref[head, :64, :] = part
        d_ref[head, 64:, :] = tail_rows(low.shape[1], [-high, -middle, -rest])


def fetch(weights, block, target, sem):
    rows = target.shape[0]
    copy = pltpu.make_async_copy(weights.at[pl.ds(block * rows, rows)], target, sem)
    copy.start()
    return copy


def deliver(core, source, near, far, sems):
    first = pltpu.make_async_copy(source.at[core], near, sems.at[0])
    second = pltpu.make_async_copy(source.at[1 - core], far, sems.at[1])
    first.start()
    second.start()
    return first, second


def wait(copies):
    for copy in copies:
        copy.wait()


def self_forward(lens, x_ref, weights, vec_ref, q_ref, k_ref, v_ref, o_ref, h_ref, s_a, s_b, m_a, m_b, w_ref, sems):
    width = x_ref.shape[1]
    rows = x_ref.shape[0]
    length = rows // PASSES
    copy = fetch(weights, 0, w_ref, sems.at[0])
    x = x_ref[...].astype(F32)
    normal, _ = normalise(x)
    low = (normal * vec_ref[0:1, :] + vec_ref[3:4, :]).astype(BF)
    copy.wait()
    put_heads(q_ref, dot(w_ref[0:width, :], low, TT), 0.125, tail_rows(rows, [1.0]))
    put_heads(k_ref, dot(w_ref[width : 2 * width, :], low, TT), 1.0, key_tail(rows, lens[0], length))
    put_heads(v_ref, dot(w_ref[2 * width : 3 * width, :], low, TT), 1.0, tail_rows(rows, [1.0, 1.0, 1.0]))

    def where_of(step):
        place = pl.multiple_of((step % PASSES) * length, length)
        return step // PASSES, place, place

    attend_forward(HEADS * PASSES, where_of, length, q_ref, k_ref, v_ref, o_ref, s_a, s_b, m_a, m_b)
    h_ref[...] = x_ref[...].astype(F32) + dot(o_ref[...], w_ref[3 * width : 4 * width, :], TN)


def cross_forward(lens, h_ref, weights, mem_ref, vec_ref, q_ref, k_ref, v_ref, o_ref, out_ref, s_a, s_b, m_a, m_b, w_ref, sems):
    width = h_ref.shape[1]
    rows = h_ref.shape[0]
    slots = mem_ref.shape[0]
    block = s_a.shape[1]
    copy = fetch(weights, 1, w_ref, sems.at[0])
    normal, _ = normalise(h_ref[...])
    low = (normal * vec_ref[1:2, :] + vec_ref[4:5, :]).astype(BF)
    copy.wait()
    memory = mem_ref[...]
    put_heads(q_ref, dot(w_ref[0:width, :], low, TT), 0.125, tail_rows(rows, [1.0]))
    put_heads(k_ref, dot(w_ref[width : 2 * width, :], memory, TT), 1.0, key_tail(slots, lens[1], slots))
    put_heads(v_ref, dot(w_ref[2 * width : 3 * width, :], memory, TT), 1.0, tail_rows(slots, [1.0, 1.0, 1.0]))
    pieces = rows // block

    def where_of(step):
        return step // pieces, pl.multiple_of((step % pieces) * block, block), 0

    attend_forward(HEADS * pieces, where_of, block, q_ref, k_ref, v_ref, o_ref, s_a, s_b, m_a, m_b)
    out_ref[...] = h_ref[...] + dot(o_ref[...], w_ref[3 * width : 4 * width, :], TN)


def feed(shards, lens, h_ref, weights, vec_ref, cot_ref, y_ref, dh_ref, near, far, gv_ref, up_s, e_s, n_s, y_s, de_s, up_ref, down_ref, g_ref, sems):
    width = h_ref.shape[1]
    rows = h_ref.shape[0]
    hidden = down_ref.shape[0]
    half = hidden // 2
    parts = hidden // width
    piece = hidden // shards // parts
    core = lens[2]
    copies = fetch(weights, 2, up_ref, sems.at[0]), fetch(weights, 3, down_ref, sems.at[1])
    normal, inverse = normalise(h_ref[...])
    n_s[...] = normal
    e_s[...] = (normal * vec_ref[2:3, :] + vec_ref[5:6, :]).astype(BF)
    spot = lax.broadcasted_iota(jnp.int32, (rows, 1), 0) % (rows // PASSES)
    cot = jnp.where(spot < lens[0], cot_ref[...].astype(F32), 0.0)
    df = cot.astype(BF)
    y_s[...] = h_ref[...] + vec_ref[6:7, :]
    de_s[...] = jnp.zeros_like(de_s)
    gv_ref[...] = jnp.zeros_like(gv_ref)
    wait(copies)
    for shard in range(shards):
        for part in range(parts):
            begin = (shard * parts + part) * piece
            up_s[part, shard * piece : (shard + 1) * piece, :] = up_ref[begin : begin + piece, :]

    def body(part, carry):
        place = pl.multiple_of(part * width, width)
        down = down_ref[pl.ds(place, width), :]
        up = up_s[part]
        pre = dot(e_s[...], up, NN) + vec_ref[pl.ds(7 + part, 1), :]
        active = jnp.maximum(pre, 0.0).astype(BF)
        y_s[...] += dot(active, down, NN)
        g_ref[place // half, 1, pl.ds(pl.multiple_of(place % half, width), width), :] = dot(active, df, TN).astype(BF)
        du = jnp.where(pre > 0, dot(df, down, NT), 0.0).astype(BF)
        gv_ref[pl.ds(7 + part, 1), :] = jnp.sum(du.astype(F32), axis=0, keepdims=True)
        gup = dot(e_s[...], du, TN).astype(BF)
        for shard in range(shards):
            begin = (shard * parts + part) * piece
            g_ref[begin // half, 0, pl.ds(pl.multiple_of(begin % half, piece), piece), :] = gup[shard * piece : (shard + 1) * piece, :]
        de_s[...] += dot(du, up, NT)
        return carry

    lax.fori_loop(0, parts, body, 0)
    copies = deliver(core, g_ref, near, far, sems)
    y_ref[...] = y_s[...].astype(BF)
    gv_ref[6:7, :] = jnp.sum(cot, axis=0, keepdims=True)
    back, gain, shift = norm_back(de_s[...], vec_ref[2:3, :], n_s[...], inverse)
    gv_ref[2:3, :] = gain
    gv_ref[5:6, :] = shift
    dh_ref[...] = cot + back
    wait(copies)


def cross_start(dh_ref, weights, o_ref, d_ref, w_ref, sems):
    width = w_ref.shape[0]
    copy = pltpu.make_async_copy(weights.at[pl.ds(7 * width, width)], w_ref, sems.at[0])
    copy.start()
    low = dh_ref[...].astype(BF)
    copy.wait()
    put_grads(d_ref, dot(w_ref[...], low, NT), o_ref, 0, HEADS)


def cross_attend(q_ref, k_ref, v_ref, d_ref, dq_ref, dk_ref, dv_ref, sk, sv):
    rows = q_ref.shape[2]
    slots = k_ref.shape[2]
    block = rows // PASSES

    def body(head, carry):
        place = pl.ds(pl.multiple_of(head * 64, 64), 64)
        for piece in range(PASSES):
            dq, dk, dv = attend_backward(head, piece * block, block, 0, slots, q_ref, k_ref, v_ref, d_ref)
            dq_ref[place, piece * block : (piece + 1) * block] = dq
            if piece == 0:
                sk[...] = dk
                sv[...] = dv
            else:
                dk_ref[place, :] = (sk[...] + dk).astype(BF)
                dv_ref[place, :] = (sv[...] + dv).astype(BF)
        return carry

    lax.fori_loop(0, HEADS, body, 0)


def cross_finish(lens, dh2_ref, weights, dq_ref, dk_ref, dv_ref, o_ref, h_ref, mem_ref, vec_ref, near, far, gmem_ref, dh_ref, gv_ref, w_ref, g_ref, sems):
    width = h_ref.shape[1]
    core = lens[2]
    copy = fetch(weights, 1, w_ref, sems.at[0])
    memory = mem_ref[...]
    normal, inverse = normalise(h_ref[...])
    low = (normal * vec_ref[1:2, :] + vec_ref[4:5, :]).astype(BF)
    dq = dq_ref[...].T
    g_ref[0, :width, :] = dot(low, dq, TN).astype(BF)
    g_ref[1, width:, :] = dot(o_ref[...], dh2_ref[...].astype(BF), NN).astype(BF)
    dk = dk_ref[...].T
    g_ref[0, width:, :] = dot(memory, dk, TN).astype(BF)
    dv = dv_ref[...].T
    g_ref[1, :width, :] = dot(memory, dv, TN).astype(BF)
    copy.wait()
    copies = deliver(core, g_ref, near, far, sems)
    back, gain, shift = norm_back(dot(dq, w_ref[0:width, :], NT), vec_ref[1:2, :], normal, inverse)
    gv_ref[...] = jnp.zeros_like(gv_ref)
    gv_ref[1:2, :] = gain
    gv_ref[4:5, :] = shift
    dh_ref[...] = dh2_ref[...] + back
    gmem_ref[...] = dot(dk, w_ref[width : 2 * width, :], NT) + dot(dv, w_ref[2 * width : 3 * width, :], NT)
    wait(copies)


def self_backward(chunk, chunks, lens, dh_ref, weights, q_ref, k_ref, v_ref, o_ref, x_ref, vec_ref, *refs):
    last = chunk == chunks - 1
    if chunk:
        before, refs = refs[0], refs[1:]
    near, far, out_ref = refs[:3]
    refs = refs[3:]
    if last:
        gv_ref, refs = refs[0], refs[1:]
    d_s, dq_s, dk_s, dv_s, w_ref, g_ref, sems = refs
    width = x_ref.shape[1]
    rows = x_ref.shape[0]
    length = rows // PASSES
    heads = HEADS // chunks
    span = width // chunks
    lanes = slice(chunk * span, (chunk + 1) * span)
    core = lens[2]
    copy = fetch(weights, 0, w_ref, sems.at[0])
    dz = dh_ref[...].astype(BF)
    g_ref[1, width:, :] = dot(o_ref[...], dz[:, lanes], NN).astype(BF)
    copy.wait()
    put_grads(d_s, dot(w_ref[3 * width + chunk * span : 3 * width + (chunk + 1) * span, :], dz, NT), o_ref, chunk * heads, heads)

    def body(head, carry):
        place = pl.ds(pl.multiple_of(head * 64, 64), 64)
        for number in range(PASSES):
            begin = number * length
            dq, dk, dv = attend_backward(head, begin, length, begin, length, q_ref, k_ref, v_ref, d_s, chunk * heads)
            dq_s[place, begin : begin + length] = dq
            dk_s[place, begin : begin + length] = dk.astype(BF)
            dv_s[place, begin : begin + length] = dv.astype(BF)
        return carry

    lax.fori_loop(0, heads, body, 0)
    normal, inverse = normalise(x_ref[...].astype(F32))
    low = (normal * vec_ref[0:1, :] + vec_ref[3:4, :]).astype(BF)
    total = before[...] if chunk else None
    grads = [store[...].T for store in (dq_s, dk_s, dv_s)]
    for number, grad in enumerate(grads):
        g_ref[number // 2, (number % 2) * width : (number % 2 + 1) * width, :] = dot(low, grad, TN).astype(BF)
    copies = deliver(core, g_ref, near, far, sems)
    for number, grad in enumerate(grads):
        part = dot(grad, w_ref[number * width : (number + 1) * width, lanes], NT)
        total = part if total is None else total + part
    if last:
        back, gain, shift = norm_back(total, vec_ref[0:1, :], normal, inverse)
        gv_ref[...] = jnp.zeros_like(gv_ref)
        gv_ref[0:1, :] = gain
        gv_ref[3:4, :] = shift
        out_ref[...] = dh_ref[...] + back
    else:
        out_ref[...] = total
    wait(copies)


def adam(flags, *refs):
    g0, g1, g2, rest, w_ref, state_ref = refs[:6]
    new_ref, upper_ref, lower_ref, g_s, order_s = refs[-5:]
    share = w_ref.shape[0]
    part = share // 4
    g_s[...] = jnp.where(flags[0] == 1, g0[...].astype(F32) + g1[...].astype(F32) + g2[...].astype(F32), rest[...])

    @pl.when(flags[1] == 1)
    def _():
        for lane in range(order_s.shape[0]):
            lanes = slice(lane * 128, (lane + 1) * 128)
            for number in range(4):
                order_s[lane, pl.ds(number, part, stride=4), :] = g_s[number * part : (number + 1) * part, lanes]
            g_s[:, lanes] = order_s[lane]

    moment, second, delta = inner_update(w_ref[...], g_s[...], state_ref[0, 0], state_ref[0, 1], decay_rate)
    new_ref[0, 0] = moment
    new_ref[0, 1] = second
    low = delta.astype(BF)
    upper_ref[...] = low[: share // 2]
    lower_ref[...] = low[share // 2 :]


def outer(replicas, one_a, one_b, two_a, two_b, w_ref, mom_ref, *refs):
    out_ref = refs[-1]
    share = w_ref.shape[0] // 2
    for half, (one, two) in enumerate(((one_a, two_a), (one_b, two_b))):
        rows = slice(half * share, (half + 1) * share)
        mean = (one[...].astype(F32) + two[...].astype(F32)) / replicas
        momentum = outer_push * mom_ref[rows, :] + mean
        out_ref[0, rows, :] = w_ref[rows, :] - rate_outer * (mean + outer_push * momentum)
        out_ref[1, rows, :] = mean
        out_ref[2, rows, :] = momentum


VM = pl.BlockSpec(memory_space=pltpu.VMEM)
SM = pl.BlockSpec(memory_space=pltpu.SMEM)
HB = pl.BlockSpec(memory_space=pl.ANY)


def call(body, name, ins, outs, scratch=(), places=None, grid=(), aliases=None):
    shapes = tuple(jax.ShapeDtypeStruct(shape, kind) for shape, kind in outs)
    return pl.pallas_call(
        body,
        name=name,
        grid=grid,
        input_output_aliases=aliases or {},
        out_shape=shapes,
        in_specs=ins,
        out_specs=tuple(places or [VM] * len(outs)),
        scratch_shapes=[item if not isinstance(item, tuple) else pltpu.VMEM(*item) for item in scratch],
        compiler_params=pltpu.CompilerParams(vmem_limit_bytes=VMEM_LIMIT),
    )


def inner_update(weight, gradient, moment_one, second, shrink):
    moment_new = beta_first * moment_one + (1.0 - beta_first) * gradient
    second_new = beta_second * second + (1.0 - beta_second) * gradient * gradient
    moment_hat = moment_new / (1.0 - beta_first**STEP)
    second_hat = second_new / (1.0 - beta_second**STEP)
    local_weight = weight - rate_inner * (
        moment_hat / (jnp.sqrt(second_hat) + adam_epsilon) + shrink * weight
    )
    return (moment_new, second_new, weight - local_weight)


def swap(values, axis, bit):
    count = lax.axis_size(axis)
    return lax.ppermute(values, axis, [(i, i ^ bit) for i in range(count)])


def total_over(values, axis):
    count = lax.axis_size(axis)
    if count & (count - 1):
        return lax.psum(values, axis)
    bit = 1
    while bit < count:
        values = values + swap(values, axis, bit)
        bit *= 2
    return values


def hop(values, *moves):
    return lax.ppermute(values, "fsdp", [(2 * one + core, 2 * two + core) for one, two in moves for core in range(2)])


def add_low(one, two):
    return (one.astype(F32) + two.astype(F32)).astype(BF)


def triple(one, two, three):
    return one.astype(F32) + two.astype(F32) + three.astype(F32)


def per_device(embed, first_tokens, sample_tokens, seq_len, mem_len, memory, cotangent, params, vecs, inner_state, inner_vecs, outer_mom, outer_vecs):
    groups = lax.axis_size("fsdp")
    replicas = lax.axis_size("rep")
    direct = groups == 8 and replicas == 4
    share, width = params.shape
    hidden = 4 * width
    me = lax.axis_index("fsdp")
    chip = me // 2
    own_up = (me >= 2 * hidden // share) & (me < 3 * hidden // share)
    low = params.astype(BF)
    low = jnp.where(own_up, low.reshape(share // 4, 4, width).transpose(1, 0, 2).reshape(share, width), low)
    count, columns = vecs.shape
    vectors = lax.dynamic_update_slice(jnp.zeros((16, width), BF), vecs.astype(BF), (0, me * columns))
    vectors = total_over(vectors, "fsdp").astype(F32)
    weights = lax.all_gather(low, "fsdp", axis=0, tiled=True)
    core = me % 2 if direct else jnp.zeros((), jnp.int32)
    x = embed[jnp.concatenate([first_tokens[0], sample_tokens[0]])]
    lens = jnp.stack([seq_len[0], mem_len[0], core]).astype(jnp.int32)
    length = first_tokens.shape[1]
    rows = PASSES * length
    cot = cotangent.reshape(rows, width)
    memory = memory[0]
    slots = memory.shape[0]

    heads_n = ((HEADS, AUG, rows), BF)
    heads_m = ((HEADS, AUG, slots), BF)
    flat_n = ((width, rows), BF)
    flat_m = ((width, slots), BF)
    full = ((rows, width), F32)
    half_g = ((hidden // 2, width), BF)
    block_w = ((hidden, width), BF)
    vec_g = ((16, width), F32)
    peak = ((8, length), F32)
    sems = pltpu.SemaphoreType.DMA((2,))
    qs, ks, vs, o_self, h = call(
        self_forward, "self_forward", [SM, VM, HB, VM],
        [heads_n, heads_n, heads_n, flat_n, full],
        [((length, length), F32)] * 2 + [peak] * 2 + [block_w, sems],
    )(lens, x, weights, vectors)
    qc, kc, vc, o_cross, h2 = call(
        cross_forward, "cross_forward", [SM, VM, HB, VM, VM],
        [heads_n, heads_m, heads_m, flat_n, full],
        [((slots, length), F32)] * 2 + [peak] * 2 + [block_w, sems],
    )(lens, h, weights, memory, vectors)
    pair_g = ((2, hidden // 2, width), BF)
    y, dh2, feed_near, feed_far, gv3 = call(
        functools.partial(feed, hidden // min(share, hidden)), "feed", [SM, VM, HB, VM, VM],
        [((rows, width), BF), full, pair_g, pair_g, vec_g],
        [((4, width, width), BF), ((rows, width), BF), full, full, full, block_w, block_w, ((2, 2, hidden // 2, width), BF), sems],
        [VM, VM, HB, HB, VM],
    )(lens, h2, weights, vectors, cot)
    if direct:
        feed_got = swap(feed_far, "fsdp", 1)
    (do_cross,) = call(
        cross_start, "cross_start", [VM, HB, VM], [heads_n], [((width, width), BF), sems],
    )(dh2, weights, o_cross)
    if direct:
        up_sum, down_sum = add_low(feed_near[0], feed_got[0]), add_low(feed_near[1], feed_got[1])
        do_cross, up_sum, down_sum = lax.optimization_barrier((do_cross, up_sum, down_sum))
        up_got = hop(up_sum, (0, 1), (3, 2))
        down_got = hop(down_sum, (0, 1), (2, 3))
    dqt, dkt, dvt = call(
        cross_attend, "cross_attend", [VM] * 4, [flat_n, flat_m, flat_m], [((64, slots), F32)] * 2,
    )(qc, kc, vc, do_cross)
    cross_near, cross_far, g_mem, dh, gv2 = call(
        cross_finish, "cross_finish", [SM, VM, HB] + [VM] * 7,
        [half_g, half_g, (memory.shape, F32), full, vec_g],
        [block_w, pair_g, sems],
        [HB, HB, VM, VM, VM],
    )(lens, dh2, weights, dqt, dkt, dvt, o_cross, h, memory, vectors)
    if direct:
        cross_got = swap(cross_far, "fsdp", 1)
    chunks = 2
    span = width // chunks
    chunk_g = ((hidden // 2, span), BF)
    scratch = [((HEADS // chunks, AUG, rows), BF)] + [((span, rows), BF)] * 3 + [block_w, ((2, hidden // 2, span), BF), sems]
    near_a, far_a, total = call(
        functools.partial(self_backward, 0, chunks), "self_backward_a", [SM, VM, HB] + [VM] * 6,
        [chunk_g, chunk_g, full], scratch, [HB, HB, VM],
    )(lens, dh, weights, qs, ks, vs, o_self, x, vectors)
    if direct:
        got_a = swap(far_a, "fsdp", 1)
        cross_sum = add_low(cross_near, cross_got)
        up_late = add_low(up_sum, up_got)
        down_late = add_low(down_sum, down_got)
        total, cross_sum, up_late, down_late = lax.optimization_barrier((total, cross_sum, up_late, down_late))
        cross_hop = hop(cross_sum, (0, 1), (3, 2))
        up_last = hop(up_late, (1, 2))
        down_last = hop(down_late, (1, 3))
    near_b, far_b, g_in, gv1 = call(
        functools.partial(self_backward, 1, chunks), "self_backward_b", [SM, VM, HB] + [VM] * 7,
        [chunk_g, chunk_g, full, vec_g], scratch, [HB, HB, VM, VM],
    )(lens, dh, weights, qs, ks, vs, o_self, x, vectors, total)

    if direct:
        sum_a = add_low(near_a, got_a)
        hop_a = hop(sum_a, (1, 0), (3, 2))
        sum_b = add_low(near_b, swap(far_b, "fsdp", 1))
        hop_b = hop(sum_b, (1, 0), (3, 2))
        cross_last = hop(add_low(cross_sum, cross_hop), (2, 1))
        last_a = hop(add_low(sum_a, hop_a), (2, 0))
        last_b = hop(add_low(sum_b, hop_b), (2, 0))
        firsts = [(sum_a, hop_a, last_a), (sum_b, hop_b, last_b)]
        rest = triple(cross_sum, cross_hop, cross_last)
        rest = jnp.where(chip == 2, triple(up_sum, up_got, up_last), rest)
        rest = jnp.where(chip == 3, triple(down_sum, down_got, down_last), rest)
        flag = chip == 0
    else:
        whole = [jnp.concatenate([near_a, near_b], axis=1), jnp.concatenate([far_a, far_b], axis=1), cross_near, cross_far]
        whole += [feed_near[0], feed_far[0], feed_near[1], feed_far[1]]
        rest = lax.psum_scatter(jnp.concatenate(whole), "fsdp", scatter_dimension=0, tiled=True).astype(F32)
        firsts = [[jnp.zeros((share, span), BF)] * 3] * chunks
        flag = False
    gv = total_over(gv1 + gv2 + gv3, "fsdp")
    grad_v = lax.dynamic_slice(gv, (0, me * columns), (count, columns))
    flags = jnp.stack([jnp.asarray(flag), own_up]).astype(jnp.int32)
    inner_new = param_results = None
    deltas = []
    for chunk in range(chunks):
        lanes = pl.BlockSpec((share, span), lambda i, c=chunk: (0, c))
        whole = pl.BlockSpec((share, span), lambda i: (0, 0))
        part = pl.BlockSpec((share // 2, span), lambda i: (0, 0))
        state = pl.BlockSpec((1, 2, share, span), lambda i, c=chunk: (0, 0, 0, c))
        inner_new, upper, lower = call(
            adam, "adam", [SM] + [whole] * 3 + [lanes, lanes, state] + [HB] * min(chunk, 1),
            [(inner_state.shape, F32)] + [((share // 2, span), BF)] * 2,
            [((share, span), F32), ((span // 128, share, 128), F32)],
            [state, part, part], (1,), {7: 0} if chunk else None,
        )(flags, *firsts[chunk], rest, params, inner_state, *([inner_new] if chunk else []))
        deltas.append((upper, lower))
    for chunk, (upper, lower) in enumerate(deltas):
        if replicas == 4:
            upper = add_low(upper, swap(upper, "rep", 1))
            lower = add_low(lower, swap(lower, "rep", 2))
            others = [swap(upper, "rep", 2), swap(lower, "rep", 1)]
        else:
            upper, lower = lax.psum(upper, "rep"), lax.psum(lower, "rep")
            others = [jnp.zeros_like(upper), jnp.zeros_like(lower)]
        lanes = pl.BlockSpec((share, span), lambda i, c=chunk: (0, c))
        part = pl.BlockSpec((share // 2, span), lambda i: (0, 0))
        (param_results,) = call(
            functools.partial(outer, replicas), "outer", [part] * 4 + [lanes, lanes] + [HB] * min(chunk, 1),
            [((3, share, width), F32)], (),
            [pl.BlockSpec((3, share, span), lambda i, c=chunk: (0, 0, c))], (1,), {6: 0} if chunk else None,
        )(upper, lower, *others, params, outer_mom, *([param_results] if chunk else []))
    moment_v, second_v, delta_v = inner_update(vecs, grad_v, inner_vecs[0, 0], inner_vecs[0, 1], 0.0)
    mean_v = total_over(delta_v.astype(BF), "rep").astype(F32) / replicas
    momentum_v = outer_push * outer_vecs + mean_v
    new_v = vecs - rate_outer * (mean_v + outer_push * momentum_v)
    return (
        y.reshape(PASSES, 1, length, width),
        g_in.reshape(PASSES, 1, length, width),
        g_mem[None],
        param_results,
        jnp.stack([new_v, mean_v, momentum_v]),
        inner_new,
        jnp.stack([moment_v, second_v])[None],
    )


def solution(mesh):
    both = ("rep", "fsdp")
    return jax.shard_map(
        per_device,
        mesh=mesh,
        in_specs=(
            P(),
            P(both, None),
            P(both, None),
            P(both),
            P(both),
            P(both, None, None),
            P(None, both, None, None),
            P("fsdp", None),
            P(None, "fsdp"),
            P("rep", None, "fsdp", None),
            P("rep", None, None, "fsdp"),
            P("fsdp", None),
            P(None, "fsdp"),
        ),
        out_specs=(
            P(None, both, None, None),
            P(None, both, None, None),
            P(both, None, None),
            P(None, "fsdp", None),
            P(None, None, "fsdp"),
            P("rep", None, "fsdp", None),
            P("rep", None, None, "fsdp"),
        ),
        check_vma=False,
    )
```

```python
import functools
import math

import jax
import jax.numpy as jnp
from jax import lax
from jax.experimental import pallas as pl
from jax.experimental.pallas import tpu as pltpu
from jax.sharding import PartitionSpec as P

HEADS = 8
STEP = 8
PASSES = 2
AUG = 80
norm_epsilon = 1e-05
beta_first = 0.9
beta_second = 0.999
adam_epsilon = 1e-08
rate_inner = 0.1
rate_outer = 0.7
outer_push = 0.9
decay_rate = 0.01

BF = jnp.bfloat16
F32 = jnp.float32
NN = (((1,), (0,)), ((), ()))
NT = (((1,), (1,)), ((), ()))
TN = (((0,), (0,)), ((), ()))
TT = (((0,), (1,)), ((), ()))


def dot(left, right, dims):
    return lax.dot_general(left, right, dims, preferred_element_type=F32)


def normalise(values):
    centre = values - jnp.mean(values, axis=-1, keepdims=True)
    spread = jnp.mean(centre * centre, axis=-1, keepdims=True)
    inverse = lax.rsqrt(spread + norm_epsilon)
    return centre * inverse, inverse


def norm_back(grad_out, gain_row, normal, inverse):
    grad_normal = grad_out * gain_row
    mean_grad = jnp.mean(grad_normal, axis=-1, keepdims=True)
    mean_proj = jnp.mean(grad_normal * normal, axis=-1, keepdims=True)
    grad_in = inverse * (grad_normal - mean_grad - normal * mean_proj)
    return grad_in, jnp.sum(grad_out * normal, axis=0, keepdims=True), jnp.sum(grad_out, axis=0, keepdims=True)


def thirds(row):
    high = row.astype(BF)
    rest = row - high.astype(F32)
    middle = rest.astype(BF)
    low = (rest - middle.astype(F32)).astype(BF)
    return high.astype(F32), middle.astype(F32), low.astype(F32)


def tail_rows(width, rows):
    place = lax.broadcasted_iota(jnp.int32, (AUG - 64, width), 0)
    tail = jnp.zeros((AUG - 64, width), F32)
    for number, row in enumerate(rows):
        tail = jnp.where(place == number, row, tail)
    return tail.astype(BF)


def put_heads(target, matrix_t, scale, tail):
    low = matrix_t.astype(BF)
    if scale != 1.0:
        low = low * BF(scale)
    size = low.shape[0] // HEADS
    for head in range(HEADS):
        target[head, :size, :] = low[head * size : (head + 1) * size]
        target[head, size:, :] = tail


def key_tail(width, count, period):
    spot = lax.broadcasted_iota(jnp.int32, (1, width), 1) % period
    bias = jnp.where(spot < count, 0.0, -1e30)
    return tail_rows(width, [bias, 1.0, 1.0, 1.0])


def attend_forward(units, where_of, block, q_ref, k_ref, v_ref, o_ref, s_a, s_b, m_a, m_b):
    keys = s_a.shape[0]

    def scores(step, store, peak):
        head, first, key_first = where_of(jnp.minimum(step, units - 1))
        value = dot(k_ref[head, :, pl.ds(key_first, keys)], q_ref[head, :, pl.ds(first, block)], TN)
        store[...] = value
        peak[...] = jnp.broadcast_to(jnp.max(value, axis=0, keepdims=True), peak.shape)

    def finish(step, store, peak):
        head, first, key_first = where_of(step)
        top = peak[0:1, :]
        weight = jnp.exp(store[...] - top).astype(BF)
        mixed = dot(v_ref[head, :, pl.ds(key_first, keys)], weight, NN)
        total = mixed[64:65, :]
        o_ref[pl.ds(pl.multiple_of(head * 64, 64), 64), pl.ds(first, block)] = (mixed[:64] * (1.0 / total)).astype(BF)
        high, middle, low = thirds(top + jnp.log(total))
        q_ref[head, 64:, pl.ds(first, block)] = tail_rows(block, [1.0, -high, -middle, -low])

    scores(0, s_a, m_a)

    def body(pair, carry):
        step = 2 * pair
        scores(step + 1, s_b, m_b)
        finish(step, s_a, m_a)
        scores(step + 2, s_a, m_a)
        finish(step + 1, s_b, m_b)
        return carry

    lax.fori_loop(0, units // 2 - 1, body, 0)
    step = units - 2
    scores(step + 1, s_b, m_b)
    finish(step, s_a, m_a)
    finish(step + 1, s_b, m_b)


def attend_backward(head, first, block, key_first, keys, q_ref, k_ref, v_ref, d_ref):
    here = pl.ds(first, block)
    there = pl.ds(key_first, keys)
    grad = d_ref[head, :, here]
    query = q_ref[head, :, here]
    key_t = k_ref[head, :, there]
    weight = jnp.exp(dot(query, key_t, TN))
    grad_scores = (weight * dot(grad, v_ref[head, :, there], TN)).astype(BF)
    grad_value = dot(grad[:64], weight.astype(BF), NN)
    grad_key = dot(query[:64], grad_scores, NN)
    grad_query = dot(key_t[:64], grad_scores, NT) * 0.125
    return grad_query.astype(BF), grad_key, grad_value


def put_grads(d_ref, grad_t, o_ref, skip, heads):
    low = grad_t.astype(BF)
    for head in range(heads):
        part = low[head * 64 : (head + 1) * 64]
        both = part.astype(F32) * o_ref[(skip + head) * 64 : (skip + head + 1) * 64, :].astype(F32)
        high, middle, rest = thirds(jnp.sum(both, axis=0, keepdims=True))
        d_ref[head, :64, :] = part
        d_ref[head, 64:, :] = tail_rows(low.shape[1], [-high, -middle, -rest])


def fetch(lens, weights, block, target, sem, first=0):
    rows = target.shape[0]
    if len(weights) == 1:
        begin = block * weights[0].shape[0] // 4 + first
        pltpu.make_async_copy(weights[0].at[pl.ds(begin, rows)], target, sem).start()
        return
    core, chip, rank = lens[2], lens[3], lens[4]
    half = weights[0].shape[0]
    quarter = half // 4
    for side in range(2):
        own, mine, by_x, by_y, upper, lower = weights[6 * side : 6 * side + 6]
        owner = core if side == 0 else 1 - core

        def put(source, place, target=target, owner=owner):
            begin = owner * half + place
            size = source.shape[0]

            def start():
                pltpu.make_async_copy(source, target.at[pl.ds(pl.multiple_of(begin - first, 16), size)], sem).start()

            if first == 0:
                start()
            else:
                pl.when(begin >= first)(start)

        @pl.when(chip == block)
        def _(own=own, put=put):
            for part in range(4):
                put(own.at[pl.ds(part * quarter, quarter)], part * quarter)

        @pl.when(chip != block)
        def _(mine=mine, by_x=by_x, by_y=by_y, upper=upper, lower=lower, put=put):
            slot = (block + 3 - chip) % 4
            put(mine.at[slot], rank * quarter)
            put(by_x.at[slot], (rank ^ 1) * quarter)
            put(by_y.at[slot], (rank ^ 2) * quarter)
            put(upper.at[slot], (rank ^ 3) * quarter)
            put(lower.at[slot], (rank ^ 3) * quarter + quarter // 2)


def fetched(target, sem):
    pltpu.make_async_copy(target, target, sem).wait()


def deliver(core, source, near, far, sems):
    first = pltpu.make_async_copy(source.at[core], near, sems.at[0])
    second = pltpu.make_async_copy(source.at[1 - core], far, sems.at[1])
    first.start()
    second.start()
    return first, second


def wait(copies):
    for copy in copies:
        copy.wait()


def self_forward(many, lens, *refs):
    weights, refs = refs[:many], refs[many:]
    x_ref, vec_ref, q_ref, k_ref, v_ref, o_ref, h_ref, s_a, s_b, m_a, m_b, w_ref, sems = refs
    width = x_ref.shape[1]
    rows = x_ref.shape[0]
    length = rows // PASSES
    fetch(lens, weights, 0, w_ref, sems.at[0])
    x = x_ref[...].astype(F32)
    normal, _ = normalise(x)
    low = (normal * vec_ref[0:1, :] + vec_ref[3:4, :]).astype(BF)
    fetched(w_ref, sems.at[0])
    put_heads(q_ref, dot(w_ref[0:width, :], low, TT), 0.125, tail_rows(rows, [1.0]))
    put_heads(k_ref, dot(w_ref[width : 2 * width, :], low, TT), 1.0, key_tail(rows, lens[0], length))
    put_heads(v_ref, dot(w_ref[2 * width : 3 * width, :], low, TT), 1.0, tail_rows(rows, [1.0, 1.0, 1.0]))

    def where_of(step):
        place = pl.multiple_of((step % PASSES) * length, length)
        return step // PASSES, place, place

    attend_forward(HEADS * PASSES, where_of, length, q_ref, k_ref, v_ref, o_ref, s_a, s_b, m_a, m_b)
    h_ref[...] = x_ref[...].astype(F32) + dot(o_ref[...], w_ref[3 * width : 4 * width, :], TN)


def cross_forward(many, lens, *refs):
    weights, refs = refs[:many], refs[many:]
    h_ref, mem_ref, vec_ref, q_ref, k_ref, v_ref, o_ref, out_ref, s_a, s_b, m_a, m_b, w_ref, sems = refs
    width = h_ref.shape[1]
    rows = h_ref.shape[0]
    slots = mem_ref.shape[0]
    block = s_a.shape[1]
    fetch(lens, weights, 1, w_ref, sems.at[0])
    normal, _ = normalise(h_ref[...])
    low = (normal * vec_ref[1:2, :] + vec_ref[4:5, :]).astype(BF)
    fetched(w_ref, sems.at[0])
    memory = mem_ref[...]
    put_heads(q_ref, dot(w_ref[0:width, :], low, TT), 0.125, tail_rows(rows, [1.0]))
    put_heads(k_ref, dot(w_ref[width : 2 * width, :], memory, TT), 1.0, key_tail(slots, lens[1], slots))
    put_heads(v_ref, dot(w_ref[2 * width : 3 * width, :], memory, TT), 1.0, tail_rows(slots, [1.0, 1.0, 1.0]))
    pieces = rows // block

    def where_of(step):
        return step // pieces, pl.multiple_of((step % pieces) * block, block), 0

    attend_forward(HEADS * pieces, where_of, block, q_ref, k_ref, v_ref, o_ref, s_a, s_b, m_a, m_b)
    out_ref[...] = h_ref[...] + dot(o_ref[...], w_ref[3 * width : 4 * width, :], TN)


def feed(shards, many, lens, *refs):
    weights, refs = refs[:many], refs[many:]
    h_ref, vec_ref, cot_ref, y_ref, dh_ref, near, far, gv_ref, up_s, e_s, n_s, y_s, de_s, up_ref, down_ref, g_ref, sems = refs
    width = h_ref.shape[1]
    rows = h_ref.shape[0]
    hidden = down_ref.shape[0]
    half = hidden // 2
    parts = hidden // width
    piece = hidden // shards // parts
    core = lens[2]
    fetch(lens, weights, 2, up_ref, sems.at[0])
    fetch(lens, weights, 3, down_ref, sems.at[1])
    normal, inverse = normalise(h_ref[...])
    n_s[...] = normal
    e_s[...] = (normal * vec_ref[2:3, :] + vec_ref[5:6, :]).astype(BF)
    spot = lax.broadcasted_iota(jnp.int32, (rows, 1), 0) % (rows // PASSES)
    cot = jnp.where(spot < lens[0], cot_ref[...].astype(F32), 0.0)
    df = cot.astype(BF)
    y_s[...] = h_ref[...] + vec_ref[6:7, :]
    de_s[...] = jnp.zeros_like(de_s)
    gv_ref[...] = jnp.zeros_like(gv_ref)
    fetched(up_ref, sems.at[0])
    fetched(down_ref, sems.at[1])
    for shard in range(shards):
        for part in range(parts):
            begin = (shard * parts + part) * piece
            up_s[part, shard * piece : (shard + 1) * piece, :] = up_ref[begin : begin + piece, :]

    def body(part, carry):
        place = pl.multiple_of(part * width, width)
        down = down_ref[pl.ds(place, width), :]
        up = up_s[part]
        pre = dot(e_s[...], up, NN) + vec_ref[pl.ds(7 + part, 1), :]
        active = jnp.maximum(pre, 0.0).astype(BF)
        y_s[...] += dot(active, down, NN)
        g_ref[place // half, 1, pl.ds(pl.multiple_of(place % half, width), width), :] = dot(active, df, TN).astype(BF)
        du = jnp.where(pre > 0, dot(df, down, NT), 0.0).astype(BF)
        gv_ref[pl.ds(7 + part, 1), :] = jnp.sum(du.astype(F32), axis=0, keepdims=True)
        gup = dot(e_s[...], du, TN).astype(BF)
        for shard in range(shards):
            begin = (shard * parts + part) * piece
            g_ref[begin // half, 0, pl.ds(pl.multiple_of(begin % half, piece), piece), :] = gup[shard * piece : (shard + 1) * piece, :]
        de_s[...] += dot(du, up, NT)
        return carry

    lax.fori_loop(0, parts, body, 0)
    copies = deliver(core, g_ref, near, far, sems)
    y_ref[...] = y_s[...].astype(BF)
    gv_ref[6:7, :] = jnp.sum(cot, axis=0, keepdims=True)
    back, gain, shift = norm_back(de_s[...], vec_ref[2:3, :], n_s[...], inverse)
    gv_ref[2:3, :] = gain
    gv_ref[5:6, :] = shift
    dh_ref[...] = cot + back
    wait(copies)


def cross_start(many, lens, *refs):
    weights, refs = refs[:many], refs[many:]
    dh_ref, o_ref, d_ref, w_ref, sems = refs
    width = dh_ref.shape[1]
    fetch(lens, weights, 1, w_ref, sems.at[0])
    low = dh_ref[...].astype(BF)
    fetched(w_ref, sems.at[0])
    put_grads(d_ref, dot(w_ref[3 * width :, :], low, NT), o_ref, 0, HEADS)


def cross_attend(q_ref, k_ref, v_ref, d_ref, dq_ref, dk_ref, dv_ref, sk, sv):
    rows = q_ref.shape[2]
    slots = k_ref.shape[2]
    block = rows // PASSES

    def body(head, carry):
        place = pl.ds(pl.multiple_of(head * 64, 64), 64)
        for piece in range(PASSES):
            dq, dk, dv = attend_backward(head, piece * block, block, 0, slots, q_ref, k_ref, v_ref, d_ref)
            dq_ref[place, piece * block : (piece + 1) * block] = dq
            if piece == 0:
                sk[...] = dk
                sv[...] = dv
            else:
                dk_ref[place, :] = (sk[...] + dk).astype(BF)
                dv_ref[place, :] = (sv[...] + dv).astype(BF)
        return carry

    lax.fori_loop(0, HEADS, body, 0)


def cross_finish(many, lens, *refs):
    weights, refs = refs[:many], refs[many:]
    dh2_ref, dq_ref, dk_ref, dv_ref, o_ref, h_ref, mem_ref, vec_ref, near, far, gmem_ref, dh_ref, gv_ref, w_ref, g_ref, sems = refs
    width = h_ref.shape[1]
    core = lens[2]
    fetch(lens, weights, 1, w_ref, sems.at[0])
    memory = mem_ref[...]
    normal, inverse = normalise(h_ref[...])
    low = (normal * vec_ref[1:2, :] + vec_ref[4:5, :]).astype(BF)
    dq = dq_ref[...].T
    g_ref[0, :width, :] = dot(low, dq, TN).astype(BF)
    g_ref[1, width:, :] = dot(o_ref[...], dh2_ref[...].astype(BF), NN).astype(BF)
    dk = dk_ref[...].T
    g_ref[0, width:, :] = dot(memory, dk, TN).astype(BF)
    dv = dv_ref[...].T
    g_ref[1, :width, :] = dot(memory, dv, TN).astype(BF)
    fetched(w_ref, sems.at[0])
    copies = deliver(core, g_ref, near, far, sems)
    back, gain, shift = norm_back(dot(dq, w_ref[0:width, :], NT), vec_ref[1:2, :], normal, inverse)
    gv_ref[...] = jnp.zeros_like(gv_ref)
    gv_ref[1:2, :] = gain
    gv_ref[4:5, :] = shift
    dh_ref[...] = dh2_ref[...] + back
    gmem_ref[...] = dot(dk, w_ref[width : 2 * width, :], NT) + dot(dv, w_ref[2 * width : 3 * width, :], NT)
    wait(copies)


def self_backward(chunk, chunks, many, lens, *refs):
    weights, refs = refs[:many], refs[many:]
    dh_ref, q_ref, k_ref, v_ref, o_ref, x_ref, vec_ref = refs[:7]
    refs = refs[7:]
    last = chunk == chunks - 1
    if chunk:
        before, refs = refs[0], refs[1:]
    near, far, out_ref = refs[:3]
    refs = refs[3:]
    if last:
        gv_ref, refs = refs[0], refs[1:]
    d_s, dq_s, dk_s, dv_s, w_ref, g_ref, sems = refs
    width = x_ref.shape[1]
    rows = x_ref.shape[0]
    length = rows // PASSES
    heads = HEADS // chunks
    span = width // chunks
    lanes = slice(chunk * span, (chunk + 1) * span)
    core = lens[2]
    fetch(lens, weights, 0, w_ref, sems.at[0])
    dz = dh_ref[...].astype(BF)
    g_ref[1, width:, :] = dot(o_ref[...], dz[:, lanes], NN).astype(BF)
    fetched(w_ref, sems.at[0])
    put_grads(d_s, dot(w_ref[3 * width + chunk * span : 3 * width + (chunk + 1) * span, :], dz, NT), o_ref, chunk * heads, heads)

    def body(head, carry):
        place = pl.ds(pl.multiple_of(head * 64, 64), 64)
        for number in range(PASSES):
            begin = number * length
            dq, dk, dv = attend_backward(head, begin, length, begin, length, q_ref, k_ref, v_ref, d_s)
            dq_s[place, begin : begin + length] = dq
            dk_s[place, begin : begin + length] = dk.astype(BF)
            dv_s[place, begin : begin + length] = dv.astype(BF)
        return carry

    lax.fori_loop(0, heads, body, 0)
    normal, inverse = normalise(x_ref[...].astype(F32))
    low = (normal * vec_ref[0:1, :] + vec_ref[3:4, :]).astype(BF)
    total = before[...] if chunk else None
    grads = [store[...].T for store in (dq_s, dk_s, dv_s)]
    for number, grad in enumerate(grads):
        g_ref[number // 2, (number % 2) * width : (number % 2 + 1) * width, :] = dot(low, grad, TN).astype(BF)
    copies = deliver(core, g_ref, near, far, sems)
    for number, grad in enumerate(grads):
        part = dot(grad, w_ref[number * width : (number + 1) * width, lanes], NT)
        total = part if total is None else total + part
    if last:
        back, gain, shift = norm_back(total, vec_ref[0:1, :], normal, inverse)
        gv_ref[...] = jnp.zeros_like(gv_ref)
        gv_ref[0:1, :] = gain
        gv_ref[3:4, :] = shift
        out_ref[...] = dh_ref[...] + back
    else:
        out_ref[...] = total
    wait(copies)


def prepare(flags, w_ref, low_ref, piece_ref, order_s):
    share = w_ref.shape[0]
    part = share // 4

    @pl.when(flags[0] == 0)
    def _():
        low_ref[...] = w_ref[...].astype(BF)

    @pl.when(flags[0] == 1)
    def _():
        for lane in range(order_s.shape[0]):
            lanes = slice(lane * 128, (lane + 1) * 128)
            order_s[lane] = w_ref[:, lanes]
            for number in range(4):
                low_ref[number * part : (number + 1) * part, lanes] = order_s[lane, pl.ds(number, part, stride=4), :].astype(BF)

    size = piece_ref.shape[0]
    piece_ref[...] = low_ref[pl.ds(pl.multiple_of(flags[1] * size, size), size), :]


def adam(chunk, blocks, flags, *refs):
    parts = refs[: 3 * blocks]
    w_ref, state_ref = refs[3 * blocks : 3 * blocks + 2]
    new_ref, upper_ref, lower_ref, g_s, order_s, three_s, sems = refs[-7:]
    share, span = w_ref.shape
    part = share // 4
    lanes = pl.ds(chunk * span, span)
    for block in range(blocks):

        @pl.when(flags[0] == block)
        def _(block=block):
            for number in range(3):
                source = parts[3 * block + number]
                source = source if source.shape[1] == span else source.at[:, lanes]
                pltpu.make_async_copy(source, three_s.at[number], sems.at[number]).start()

    for number in range(3):
        pltpu.make_async_copy(three_s.at[number], three_s.at[number], sems.at[number]).wait()
    g_s[...] = three_s[0].astype(F32) + three_s[1].astype(F32) + three_s[2].astype(F32)

    @pl.when(flags[1] == 1)
    def _():
        for lane in range(order_s.shape[0]):
            lanes = slice(lane * 128, (lane + 1) * 128)
            for number in range(4):
                order_s[lane, pl.ds(number, part, stride=4), :] = g_s[number * part : (number + 1) * part, lanes]
            g_s[:, lanes] = order_s[lane]

    moment, second, delta = inner_update(w_ref[...], g_s[...], state_ref[0, 0], state_ref[0, 1], decay_rate)
    new_ref[0, 0] = moment
    new_ref[0, 1] = second
    low = delta.astype(BF)
    upper_ref[...] = low[: share // 2]
    lower_ref[...] = low[share // 2 :]


def outer(replicas, one_a, one_b, two_a, two_b, w_ref, mom_ref, *refs):
    out_ref = refs[-1]
    share = w_ref.shape[0] // 2
    for half, (one, two) in enumerate(((one_a, two_a), (one_b, two_b))):
        rows = slice(half * share, (half + 1) * share)
        mean = (one[...].astype(F32) + two[...].astype(F32)) / replicas
        momentum = outer_push * mom_ref[rows, :] + mean
        out_ref[0, rows, :] = w_ref[rows, :] - rate_outer * (mean + outer_push * momentum)
        out_ref[1, rows, :] = mean
        out_ref[2, rows, :] = momentum


VM = pl.BlockSpec(memory_space=pltpu.VMEM)
SM = pl.BlockSpec(memory_space=pltpu.SMEM)
HB = pl.BlockSpec(memory_space=pl.ANY)
FAR = pl.BlockSpec(memory_space=pltpu.HBM)


def call(body, name, ins, outs, scratch=(), places=None, grid=(), aliases=None, room=24):
    shapes = tuple(jax.ShapeDtypeStruct(shape, kind) for shape, kind in outs)
    return pl.pallas_call(
        body,
        name=name,
        grid=grid,
        cost_estimate=pl.CostEstimate(flops=0, transcendentals=0, bytes_accessed=0),
        input_output_aliases=aliases or {},
        out_shape=shapes,
        in_specs=ins,
        out_specs=tuple(places or [VM] * len(outs)),
        scratch_shapes=[item if not isinstance(item, tuple) else pltpu.VMEM(*item) for item in scratch],
        compiler_params=pltpu.CompilerParams(vmem_limit_bytes=room << 20),
    )


def inner_update(weight, gradient, moment_one, second, shrink):
    moment_new = beta_first * moment_one + (1.0 - beta_first) * gradient
    second_new = beta_second * second + (1.0 - beta_second) * gradient * gradient
    moment_hat = moment_new / (1.0 - beta_first**STEP)
    second_hat = second_new / (1.0 - beta_second**STEP)
    local_weight = weight - rate_inner * (
        moment_hat / (jnp.sqrt(second_hat) + adam_epsilon) + shrink * weight
    )
    return (moment_new, second_new, weight - local_weight)


def swap(values, axis, bit):
    count = lax.axis_size(axis)
    return lax.ppermute(values, axis, [(i, i ^ bit) for i in range(count)])


def total_over(values, axis):
    count = lax.axis_size(axis)
    if count & (count - 1):
        return lax.psum(values, axis)
    bit = 1
    while bit < count:
        values = values + swap(values, axis, bit)
        bit *= 2
    return values


def hop(values, *moves):
    return lax.ppermute(values, "fsdp", [(2 * one + core, 2 * two + core) for one, two in moves for core in range(2)])


def add_low(one, two):
    return (one.astype(F32) + two.astype(F32)).astype(BF)


def cycle(values, distance):
    count = lax.axis_size("fsdp")
    return lax.ppermute(values, "fsdp", [((to + 2 * distance) % count, to) for to in range(count)])


def gather_weights(low, piece, vectors, x):
    half = piece.shape[0] // 2
    low_far = swap(low, "fsdp", 1)
    vectors = vectors + swap(vectors, "fsdp", 1)
    slots = [cycle(piece, distance) for distance in (1, 2, 3)]
    vectors = vectors + swap(vectors, "fsdp", 2)
    slots, vectors, x = lax.optimization_barrier((slots, vectors, x))
    mine = jnp.stack(slots)
    by_x = swap(mine, "rep", 1)
    by_y = swap(mine, "rep", 2)
    vectors = vectors + swap(vectors, "fsdp", 4)
    mine_far = swap(mine, "fsdp", 1)
    upper = swap(by_x[:, :half], "rep", 2)
    lower = swap(by_y[:, half:], "rep", 1)
    by_x_far = swap(by_x, "fsdp", 1)
    by_y_far = swap(by_y, "fsdp", 1)
    near = [low, mine, by_x, by_y, upper, lower]
    far = [low_far, mine_far, by_x_far, by_y_far, swap(upper, "fsdp", 1), swap(lower, "fsdp", 1)]
    return near + far, vectors, x


def per_device(embed, first_tokens, sample_tokens, seq_len, mem_len, memory, cotangent, params, vecs, inner_state, inner_vecs, outer_mom, outer_vecs):
    groups = lax.axis_size("fsdp")
    replicas = lax.axis_size("rep")
    direct = groups == 8 and replicas == 4
    share, width = params.shape
    hidden = 4 * width
    me = lax.axis_index("fsdp")
    chip = me // 2
    own_up = (me >= 2 * hidden // share) & (me < 3 * hidden // share)
    rank = lax.axis_index("rep")
    count, columns = vecs.shape
    vectors = lax.dynamic_update_slice(jnp.zeros((16, width), BF), vecs.astype(BF), (0, me * columns))
    low, piece = call(
        prepare, "prepare", [SM, VM], [((share, width), BF), ((share // 4, width), BF)],
        [((width // 128, share, 128), F32)],
    )(jnp.stack([own_up, rank if direct else 0]).astype(jnp.int32), params)
    x = embed[jnp.concatenate([first_tokens[0], sample_tokens[0]])]
    if direct:
        weights, vectors, x = gather_weights(low, piece, vectors, x)
        core = me % 2
    else:
        weights = [lax.all_gather(low, "fsdp", axis=0, tiled=True)]
        vectors = total_over(vectors, "fsdp")
        core = 0
    vectors = vectors.astype(F32)
    lens = jnp.stack([seq_len[0], mem_len[0], core, chip, rank]).astype(jnp.int32)
    many = len(weights)
    far_w = [FAR] * many
    length = first_tokens.shape[1]
    rows = PASSES * length
    cot = cotangent.reshape(rows, width)
    memory = memory[0]
    slots = memory.shape[0]

    heads_n = ((HEADS, AUG, rows), BF)
    heads_m = ((HEADS, AUG, slots), BF)
    flat_n = ((width, rows), BF)
    flat_m = ((width, slots), BF)
    full = ((rows, width), F32)
    half_g = ((hidden // 2, width), BF)
    block_w = ((hidden, width), BF)
    vec_g = ((16, width), F32)
    peak = ((8, length), F32)
    sems = pltpu.SemaphoreType.DMA((2,))
    qs, ks, vs, o_self, h = call(
        functools.partial(self_forward, many), "self_forward", [SM] + far_w + [VM] * 2,
        [heads_n, heads_n, heads_n, flat_n, full],
        [((length, length), F32)] * 2 + [peak] * 2 + [block_w, sems],
    )(lens, *weights, x, vectors)
    qc, kc, vc, o_cross, h2 = call(
        functools.partial(cross_forward, many), "cross_forward", [SM] + far_w + [VM] * 3,
        [heads_n, heads_m, heads_m, flat_n, full],
        [((slots, length), F32)] * 2 + [peak] * 2 + [block_w, sems],
    )(lens, *weights, h, memory, vectors)
    pair_g = ((2, hidden // 2, width), BF)
    y, dh2, feed_near, feed_far, gv3 = call(
        functools.partial(feed, hidden // min(share, hidden), many), "feed", [SM] + far_w + [VM] * 3,
        [((rows, width), BF), full, pair_g, pair_g, vec_g],
        [((4, width, width), BF), ((rows, width), BF), full, full, full, block_w, block_w, ((2, 2, hidden // 2, width), BF), sems],
        [VM, VM, HB, HB, VM], room=32,
    )(lens, *weights, h2, vectors, cot)
    if direct:
        feed_got = swap(feed_far, "fsdp", 1)
    (do_cross,) = call(
        functools.partial(cross_start, many), "cross_start", [SM] + far_w + [VM] * 2, [heads_n], [block_w, sems],
    )(lens, *weights, dh2, o_cross)
    if direct:
        up_sum, down_sum = add_low(feed_near[0], feed_got[0]), add_low(feed_near[1], feed_got[1])
        do_cross, up_sum, down_sum = lax.optimization_barrier((do_cross, up_sum, down_sum))
        up_got = hop(up_sum, (0, 1), (3, 2))
        down_got = hop(down_sum, (0, 1), (2, 3))
    dqt, dkt, dvt = call(
        cross_attend, "cross_attend", [VM] * 4, [flat_n, flat_m, flat_m], [((64, slots), F32)] * 2,
    )(qc, kc, vc, do_cross)
    cross_near, cross_far, g_mem, dh, gv2 = call(
        functools.partial(cross_finish, many), "cross_finish", [SM] + far_w + [VM] * 8,
        [half_g, half_g, (memory.shape, F32), full, vec_g],
        [block_w, pair_g, sems],
        [HB, HB, VM, VM, VM],
    )(lens, *weights, dh2, dqt, dkt, dvt, o_cross, h, memory, vectors)
    if direct:
        cross_got = swap(cross_far, "fsdp", 1)
    chunks = 2
    span = width // chunks
    chunk_g = ((hidden // 2, span), BF)
    scratch = [((HEADS // chunks, AUG, rows), BF)] + [((span, rows), BF)] * 3 + [block_w, ((2, hidden // 2, span), BF), sems]
    if direct:
        up_late = add_low(up_sum, up_got)
        down_late = add_low(down_sum, down_got)
        cross_sum = add_low(cross_near, cross_got)
        dh, up_late, down_late, cross_sum = lax.optimization_barrier((dh, up_late, down_late, cross_sum))
        up_last = hop(up_late, (1, 2))
        cross_hop = hop(cross_sum, (0, 1), (3, 2))

    def heads_of(chunk):
        return [pl.BlockSpec((HEADS // chunks, AUG, rows), lambda i: (chunk, 0, 0))] * 3

    near_a, far_a, total = call(
        functools.partial(self_backward, 0, chunks, many), "self_backward_a", [SM] + far_w + [VM] + heads_of(0) + [VM] * 3,
        [chunk_g, chunk_g, full], scratch, [HB, HB, VM], (1,),
    )(lens, *weights, dh, qs, ks, vs, o_self, x, vectors)
    if direct:
        got_a = swap(far_a, "fsdp", 1)
    near_b, far_b, g_in, gv1 = call(
        functools.partial(self_backward, 1, chunks, many), "self_backward_b", [SM] + far_w + [VM] + heads_of(1) + [VM] * 4,
        [chunk_g, chunk_g, full, vec_g], scratch, [HB, HB, VM, VM], (1,),
    )(lens, *weights, dh, qs, ks, vs, o_self, x, vectors, total)

    gv = gv1 + gv2 + gv3
    if direct:
        far_b, gv, up_last, cross_hop, got_a = lax.optimization_barrier((far_b, gv, up_last, cross_hop, got_a))
        got_b = swap(far_b, "fsdp", 1)
        sum_a = add_low(near_a, got_a)
        hop_a = hop(sum_a, (1, 0), (3, 2))
        cross_last = hop(add_low(cross_sum, cross_hop), (2, 1))
        down_last = hop(down_late, (1, 3))
        gv = gv + swap(gv, "fsdp", 1)
        sum_b = add_low(near_b, got_b)
        sum_b, gv = lax.optimization_barrier((sum_b, gv))
        hop_b = hop(sum_b, (1, 0), (3, 2))
        late_a, hop_a = lax.optimization_barrier((add_low(sum_a, hop_a), hop_a))
        last_a = hop(late_a, (2, 0))
        late_b, hop_b = lax.optimization_barrier((add_low(sum_b, hop_b), hop_b))
        last_b = hop(late_b, (2, 0))
        last_a, last_b, gv, cross_last, down_last = lax.optimization_barrier((last_a, last_b, gv, cross_last, down_last))
        gv = gv + swap(gv, "fsdp", 2)
        gv = gv + swap(gv, "fsdp", 4)
        grad_v = lax.dynamic_slice(gv, (0, me * columns), (count, columns))
        cross = (cross_sum, cross_hop, cross_last)
        feeds = [(up_sum, up_got, up_last), (down_sum, down_got, down_last)]
        parts = [[first, cross, *feeds] for first in ((sum_a, hop_a, last_a), (sum_b, hop_b, last_b))]
        block = chip
    else:
        whole = [jnp.concatenate([near_a, near_b], axis=1), jnp.concatenate([far_a, far_b], axis=1), cross_near, cross_far]
        whole += [feed_near[0], feed_far[0], feed_near[1], feed_far[1]]
        rest = lax.psum_scatter(jnp.concatenate(whole), "fsdp", scatter_dimension=0, tiled=True)
        parts = [[[rest, jnp.zeros_like(rest), jnp.zeros_like(rest)]]] * chunks
        block = 0
        grad_v = lax.dynamic_slice(total_over(gv, "fsdp"), (0, me * columns), (count, columns))
    flags = jnp.stack([block, own_up]).astype(jnp.int32)
    inner_new = param_results = None
    deltas = []
    for chunk in range(chunks):
        lanes = pl.BlockSpec((share, span), lambda i, c=chunk: (0, c))
        taken = [item for three in parts[chunk] for item in three]
        part = pl.BlockSpec((share // 2, span), lambda i: (0, 0))
        state = pl.BlockSpec((1, 2, share, span), lambda i, c=chunk: (0, 0, 0, c))
        inner_new, upper, lower = call(
            functools.partial(adam, chunk, len(parts[chunk])), "adam", [SM] + [FAR] * len(taken) + [lanes, state] + [HB] * min(chunk, 1),
            [(inner_state.shape, F32)] + [((share // 2, span), BF)] * 2,
            [((share, span), F32), ((span // 128, share, 128), F32), ((3, share, span), BF), pltpu.SemaphoreType.DMA((3,))],
            [state, part, part], (1,), {len(taken) + 3: 0} if chunk else None,
        )(flags, *taken, params, inner_state, *([inner_new] if chunk else []))
        deltas.append((upper, lower))
    for chunk, (upper, lower) in enumerate(deltas):
        if replicas == 4:
            upper = add_low(upper, swap(upper, "rep", 1))
            lower = add_low(lower, swap(lower, "rep", 2))
            others = [swap(upper, "rep", 2), swap(lower, "rep", 1)]
        else:
            upper, lower = lax.psum(upper, "rep"), lax.psum(lower, "rep")
            others = [jnp.zeros_like(upper), jnp.zeros_like(lower)]
        lanes = pl.BlockSpec((share, span), lambda i, c=chunk: (0, c))
        part = pl.BlockSpec((share // 2, span), lambda i: (0, 0))
        (param_results,) = call(
            functools.partial(outer, replicas), "outer", [part] * 4 + [lanes, lanes] + [HB] * min(chunk, 1),
            [((3, share, width), F32)], (),
            [pl.BlockSpec((3, share, span), lambda i, c=chunk: (0, 0, c))], (1,), {6: 0} if chunk else None,
        )(upper, lower, *others, params, outer_mom, *([param_results] if chunk else []))
    moment_v, second_v, delta_v = inner_update(vecs, grad_v, inner_vecs[0, 0], inner_vecs[0, 1], 0.0)
    mean_v = total_over(delta_v.astype(BF), "rep").astype(F32) / replicas
    momentum_v = outer_push * outer_vecs + mean_v
    new_v = vecs - rate_outer * (mean_v + outer_push * momentum_v)
    return (
        y.reshape(PASSES, 1, length, width),
        g_in.reshape(PASSES, 1, length, width),
        g_mem[None],
        param_results,
        jnp.stack([new_v, mean_v, momentum_v]),
        inner_new,
        jnp.stack([moment_v, second_v])[None],
    )


def solution(mesh):
    both = ("rep", "fsdp")
    return jax.shard_map(
        per_device,
        mesh=mesh,
        in_specs=(
            P(),
            P(both, None),
            P(both, None),
            P(both),
            P(both),
            P(both, None, None),
            P(None, both, None, None),
            P("fsdp", None),
            P(None, "fsdp"),
            P("rep", None, "fsdp", None),
            P("rep", None, None, "fsdp"),
            P("fsdp", None),
            P(None, "fsdp"),
        ),
        out_specs=(
            P(None, both, None, None),
            P(None, both, None, None),
            P(both, None, None),
            P(None, "fsdp", None),
            P(None, None, "fsdp"),
            P("rep", None, "fsdp", None),
            P("rep", None, None, "fsdp"),
        ),
        check_vma=False,
    )
```

```python
import functools
import math

import jax
import jax.numpy as jnp
from jax import lax
from jax.experimental import pallas as pl
from jax.experimental.pallas import tpu as pltpu
from jax.sharding import PartitionSpec as P

HEADS = 8
STEP = 8
PASSES = 2
AUG = 80
norm_epsilon = 1e-05
beta_first = 0.9
beta_second = 0.999
adam_epsilon = 1e-08
rate_inner = 0.1
rate_outer = 0.7
outer_push = 0.9
decay_rate = 0.01

BF = jnp.bfloat16
F32 = jnp.float32
NN = (((1,), (0,)), ((), ()))
NT = (((1,), (1,)), ((), ()))
TN = (((0,), (0,)), ((), ()))
TT = (((0,), (1,)), ((), ()))


def dot(left, right, dims):
    return lax.dot_general(left, right, dims, preferred_element_type=F32)


def normalise(values):
    centre = values - jnp.mean(values, axis=-1, keepdims=True)
    spread = jnp.mean(centre * centre, axis=-1, keepdims=True)
    inverse = lax.rsqrt(spread + norm_epsilon)
    return centre * inverse, inverse


def norm_back(grad_out, gain_row, normal, inverse):
    grad_normal = grad_out * gain_row
    mean_grad = jnp.mean(grad_normal, axis=-1, keepdims=True)
    mean_proj = jnp.mean(grad_normal * normal, axis=-1, keepdims=True)
    grad_in = inverse * (grad_normal - mean_grad - normal * mean_proj)
    return grad_in, jnp.sum(grad_out * normal, axis=0, keepdims=True), jnp.sum(grad_out, axis=0, keepdims=True)


def thirds(row):
    high = row.astype(BF)
    rest = row - high.astype(F32)
    middle = rest.astype(BF)
    low = (rest - middle.astype(F32)).astype(BF)
    return high.astype(F32), middle.astype(F32), low.astype(F32)


def tail_rows(width, rows):
    place = lax.broadcasted_iota(jnp.int32, (AUG - 64, width), 0)
    tail = jnp.zeros((AUG - 64, width), F32)
    for number, row in enumerate(rows):
        tail = jnp.where(place == number, row, tail)
    return tail.astype(BF)


def put_heads(target, matrix_t, scale, tail):
    low = matrix_t.astype(BF)
    if scale != 1.0:
        low = low * BF(scale)
    size = low.shape[0] // HEADS
    for head in range(HEADS):
        target[head, :size, :] = low[head * size : (head + 1) * size]
        target[head, size:, :] = tail


def key_tail(width, count, period):
    spot = lax.broadcasted_iota(jnp.int32, (1, width), 1) % period
    bias = jnp.where(spot < count, 0.0, -1e30)
    return tail_rows(width, [bias, 1.0, 1.0, 1.0])


def attend_forward(units, where_of, block, q_ref, k_ref, v_ref, o_ref, s_a, s_b, m_a, m_b):
    keys = s_a.shape[0]

    def scores(step, store, peak):
        head, first, key_first = where_of(jnp.minimum(step, units - 1))
        value = dot(k_ref[head, :, pl.ds(key_first, keys)], q_ref[head, :, pl.ds(first, block)], TN)
        store[...] = value
        peak[...] = jnp.broadcast_to(jnp.max(value, axis=0, keepdims=True), peak.shape)

    def finish(step, store, peak):
        head, first, key_first = where_of(step)
        top = peak[0:1, :]
        weight = jnp.exp(store[...] - top).astype(BF)
        mixed = dot(v_ref[head, :, pl.ds(key_first, keys)], weight, NN)
        total = mixed[64:65, :]
        o_ref[pl.ds(pl.multiple_of(head * 64, 64), 64), pl.ds(first, block)] = (mixed[:64] * (1.0 / total)).astype(BF)
        high, middle, low = thirds(top + jnp.log(total))
        q_ref[head, 64:, pl.ds(first, block)] = tail_rows(block, [1.0, -high, -middle, -low])

    scores(0, s_a, m_a)

    def body(pair, carry):
        step = 2 * pair
        scores(step + 1, s_b, m_b)
        finish(step, s_a, m_a)
        scores(step + 2, s_a, m_a)
        finish(step + 1, s_b, m_b)
        return carry

    lax.fori_loop(0, units // 2 - 1, body, 0)
    step = units - 2
    scores(step + 1, s_b, m_b)
    finish(step, s_a, m_a)
    finish(step + 1, s_b, m_b)


def attend_backward(head, first, block, key_first, keys, q_ref, k_ref, v_ref, d_ref):
    here = pl.ds(first, block)
    there = pl.ds(key_first, keys)
    grad = d_ref[head, :, here]
    query = q_ref[head, :, here]
    key_t = k_ref[head, :, there]
    weight = jnp.exp(dot(query, key_t, TN))
    grad_scores = (weight * dot(grad, v_ref[head, :, there], TN)).astype(BF)
    grad_value = dot(grad[:64], weight.astype(BF), NN)
    grad_key = dot(query[:64], grad_scores, NN)
    grad_query = dot(key_t[:64], grad_scores, NT) * 0.125
    return grad_query.astype(BF), grad_key, grad_value


def put_grads(d_ref, grad_t, o_ref, skip, heads):
    low = grad_t.astype(BF)
    for head in range(heads):
        part = low[head * 64 : (head + 1) * 64]
        both = part.astype(F32) * o_ref[(skip + head) * 64 : (skip + head + 1) * 64, :].astype(F32)
        high, middle, rest = thirds(jnp.sum(both, axis=0, keepdims=True))
        d_ref[head, :64, :] = part
        d_ref[head, 64:, :] = tail_rows(low.shape[1], [-high, -middle, -rest])


def assemble(lens, weights, block, put, target, sem):
    if len(weights) == 1:
        rows = target.shape[0]
        copy = pltpu.make_async_copy(weights[0].at[pl.ds(block * rows, rows)], target, sem)
        copy.start()
        copy.wait()
        return
    core, rank = lens[2], lens[4]
    for side in range(2):
        for distance in range(4):
            source = weights[4 * side + distance]
            value = source[block % 2] if len(source.shape) == 3 else source[...]
            put(core if side == 0 else 1 - core, rank ^ distance, value)


def rows_of(target):
    quarter = target.shape[0] // 8

    def put(owner, number, value):
        target[pl.ds(pl.multiple_of((4 * owner + number) * quarter, quarter), quarter), :] = value

    return put


def deliver(core, source, near, far, sems):
    first = pltpu.make_async_copy(source.at[core], near, sems.at[0])
    second = pltpu.make_async_copy(source.at[1 - core], far, sems.at[1])
    first.start()
    second.start()
    return first, second


def wait(copies):
    for copy in copies:
        copy.wait()


def self_forward(many, lens, *refs):
    weights, refs = refs[:many], refs[many:]
    x_ref, vec_ref, q_ref, k_ref, v_ref, o_ref, h_ref, w_ref, s_a, s_b, m_a, m_b, sems = refs
    width = x_ref.shape[1]
    rows = x_ref.shape[0]
    length = rows // PASSES
    assemble(lens, weights, 0, rows_of(w_ref), w_ref, sems.at[0])
    x = x_ref[...].astype(F32)
    normal, _ = normalise(x)
    low = (normal * vec_ref[0:1, :] + vec_ref[3:4, :]).astype(BF)
    put_heads(q_ref, dot(w_ref[0:width, :], low, TT), 0.125, tail_rows(rows, [1.0]))
    put_heads(k_ref, dot(w_ref[width : 2 * width, :], low, TT), 1.0, key_tail(rows, lens[0], length))
    put_heads(v_ref, dot(w_ref[2 * width : 3 * width, :], low, TT), 1.0, tail_rows(rows, [1.0, 1.0, 1.0]))

    def where_of(step):
        place = pl.multiple_of((step % PASSES) * length, length)
        return step // PASSES, place, place

    attend_forward(HEADS * PASSES, where_of, length, q_ref, k_ref, v_ref, o_ref, s_a, s_b, m_a, m_b)
    h_ref[...] = x_ref[...].astype(F32) + dot(o_ref[...], w_ref[3 * width : 4 * width, :], TN)


def cross_forward(many, lens, *refs):
    weights, refs = refs[:many], refs[many:]
    h_ref, mem_ref, vec_ref, q_ref, k_ref, v_ref, o_ref, out_ref, w_ref, s_a, s_b, m_a, m_b, sems = refs
    width = h_ref.shape[1]
    rows = h_ref.shape[0]
    slots = mem_ref.shape[0]
    block = s_a.shape[1]
    assemble(lens, weights, 1, rows_of(w_ref), w_ref, sems.at[0])
    normal, _ = normalise(h_ref[...])
    low = (normal * vec_ref[1:2, :] + vec_ref[4:5, :]).astype(BF)
    memory = mem_ref[...]
    put_heads(q_ref, dot(w_ref[0:width, :], low, TT), 0.125, tail_rows(rows, [1.0]))
    put_heads(k_ref, dot(w_ref[width : 2 * width, :], memory, TT), 1.0, key_tail(slots, lens[1], slots))
    put_heads(v_ref, dot(w_ref[2 * width : 3 * width, :], memory, TT), 1.0, tail_rows(slots, [1.0, 1.0, 1.0]))
    pieces = rows // block

    def where_of(step):
        return step // pieces, pl.multiple_of((step % pieces) * block, block), 0

    attend_forward(HEADS * pieces, where_of, block, q_ref, k_ref, v_ref, o_ref, s_a, s_b, m_a, m_b)
    out_ref[...] = h_ref[...] + dot(o_ref[...], w_ref[3 * width : 4 * width, :], TN)


def feed(shards, many, lens, *refs):
    weights, refs = refs[:many], refs[many:]
    h_ref, vec_ref, cot_ref, y_ref, dh_ref, near, far, gv_ref, up_s, e_s, n_s, y_s, de_s, down_ref, g_ref, sems = refs
    width = h_ref.shape[1]
    rows = h_ref.shape[0]
    hidden = down_ref.shape[0]
    half = hidden // 2
    parts = hidden // width
    piece = hidden // shards // parts
    core = lens[2]

    def put_up(owner, number, value):
        size = value.shape[0]
        up_s[number, pl.ds(pl.multiple_of(owner * size, size), size), :] = value

    assemble(lens, weights, 2, put_up, down_ref, sems.at[0])
    if many == 1:
        for shard in range(shards):
            for part in range(parts):
                begin = (shard * parts + part) * piece
                up_s[part, shard * piece : (shard + 1) * piece, :] = down_ref[begin : begin + piece, :]
    assemble(lens, weights, 3, rows_of(down_ref), down_ref, sems.at[1])
    normal, inverse = normalise(h_ref[...])
    n_s[...] = normal
    e_s[...] = (normal * vec_ref[2:3, :] + vec_ref[5:6, :]).astype(BF)
    spot = lax.broadcasted_iota(jnp.int32, (rows, 1), 0) % (rows // PASSES)
    cot = jnp.where(spot < lens[0], cot_ref[...].astype(F32), 0.0)
    df = cot.astype(BF)
    y_s[...] = h_ref[...] + vec_ref[6:7, :]
    de_s[...] = jnp.zeros_like(de_s)
    gv_ref[...] = jnp.zeros_like(gv_ref)

    def body(part, carry):
        place = pl.multiple_of(part * width, width)
        down = down_ref[pl.ds(place, width), :]
        up = up_s[part]
        pre = dot(e_s[...], up, NN) + vec_ref[pl.ds(7 + part, 1), :]
        active = jnp.maximum(pre, 0.0).astype(BF)
        y_s[...] += dot(active, down, NN)
        g_ref[place // half, 1, pl.ds(pl.multiple_of(place % half, width), width), :] = dot(active, df, TN).astype(BF)
        du = jnp.where(pre > 0, dot(df, down, NT), 0.0).astype(BF)
        gv_ref[pl.ds(7 + part, 1), :] = jnp.sum(du.astype(F32), axis=0, keepdims=True)
        gup = dot(e_s[...], du, TN).astype(BF)
        for shard in range(shards):
            begin = (shard * parts + part) * piece
            g_ref[begin // half, 0, pl.ds(pl.multiple_of(begin % half, piece), piece), :] = gup[shard * piece : (shard + 1) * piece, :]
        de_s[...] += dot(du, up, NT)
        return carry

    lax.fori_loop(0, parts, body, 0)
    copies = deliver(core, g_ref, near, far, sems)
    y_ref[...] = y_s[...].astype(BF)
    gv_ref[6:7, :] = jnp.sum(cot, axis=0, keepdims=True)
    back, gain, shift = norm_back(de_s[...], vec_ref[2:3, :], n_s[...], inverse)
    gv_ref[2:3, :] = gain
    gv_ref[5:6, :] = shift
    dh_ref[...] = cot + back
    wait(copies)


def cross_start(w_ref, dh_ref, o_ref, d_ref):
    width = dh_ref.shape[1]
    low = dh_ref[...].astype(BF)
    put_grads(d_ref, dot(w_ref[3 * width :, :], low, NT), o_ref, 0, HEADS)


def cross_attend(q_ref, k_ref, v_ref, d_ref, dq_ref, dk_ref, dv_ref, sk, sv):
    rows = q_ref.shape[2]
    slots = k_ref.shape[2]
    block = rows // PASSES

    def body(head, carry):
        place = pl.ds(pl.multiple_of(head * 64, 64), 64)
        for piece in range(PASSES):
            dq, dk, dv = attend_backward(head, piece * block, block, 0, slots, q_ref, k_ref, v_ref, d_ref)
            dq_ref[place, piece * block : (piece + 1) * block] = dq
            if piece == 0:
                sk[...] = dk
                sv[...] = dv
            else:
                dk_ref[place, :] = (sk[...] + dk).astype(BF)
                dv_ref[place, :] = (sv[...] + dv).astype(BF)
        return carry

    lax.fori_loop(0, HEADS, body, 0)


def cross_finish(lens, w_ref, dh2_ref, dq_ref, dk_ref, dv_ref, o_ref, h_ref, mem_ref, vec_ref, near, far, dh_ref, gv_ref, g_ref, sems):
    width = h_ref.shape[1]
    core = lens[2]
    memory = mem_ref[...]
    normal, inverse = normalise(h_ref[...])
    low = (normal * vec_ref[1:2, :] + vec_ref[4:5, :]).astype(BF)
    dq = dq_ref[...].T
    g_ref[0, :width, :] = dot(low, dq, TN).astype(BF)
    g_ref[1, width:, :] = dot(o_ref[...], dh2_ref[...].astype(BF), NN).astype(BF)
    dk = dk_ref[...].T
    g_ref[0, width:, :] = dot(memory, dk, TN).astype(BF)
    dv = dv_ref[...].T
    g_ref[1, :width, :] = dot(memory, dv, TN).astype(BF)
    copies = deliver(core, g_ref, near, far, sems)
    back, gain, shift = norm_back(dot(dq, w_ref[0:width, :], NT), vec_ref[1:2, :], normal, inverse)
    gv_ref[...] = jnp.zeros_like(gv_ref)
    gv_ref[1:2, :] = gain
    gv_ref[4:5, :] = shift
    dh_ref[...] = dh2_ref[...] + back
    wait(copies)


def self_backward(chunk, chunks, lens, w_ref, dh_ref, q_ref, k_ref, v_ref, o_ref, x_ref, vec_ref, near, far, dq_ref, dk_ref, dv_ref, d_s, g_ref, sems):
    width = x_ref.shape[1]
    rows = x_ref.shape[0]
    length = rows // PASSES
    heads = HEADS // chunks
    span = width // chunks
    lanes = slice(chunk * span, (chunk + 1) * span)
    core = lens[2]
    dz = dh_ref[...].astype(BF)
    g_ref[1, width:, :] = dot(o_ref[...], dz[:, lanes], NN).astype(BF)
    put_grads(d_s, dot(w_ref[3 * width + chunk * span : 3 * width + (chunk + 1) * span, :], dz, NT), o_ref, chunk * heads, heads)

    def body(head, carry):
        place = pl.ds(pl.multiple_of(head * 64, 64), 64)
        for number in range(PASSES):
            begin = number * length
            dq, dk, dv = attend_backward(head, begin, length, begin, length, q_ref, k_ref, v_ref, d_s)
            dq_ref[place, begin : begin + length] = dq
            dk_ref[place, begin : begin + length] = dk.astype(BF)
            dv_ref[place, begin : begin + length] = dv.astype(BF)
        return carry

    lax.fori_loop(0, heads, body, 0)
    normal, _ = normalise(x_ref[...].astype(F32))
    low = (normal * vec_ref[0:1, :] + vec_ref[3:4, :]).astype(BF)
    for number, store in enumerate((dq_ref, dk_ref, dv_ref)):
        g_ref[number // 2, (number % 2) * width : (number % 2 + 1) * width, :] = dot(low, store[...].T, TN).astype(BF)
    wait(deliver(core, g_ref, near, far, sems))


def self_finish(w_ref, *refs):
    parts = refs[:-5]
    dh_ref, x_ref, vec_ref, out_ref, gv_ref = refs[-5:]
    width = x_ref.shape[1]
    normal, inverse = normalise(x_ref[...].astype(F32))
    total = None
    span = parts[0].shape[0]
    for place, part in enumerate(parts):
        chunk, number = place // 3, place % 3
        lanes = slice(chunk * span, (chunk + 1) * span)
        value = dot(part[...].T, w_ref[number * width : (number + 1) * width, lanes], NT)
        total = value if total is None else total + value
    back, gain, shift = norm_back(total, vec_ref[0:1, :], normal, inverse)
    gv_ref[...] = jnp.zeros_like(gv_ref)
    gv_ref[0:1, :] = gain
    gv_ref[3:4, :] = shift
    out_ref[...] = dh_ref[...] + back


def memory_finish(w_ref, dk_ref, dv_ref, out_ref):
    width = dk_ref.shape[0]
    dk, dv = dk_ref[...].T, dv_ref[...].T
    out_ref[...] = dot(dk, w_ref[width : 2 * width, :], NT) + dot(dv, w_ref[2 * width : 3 * width, :], NT)


def prepare(flags, w_ref, low_ref, piece_ref, order_s):
    share = w_ref.shape[0]
    part = share // 4

    @pl.when(flags[0] == 0)
    def _():
        low_ref[...] = w_ref[...].astype(BF)

    @pl.when(flags[0] == 1)
    def _():
        for lane in range(order_s.shape[0]):
            lanes = slice(lane * 128, (lane + 1) * 128)
            order_s[lane] = w_ref[:, lanes]
            for number in range(4):
                low_ref[number * part : (number + 1) * part, lanes] = order_s[lane, pl.ds(number, part, stride=4), :].astype(BF)

    size = piece_ref.shape[0]
    piece_ref[...] = low_ref[pl.ds(pl.multiple_of(flags[1] * size, size), size), :]


def adam(chunk, blocks, flags, *refs):
    parts = refs[: 3 * blocks]
    w_ref, state_ref = refs[3 * blocks : 3 * blocks + 2]
    new_ref, upper_ref, lower_ref, g_s, order_s, three_s, sems = refs[-7:]
    share, span = w_ref.shape
    part = share // 4
    lanes = pl.ds(chunk * span, span)
    for block in range(blocks):

        @pl.when(flags[0] == block)
        def _(block=block):
            for number in range(3):
                source = parts[3 * block + number]
                source = source if source.shape[1] == span else source.at[:, lanes]
                pltpu.make_async_copy(source, three_s.at[number], sems.at[number]).start()

    for number in range(3):
        pltpu.make_async_copy(three_s.at[number], three_s.at[number], sems.at[number]).wait()
    g_s[...] = three_s[0].astype(F32) + three_s[1].astype(F32) + three_s[2].astype(F32)

    @pl.when(flags[1] == 1)
    def _():
        for lane in range(order_s.shape[0]):
            lanes = slice(lane * 128, (lane + 1) * 128)
            for number in range(4):
                order_s[lane, pl.ds(number, part, stride=4), :] = g_s[number * part : (number + 1) * part, lanes]
            g_s[:, lanes] = order_s[lane]

    moment, second, delta = inner_update(w_ref[...], g_s[...], state_ref[0, 0], state_ref[0, 1], decay_rate)
    new_ref[0, 0] = moment
    new_ref[0, 1] = second
    low = delta.astype(BF)
    upper_ref[...] = low[: share // 2]
    lower_ref[...] = low[share // 2 :]


def outer(replicas, one_a, one_b, two_a, two_b, w_ref, mom_ref, *refs):
    out_ref = refs[-1]
    share = w_ref.shape[0] // 2
    for half, (one, two) in enumerate(((one_a, two_a), (one_b, two_b))):
        rows = slice(half * share, (half + 1) * share)
        mean = (one[...].astype(F32) + two[...].astype(F32)) / replicas
        momentum = outer_push * mom_ref[rows, :] + mean
        out_ref[0, rows, :] = w_ref[rows, :] - rate_outer * (mean + outer_push * momentum)
        out_ref[1, rows, :] = mean
        out_ref[2, rows, :] = momentum


VM = pl.BlockSpec(memory_space=pltpu.VMEM)
SM = pl.BlockSpec(memory_space=pltpu.SMEM)
HB = pl.BlockSpec(memory_space=pl.ANY)
FAR = pl.BlockSpec(memory_space=pltpu.HBM)


def call(body, name, ins, outs, scratch=(), places=None, grid=(), aliases=None, room=12):
    shapes = tuple(jax.ShapeDtypeStruct(shape, kind) for shape, kind in outs)
    return pl.pallas_call(
        body,
        name=name,
        grid=grid,
        cost_estimate=pl.CostEstimate(flops=0, transcendentals=0, bytes_accessed=0),
        input_output_aliases=aliases or {},
        out_shape=shapes,
        in_specs=ins,
        out_specs=tuple(places or [VM] * len(outs)),
        scratch_shapes=[item if not isinstance(item, tuple) else pltpu.VMEM(*item) for item in scratch],
        compiler_params=pltpu.CompilerParams(vmem_limit_bytes=room << 20),
    )


def inner_update(weight, gradient, moment_one, second, shrink):
    moment_new = beta_first * moment_one + (1.0 - beta_first) * gradient
    second_new = beta_second * second + (1.0 - beta_second) * gradient * gradient
    moment_hat = moment_new / (1.0 - beta_first**STEP)
    second_hat = second_new / (1.0 - beta_second**STEP)
    local_weight = weight - rate_inner * (
        moment_hat / (jnp.sqrt(second_hat) + adam_epsilon) + shrink * weight
    )
    return (moment_new, second_new, weight - local_weight)


def swap(values, axis, bit):
    count = lax.axis_size(axis)
    return lax.ppermute(values, axis, [(i, i ^ bit) for i in range(count)])


def total_over(values, axis):
    count = lax.axis_size(axis)
    if count & (count - 1):
        return lax.psum(values, axis)
    bit = 1
    while bit < count:
        values = values + swap(values, axis, bit)
        bit *= 2
    return values


def hop(values, *moves):
    return lax.ppermute(values, "fsdp", [(2 * one + core, 2 * two + core) for one, two in moves for core in range(2)])


def add_low(one, two):
    return (one.astype(F32) + two.astype(F32)).astype(BF)


def cycle(values, distance):
    count = lax.axis_size("fsdp")
    return lax.ppermute(values, "fsdp", [((to + 2 * distance) % count, to) for to in range(count)])


def around(piece):
    return [piece] + [swap(piece, "rep", distance) for distance in (1, 2, 3)]


def with_other(quarters):
    return quarters + [swap(quarter, "fsdp", 1) for quarter in quarters]


def gather_pieces(piece, vectors, x):
    chip = lax.axis_index("fsdp") // 2
    vectors = vectors + swap(vectors, "fsdp", 1)
    slots = [piece] + [cycle(piece, distance) for distance in (1, 2, 3)]
    vectors = vectors + swap(vectors, "fsdp", 2)
    slots, vectors, x = lax.optimization_barrier((slots, vectors, x))
    pieces = [lax.select_n((block - chip) % 4, *slots) for block in range(4)]
    return pieces, vectors + swap(vectors, "fsdp", 4), x


def per_device(embed, first_tokens, sample_tokens, seq_len, mem_len, memory, cotangent, params, vecs, inner_state, inner_vecs, outer_mom, outer_vecs):
    groups = lax.axis_size("fsdp")
    replicas = lax.axis_size("rep")
    direct = groups == 8 and replicas == 4
    share, width = params.shape
    hidden = 4 * width
    me = lax.axis_index("fsdp")
    chip = me // 2
    own_up = (me >= 2 * hidden // share) & (me < 3 * hidden // share)
    rank = lax.axis_index("rep")
    count, columns = vecs.shape
    vectors = lax.dynamic_update_slice(jnp.zeros((16, width), BF), vecs.astype(BF), (0, me * columns))
    low, piece = call(
        prepare, "prepare", [SM, VM], [((share, width), BF), ((share // 4, width), BF)],
        [((width // 128, share, 128), F32)],
    )(jnp.stack([own_up, rank if direct else 0]).astype(jnp.int32), params)
    x = embed[jnp.concatenate([first_tokens[0], sample_tokens[0]])]
    if direct:
        pieces, vectors, x = gather_pieces(piece, vectors, x)
        core = me % 2
        w_self = with_other(around(pieces[0]))
        w_cross = around(pieces[1])
    else:
        w_self = w_cross = w_feed = [lax.all_gather(low, "fsdp", axis=0, tiled=True)]
        vectors = total_over(vectors, "fsdp")
        core = 0
    vectors = vectors.astype(F32)
    lens = jnp.stack([seq_len[0], mem_len[0], core, chip, rank]).astype(jnp.int32)
    many = len(w_self)
    far_w = [FAR if many == 1 else VM] * many
    length = first_tokens.shape[1]
    rows = PASSES * length
    cot = cotangent.reshape(rows, width)
    memory = memory[0]
    slots = memory.shape[0]

    heads_n = ((HEADS, AUG, rows), BF)
    heads_m = ((HEADS, AUG, slots), BF)
    flat_n = ((width, rows), BF)
    flat_m = ((width, slots), BF)
    full = ((rows, width), F32)
    half_g = ((hidden // 2, width), BF)
    block_w = ((hidden, width), BF)
    vec_g = ((16, width), F32)
    peak = ((8, length), F32)
    sems = pltpu.SemaphoreType.DMA((2,))
    qs, ks, vs, o_self, h, weights_self = call(
        functools.partial(self_forward, many), "self_forward", [SM] + far_w + [VM] * 2,
        [heads_n, heads_n, heads_n, flat_n, full, block_w],
        [((length, length), F32)] * 2 + [peak] * 2 + [sems],
    )(lens, *w_self, x, vectors)
    if direct:
        h, w_cross = lax.optimization_barrier((h, w_cross))
        w_cross = with_other(w_cross)
        w_feed = around(jnp.stack(pieces[2:]))
    qc, kc, vc, o_cross, h2, weights_cross = call(
        functools.partial(cross_forward, many), "cross_forward", [SM] + far_w + [VM] * 3,
        [heads_n, heads_m, heads_m, flat_n, full, block_w],
        [((slots, length), F32)] * 2 + [peak] * 2 + [sems],
    )(lens, *w_cross, h, memory, vectors)
    if direct:
        h2, w_feed = lax.optimization_barrier((h2, w_feed))
        w_feed = with_other(w_feed)
    pair_g = ((2, hidden // 2, width), BF)
    y, dh2, feed_near, feed_far, gv3 = call(
        functools.partial(feed, hidden // min(share, hidden), many), "feed", [SM] + far_w + [VM] * 3,
        [((rows, width), BF), full, pair_g, pair_g, vec_g],
        [((4, width, width), BF), ((rows, width), BF), full, full, full, block_w, ((2, 2, hidden // 2, width), BF), sems],
        [VM, VM, HB, HB, VM], room=26,
    )(lens, *w_feed, h2, vectors, cot)
    if direct:
        feed_got = swap(feed_far, "fsdp", 1)
    (do_cross,) = call(
        cross_start, "cross_start", [VM] * 3, [heads_n],
    )(weights_cross, dh2, o_cross)
    if direct:
        up_sum, down_sum = add_low(feed_near[0], feed_got[0]), add_low(feed_near[1], feed_got[1])
        do_cross, up_sum, down_sum = lax.optimization_barrier((do_cross, up_sum, down_sum))
        up_got = hop(up_sum, (0, 1), (3, 2))
        down_got = hop(down_sum, (0, 1), (2, 3))
    dqt, dkt, dvt = call(
        cross_attend, "cross_attend", [VM] * 4, [flat_n, flat_m, flat_m], [((64, slots), F32)] * 2,
    )(qc, kc, vc, do_cross)
    cross_near, cross_far, dh, gv2 = call(
        cross_finish, "cross_finish", [SM] + [VM] * 9,
        [half_g, half_g, full, vec_g],
        [pair_g, sems],
        [HB, HB, VM, VM],
    )(lens, weights_cross, dh2, dqt, dkt, dvt, o_cross, h, memory, vectors)
    if direct:
        cross_got = swap(cross_far, "fsdp", 1)
    (g_mem,) = call(
        memory_finish, "memory_finish", [VM] * 3, [(memory.shape, F32)],
    )(weights_cross, dkt, dvt)
    chunks = 2
    span = width // chunks
    chunk_g = ((hidden // 2, span), BF)
    if direct:
        up_late = add_low(up_sum, up_got)
        down_late = add_low(down_sum, down_got)
        cross_sum = add_low(cross_near, cross_got)
        dh, g_mem, up_late, down_late, cross_sum = lax.optimization_barrier((dh, g_mem, up_late, down_late, cross_sum))
        up_last = hop(up_late, (1, 2))
        cross_hop = hop(cross_sum, (0, 1), (3, 2))

    def chunk_of(chunk):
        heads = [pl.BlockSpec((HEADS // chunks, AUG, rows), lambda i: (chunk, 0, 0))] * 3
        return call(
            functools.partial(self_backward, chunk, chunks), "self_backward", [SM] + [VM] * 2 + heads + [VM] * 3,
            [chunk_g, chunk_g] + [((span, rows), BF)] * 3,
            [((HEADS // chunks, AUG, rows), BF), ((2, hidden // 2, span), BF), sems],
            [HB, HB, VM, VM, VM], (1,),
        )(lens, weights_self, dh, qs, ks, vs, o_self, x, vectors)

    near_a, far_a, *grads_a = chunk_of(0)
    if direct:
        got_a = swap(far_a, "fsdp", 1)
        dh, grads_a = lax.optimization_barrier((dh, grads_a))
    near_b, far_b, *grads_b = chunk_of(1)
    if direct:
        far_b, up_last, cross_hop, got_a, dh = lax.optimization_barrier((far_b, up_last, cross_hop, got_a, dh))
        got_b = swap(far_b, "fsdp", 1)
        sum_a = add_low(near_a, got_a)
        hop_a = hop(sum_a, (1, 0), (3, 2))
        cross_late = add_low(cross_sum, cross_hop)
        cross_last = hop(cross_late, (2, 1))
        down_last = hop(down_late, (1, 3))
        sum_b = add_low(near_b, got_b)
        hop_b = hop(sum_b, (1, 0), (3, 2))
        late_a, hop_a, dh = lax.optimization_barrier((add_low(sum_a, hop_a), hop_a, dh))
        last_a = hop(late_a, (2, 0))
    g_in, gv1 = call(
        self_finish, "self_finish", [VM] * 10, [full, vec_g],
    )(weights_self, *grads_a, *grads_b, dh, x, vectors)
    gv = gv1 + gv2 + gv3
    if direct:
        late_b, hop_b, gv, g_in = lax.optimization_barrier((add_low(sum_b, hop_b), hop_b, gv, g_in))
        last_b = hop(late_b, (2, 0))
        gv = gv + swap(gv, "fsdp", 1)
        last_a, gv = lax.optimization_barrier((last_a, gv))
        gv = gv + swap(gv, "fsdp", 2)
        last_b, gv = lax.optimization_barrier((last_b, gv))
        gv = gv + swap(gv, "fsdp", 4)
        grad_v = lax.dynamic_slice(gv, (0, me * columns), (count, columns))
        cross = (cross_sum, cross_hop, cross_last)
        feeds = [(up_sum, up_got, up_last), (down_sum, down_got, down_last)]
        parts = [[first, cross, *feeds] for first in ((sum_a, hop_a, last_a), (sum_b, hop_b, last_b))]
        block = chip
    else:
        whole = [jnp.concatenate([near_a, near_b], axis=1), jnp.concatenate([far_a, far_b], axis=1), cross_near, cross_far]
        whole += [feed_near[0], feed_far[0], feed_near[1], feed_far[1]]
        rest = lax.psum_scatter(jnp.concatenate(whole), "fsdp", scatter_dimension=0, tiled=True)
        parts = [[[rest, jnp.zeros_like(rest), jnp.zeros_like(rest)]]] * chunks
        block = 0
        grad_v = lax.dynamic_slice(total_over(gv, "fsdp"), (0, me * columns), (count, columns))
    flags = jnp.stack([block, own_up]).astype(jnp.int32)
    inner_new = param_results = None
    deltas = []
    for chunk in range(chunks):
        lanes = pl.BlockSpec((share, span), lambda i, c=chunk: (0, c))
        taken = [item for three in parts[chunk] for item in three]
        part = pl.BlockSpec((share // 2, span), lambda i: (0, 0))
        state = pl.BlockSpec((1, 2, share, span), lambda i, c=chunk: (0, 0, 0, c))
        inner_new, upper, lower = call(
            functools.partial(adam, chunk, len(parts[chunk])), "adam", [SM] + [FAR] * len(taken) + [lanes, state] + [HB] * min(chunk, 1),
            [(inner_state.shape, F32)] + [((share // 2, span), BF)] * 2,
            [((share, span), F32), ((span // 128, share, 128), F32), ((3, share, span), BF), pltpu.SemaphoreType.DMA((3,))],
            [state, part, part], (1,), {len(taken) + 3: 0} if chunk else None, 16,
        )(flags, *taken, params, inner_state, *([inner_new] if chunk else []))
        deltas.append((upper, lower))
    for chunk, (upper, lower) in enumerate(deltas):
        if replicas == 4:
            upper = add_low(upper, swap(upper, "rep", 1))
            lower = add_low(lower, swap(lower, "rep", 2))
            others = [swap(upper, "rep", 2), swap(lower, "rep", 1)]
        else:
            upper, lower = lax.psum(upper, "rep"), lax.psum(lower, "rep")
            others = [jnp.zeros_like(upper), jnp.zeros_like(lower)]
        lanes = pl.BlockSpec((share, span), lambda i, c=chunk: (0, c))
        part = pl.BlockSpec((share // 2, span), lambda i: (0, 0))
        (param_results,) = call(
            functools.partial(outer, replicas), "outer", [part] * 4 + [lanes, lanes] + [HB] * min(chunk, 1),
            [((3, share, width), F32)], (),
            [pl.BlockSpec((3, share, span), lambda i, c=chunk: (0, 0, c))], (1,), {6: 0} if chunk else None,
        )(upper, lower, *others, params, outer_mom, *([param_results] if chunk else []))
    moment_v, second_v, delta_v = inner_update(vecs, grad_v, inner_vecs[0, 0], inner_vecs[0, 1], 0.0)
    if replicas == 4:
        low_v = delta_v.astype(BF)
        mean_v = sum([swap(low_v, "rep", bit).astype(F32) for bit in (1, 2, 3)], low_v.astype(F32)) / replicas
    else:
        mean_v = lax.psum(delta_v.astype(BF), "rep").astype(F32) / replicas
    momentum_v = outer_push * outer_vecs + mean_v
    new_v = vecs - rate_outer * (mean_v + outer_push * momentum_v)
    return (
        y.reshape(PASSES, 1, length, width),
        g_in.reshape(PASSES, 1, length, width),
        g_mem[None],
        param_results,
        jnp.stack([new_v, mean_v, momentum_v]),
        inner_new,
        jnp.stack([moment_v, second_v])[None],
    )


def solution(mesh):
    both = ("rep", "fsdp")
    return jax.shard_map(
        per_device,
        mesh=mesh,
        in_specs=(
            P(),
            P(both, None),
            P(both, None),
            P(both),
            P(both),
            P(both, None, None),
            P(None, both, None, None),
            P("fsdp", None),
            P(None, "fsdp"),
            P("rep", None, "fsdp", None),
            P("rep", None, None, "fsdp"),
            P("fsdp", None),
            P(None, "fsdp"),
        ),
        out_specs=(
            P(None, both, None, None),
            P(None, both, None, None),
            P(both, None, None),
            P(None, "fsdp", None),
            P(None, None, "fsdp"),
            P("rep", None, "fsdp", None),
            P("rep", None, None, "fsdp"),
        ),
        check_vma=False,
    )
```

```python
import functools
import math

import jax
import jax.numpy as jnp
from jax import lax
from jax.experimental import pallas as pl
from jax.experimental.pallas import tpu as pltpu
from jax.sharding import PartitionSpec as P

HEADS = 8
STEP = 8
PASSES = 2
AUG = 80
norm_epsilon = 1e-05
beta_first = 0.9
beta_second = 0.999
adam_epsilon = 1e-08
rate_inner = 0.1
rate_outer = 0.7
outer_push = 0.9
decay_rate = 0.01

BF = jnp.bfloat16
F32 = jnp.float32
NN = (((1,), (0,)), ((), ()))
NT = (((1,), (1,)), ((), ()))
TN = (((0,), (0,)), ((), ()))
TT = (((0,), (1,)), ((), ()))


def dot(left, right, dims):
    return lax.dot_general(left, right, dims, preferred_element_type=F32)


def normalise(values):
    centre = values - jnp.mean(values, axis=-1, keepdims=True)
    spread = jnp.mean(centre * centre, axis=-1, keepdims=True)
    inverse = lax.rsqrt(spread + norm_epsilon)
    return centre * inverse, inverse


def norm_back(grad_out, gain_row, normal, inverse):
    grad_normal = grad_out * gain_row
    mean_grad = jnp.mean(grad_normal, axis=-1, keepdims=True)
    mean_proj = jnp.mean(grad_normal * normal, axis=-1, keepdims=True)
    grad_in = inverse * (grad_normal - mean_grad - normal * mean_proj)
    return grad_in, jnp.sum(grad_out * normal, axis=0, keepdims=True), jnp.sum(grad_out, axis=0, keepdims=True)


def thirds(row):
    high = row.astype(BF)
    rest = row - high.astype(F32)
    middle = rest.astype(BF)
    low = (rest - middle.astype(F32)).astype(BF)
    return high.astype(F32), middle.astype(F32), low.astype(F32)


def tail_rows(width, rows):
    place = lax.broadcasted_iota(jnp.int32, (AUG - 64, width), 0)
    tail = jnp.zeros((AUG - 64, width), F32)
    for number, row in enumerate(rows):
        tail = jnp.where(place == number, row, tail)
    return tail.astype(BF)


def put_heads(target, matrix_t, scale, tail):
    low = matrix_t.astype(BF)
    if scale != 1.0:
        low = low * BF(scale)
    size = low.shape[0] // HEADS
    for head in range(HEADS):
        target[head, :size, :] = low[head * size : (head + 1) * size]
        target[head, size:, :] = tail


def key_tail(width, count, period):
    spot = lax.broadcasted_iota(jnp.int32, (1, width), 1) % period
    bias = jnp.where(spot < count, 0.0, -1e30)
    return tail_rows(width, [bias, 1.0, 1.0, 1.0])


def attend_forward(units, where_of, block, q_ref, k_ref, v_ref, o_ref, s_a, s_b, m_a, m_b):
    keys = s_a.shape[0]

    def scores(step, store, peak):
        head, first, key_first = where_of(jnp.minimum(step, units - 1))
        value = dot(k_ref[head, :, pl.ds(key_first, keys)], q_ref[head, :, pl.ds(first, block)], TN)
        store[...] = value
        peak[...] = jnp.broadcast_to(jnp.max(value, axis=0, keepdims=True), peak.shape)

    def finish(step, store, peak):
        head, first, key_first = where_of(step)
        top = peak[0:1, :]
        weight = jnp.exp(store[...] - top).astype(BF)
        mixed = dot(v_ref[head, :, pl.ds(key_first, keys)], weight, NN)
        total = mixed[64:65, :]
        o_ref[pl.ds(pl.multiple_of(head * 64, 64), 64), pl.ds(first, block)] = (mixed[:64] * (1.0 / total)).astype(BF)
        high, middle, low = thirds(top + jnp.log(total))
        q_ref[head, 64:, pl.ds(first, block)] = tail_rows(block, [1.0, -high, -middle, -low])

    scores(0, s_a, m_a)

    def body(pair, carry):
        step = 2 * pair
        scores(step + 1, s_b, m_b)
        finish(step, s_a, m_a)
        scores(step + 2, s_a, m_a)
        finish(step + 1, s_b, m_b)
        return carry

    lax.fori_loop(0, units // 2 - 1, body, 0)
    step = units - 2
    scores(step + 1, s_b, m_b)
    finish(step, s_a, m_a)
    finish(step + 1, s_b, m_b)


def attend_backward(head, first, block, key_first, keys, q_ref, k_ref, v_ref, d_ref):
    here = pl.ds(first, block)
    there = pl.ds(key_first, keys)
    grad = d_ref[head, :, here]
    query = q_ref[head, :, here]
    key_t = k_ref[head, :, there]
    weight = jnp.exp(dot(query, key_t, TN))
    grad_scores = (weight * dot(grad, v_ref[head, :, there], TN)).astype(BF)
    grad_value = dot(grad[:64], weight.astype(BF), NN)
    grad_key = dot(query[:64], grad_scores, NN)
    grad_query = dot(key_t[:64], grad_scores, NT) * 0.125
    return grad_query.astype(BF), grad_key, grad_value


def put_grads(d_ref, grad_t, o_ref, skip, heads):
    low = grad_t.astype(BF)
    for head in range(heads):
        part = low[head * 64 : (head + 1) * 64]
        both = part.astype(F32) * o_ref[(skip + head) * 64 : (skip + head + 1) * 64, :].astype(F32)
        high, middle, rest = thirds(jnp.sum(both, axis=0, keepdims=True))
        d_ref[head, :64, :] = part
        d_ref[head, 64:, :] = tail_rows(low.shape[1], [-high, -middle, -rest])


def assemble(lens, weights, block, put, target, sem):
    if len(weights) == 1:
        rows = target.shape[0]
        copy = pltpu.make_async_copy(weights[0].at[pl.ds(block * rows, rows)], target, sem)
        copy.start()
        copy.wait()
        return
    core, rank = lens[2], lens[4]
    for side in range(2):
        for distance in range(4):
            source = weights[4 * side + distance]
            value = source[block % 2] if len(source.shape) == 3 else source[...]
            put(core if side == 0 else 1 - core, rank ^ distance, value)


def rows_of(target):
    quarter = target.shape[0] // 8

    def put(owner, number, value):
        target[pl.ds(pl.multiple_of((4 * owner + number) * quarter, quarter), quarter), :] = value

    return put


def deliver(core, source, near, far, sems):
    first = pltpu.make_async_copy(source.at[core], near, sems.at[0])
    second = pltpu.make_async_copy(source.at[1 - core], far, sems.at[1])
    first.start()
    second.start()
    return first, second


def wait(copies):
    for copy in copies:
        copy.wait()


def self_forward(many, lens, *refs):
    weights, refs = refs[:many], refs[many:]
    x_ref, vec_ref, q_ref, k_ref, v_ref, o_ref, h_ref, w_ref, s_a, s_b, m_a, m_b, sems = refs
    width = x_ref.shape[1]
    rows = x_ref.shape[0]
    length = rows // PASSES
    assemble(lens, weights, 0, rows_of(w_ref), w_ref, sems.at[0])
    x = x_ref[...].astype(F32)
    normal, _ = normalise(x)
    low = (normal * vec_ref[0:1, :] + vec_ref[3:4, :]).astype(BF)
    put_heads(q_ref, dot(w_ref[0:width, :], low, TT), 0.125, tail_rows(rows, [1.0]))
    put_heads(k_ref, dot(w_ref[width : 2 * width, :], low, TT), 1.0, key_tail(rows, lens[0], length))
    put_heads(v_ref, dot(w_ref[2 * width : 3 * width, :], low, TT), 1.0, tail_rows(rows, [1.0, 1.0, 1.0]))

    def where_of(step):
        place = pl.multiple_of((step % PASSES) * length, length)
        return step // PASSES, place, place

    attend_forward(HEADS * PASSES, where_of, length, q_ref, k_ref, v_ref, o_ref, s_a, s_b, m_a, m_b)
    h_ref[...] = x_ref[...].astype(F32) + dot(o_ref[...], w_ref[3 * width : 4 * width, :], TN)


def cross_forward(many, lens, *refs):
    weights, refs = refs[:many], refs[many:]
    h_ref, mem_ref, vec_ref, q_ref, k_ref, v_ref, o_ref, out_ref, w_ref, s_a, s_b, m_a, m_b, sems = refs
    width = h_ref.shape[1]
    rows = h_ref.shape[0]
    slots = mem_ref.shape[0]
    block = s_a.shape[1]
    assemble(lens, weights, 1, rows_of(w_ref), w_ref, sems.at[0])
    normal, _ = normalise(h_ref[...])
    low = (normal * vec_ref[1:2, :] + vec_ref[4:5, :]).astype(BF)
    memory = mem_ref[...]
    put_heads(q_ref, dot(w_ref[0:width, :], low, TT), 0.125, tail_rows(rows, [1.0]))
    put_heads(k_ref, dot(w_ref[width : 2 * width, :], memory, TT), 1.0, key_tail(slots, lens[1], slots))
    put_heads(v_ref, dot(w_ref[2 * width : 3 * width, :], memory, TT), 1.0, tail_rows(slots, [1.0, 1.0, 1.0]))
    pieces = rows // block

    def where_of(step):
        return step // pieces, pl.multiple_of((step % pieces) * block, block), 0

    attend_forward(HEADS * pieces, where_of, block, q_ref, k_ref, v_ref, o_ref, s_a, s_b, m_a, m_b)
    out_ref[...] = h_ref[...] + dot(o_ref[...], w_ref[3 * width : 4 * width, :], TN)


def feed(shards, many, lens, *refs):
    weights, refs = refs[:many], refs[many:]
    h_ref, vec_ref, cot_ref, y_ref, dh_ref, near, far, gv_ref, up_s, e_s, n_s, y_s, de_s, down_ref, g_ref, sems = refs
    width = h_ref.shape[1]
    rows = h_ref.shape[0]
    hidden = down_ref.shape[0]
    half = hidden // 2
    parts = hidden // width
    piece = hidden // shards // parts
    core = lens[2]

    def put_up(owner, number, value):
        size = value.shape[0]
        up_s[number, pl.ds(pl.multiple_of(owner * size, size), size), :] = value

    assemble(lens, weights, 2, put_up, down_ref, sems.at[0])
    if many == 1:
        for shard in range(shards):
            for part in range(parts):
                begin = (shard * parts + part) * piece
                up_s[part, shard * piece : (shard + 1) * piece, :] = down_ref[begin : begin + piece, :]
    assemble(lens, weights, 3, rows_of(down_ref), down_ref, sems.at[1])
    normal, inverse = normalise(h_ref[...])
    n_s[...] = normal
    e_s[...] = (normal * vec_ref[2:3, :] + vec_ref[5:6, :]).astype(BF)
    spot = lax.broadcasted_iota(jnp.int32, (rows, 1), 0) % (rows // PASSES)
    cot = jnp.where(spot < lens[0], cot_ref[...].astype(F32), 0.0)
    df = cot.astype(BF)
    y_s[...] = h_ref[...] + vec_ref[6:7, :]
    de_s[...] = jnp.zeros_like(de_s)
    gv_ref[...] = jnp.zeros_like(gv_ref)

    def body(part, carry):
        place = pl.multiple_of(part * width, width)
        down = down_ref[pl.ds(place, width), :]
        up = up_s[part]
        pre = dot(e_s[...], up, NN) + vec_ref[pl.ds(7 + part, 1), :]
        active = jnp.maximum(pre, 0.0).astype(BF)
        y_s[...] += dot(active, down, NN)
        g_ref[place // half, 1, pl.ds(pl.multiple_of(place % half, width), width), :] = dot(active, df, TN).astype(BF)
        du = jnp.where(pre > 0, dot(df, down, NT), 0.0).astype(BF)
        gv_ref[pl.ds(7 + part, 1), :] = jnp.sum(du.astype(F32), axis=0, keepdims=True)
        gup = dot(e_s[...], du, TN).astype(BF)
        for shard in range(shards):
            begin = (shard * parts + part) * piece
            g_ref[begin // half, 0, pl.ds(pl.multiple_of(begin % half, piece), piece), :] = gup[shard * piece : (shard + 1) * piece, :]
        de_s[...] += dot(du, up, NT)
        return carry

    lax.fori_loop(0, parts, body, 0)
    copies = deliver(core, g_ref, near, far, sems)
    y_ref[...] = y_s[...].astype(BF)
    gv_ref[6:7, :] = jnp.sum(cot, axis=0, keepdims=True)
    back, gain, shift = norm_back(de_s[...], vec_ref[2:3, :], n_s[...], inverse)
    gv_ref[2:3, :] = gain
    gv_ref[5:6, :] = shift
    dh_ref[...] = cot + back
    wait(copies)


def cross_start(w_ref, dh_ref, o_ref, d_ref, g_ref):
    width = dh_ref.shape[1]
    low = dh_ref[...].astype(BF)
    g_ref[...] = dot(o_ref[...], low, NN).astype(BF)
    put_grads(d_ref, dot(w_ref[3 * width :, :], low, NT), o_ref, 0, HEADS)


def cross_attend(q_ref, k_ref, v_ref, d_ref, dq_ref, dk_ref, dv_ref, sk, sv):
    rows = q_ref.shape[2]
    slots = k_ref.shape[2]
    block = rows // 4

    def body(head, carry):
        place = pl.ds(pl.multiple_of(head * 64, 64), 64)
        for piece in range(4):
            dq, dk, dv = attend_backward(head, piece * block, block, 0, slots, q_ref, k_ref, v_ref, d_ref)
            dq_ref[place, piece * block : (piece + 1) * block] = dq
            if piece == 0:
                sk[...] = dk
                sv[...] = dv
            elif piece < 3:
                sk[...] += dk
                sv[...] += dv
            else:
                dk_ref[place, :] = (sk[...] + dk).astype(BF)
                dv_ref[place, :] = (sv[...] + dv).astype(BF)
        return carry

    lax.fori_loop(0, HEADS, body, 0)


def cross_finish(lens, w_ref, dh2_ref, dq_ref, dk_ref, dv_ref, out_ref, h_ref, mem_ref, vec_ref, near, far, dh_ref, gv_ref, g_ref, sems):
    width = h_ref.shape[1]
    core = lens[2]
    memory = mem_ref[...]
    normal, inverse = normalise(h_ref[...])
    low = (normal * vec_ref[1:2, :] + vec_ref[4:5, :]).astype(BF)
    dq = dq_ref[...].T
    g_ref[0, :width, :] = dot(low, dq, TN).astype(BF)
    g_ref[1, width:, :] = out_ref[...]
    dk = dk_ref[...].T
    g_ref[0, width:, :] = dot(memory, dk, TN).astype(BF)
    dv = dv_ref[...].T
    g_ref[1, :width, :] = dot(memory, dv, TN).astype(BF)
    copies = deliver(core, g_ref, near, far, sems)
    back, gain, shift = norm_back(dot(dq, w_ref[0:width, :], NT), vec_ref[1:2, :], normal, inverse)
    gv_ref[...] = jnp.zeros_like(gv_ref)
    gv_ref[1:2, :] = gain
    gv_ref[4:5, :] = shift
    dh_ref[...] = dh2_ref[...] + back
    wait(copies)


def self_backward(chunk, chunks, lens, w_ref, dh_ref, q_ref, k_ref, v_ref, o_ref, x_ref, vec_ref, near, far, dq_ref, dk_ref, dv_ref, d_s, g_ref, sems):
    width = x_ref.shape[1]
    rows = x_ref.shape[0]
    length = rows // PASSES
    heads = HEADS // chunks
    span = width // chunks
    lanes = slice(chunk * span, (chunk + 1) * span)
    core = lens[2]
    dz = dh_ref[...].astype(BF)
    g_ref[1, width:, :] = dot(o_ref[...], dz[:, lanes], NN).astype(BF)
    put_grads(d_s, dot(w_ref[3 * width + chunk * span : 3 * width + (chunk + 1) * span, :], dz, NT), o_ref, chunk * heads, heads)

    def body(head, carry):
        place = pl.ds(pl.multiple_of(head * 64, 64), 64)
        for number in range(PASSES):
            begin = number * length
            dq, dk, dv = attend_backward(head, begin, length, begin, length, q_ref, k_ref, v_ref, d_s)
            dq_ref[place, begin : begin + length] = dq
            dk_ref[place, begin : begin + length] = dk.astype(BF)
            dv_ref[place, begin : begin + length] = dv.astype(BF)
        return carry

    lax.fori_loop(0, heads, body, 0)
    normal, _ = normalise(x_ref[...].astype(F32))
    low = (normal * vec_ref[0:1, :] + vec_ref[3:4, :]).astype(BF)
    for number, store in enumerate((dq_ref, dk_ref, dv_ref)):
        g_ref[number // 2, (number % 2) * width : (number % 2 + 1) * width, :] = dot(low, store[...].T, TN).astype(BF)
    wait(deliver(core, g_ref, near, far, sems))


def self_finish(w_ref, *refs):
    parts = refs[:-5]
    dh_ref, x_ref, vec_ref, out_ref, gv_ref = refs[-5:]
    width = x_ref.shape[1]
    normal, inverse = normalise(x_ref[...].astype(F32))
    total = None
    span = parts[0].shape[0]
    for place, part in enumerate(parts):
        chunk, number = place // 3, place % 3
        lanes = slice(chunk * span, (chunk + 1) * span)
        value = dot(part[...].T, w_ref[number * width : (number + 1) * width, lanes], NT)
        total = value if total is None else total + value
    back, gain, shift = norm_back(total, vec_ref[0:1, :], normal, inverse)
    gv_ref[...] = jnp.zeros_like(gv_ref)
    gv_ref[0:1, :] = gain
    gv_ref[3:4, :] = shift
    out_ref[...] = dh_ref[...] + back


def memory_finish(w_ref, dk_ref, dv_ref, out_ref):
    width = dk_ref.shape[0]
    dk, dv = dk_ref[...].T, dv_ref[...].T
    out_ref[...] = dot(dk, w_ref[width : 2 * width, :], NT) + dot(dv, w_ref[2 * width : 3 * width, :], NT)


def prepare(flags, w_ref, low_ref, whole_s, order_s, sems):
    size = low_ref.shape[0]
    share = w_ref.shape[0]
    parts = share // size
    begin = pl.multiple_of(flags[1] * size, size)

    @pl.when(flags[0] == 0)
    def _():
        part = whole_s.at[pl.ds(0, size)]
        copy = pltpu.make_async_copy(w_ref.at[pl.ds(begin, size)], part, sems.at[0])
        copy.start()
        copy.wait()
        low_ref[...] = part[...].astype(BF)

    @pl.when(flags[0] == 1)
    def _():
        copy = pltpu.make_async_copy(w_ref, whole_s, sems.at[1])
        copy.start()
        copy.wait()
        for lane in range(order_s.shape[0]):
            lanes = slice(lane * 128, (lane + 1) * 128)
            order_s[lane] = whole_s[:, lanes]
            if parts == 4:
                low_ref[:, lanes] = order_s[lane, pl.ds(flags[1], size, stride=4), :].astype(BF)
            else:
                for number in range(4):
                    rows = slice(number * share // 4, (number + 1) * share // 4)
                    low_ref[rows, lanes] = order_s[lane, pl.ds(number, share // 4, stride=4), :].astype(BF)


def adam(chunk, blocks, flags, *refs):
    parts = refs[: 3 * blocks]
    w_ref, state_ref = refs[3 * blocks : 3 * blocks + 2]
    new_ref, upper_ref, lower_ref, g_s, order_s, three_s, sems = refs[-7:]
    share, span = w_ref.shape
    part = share // 4
    lanes = pl.ds(chunk * span, span)
    for block in range(blocks):

        @pl.when(flags[0] == block)
        def _(block=block):
            for number in range(3):
                source = parts[3 * block + number]
                source = source if source.shape[1] == span else source.at[:, lanes]
                pltpu.make_async_copy(source, three_s.at[number], sems.at[number]).start()

    for number in range(3):
        pltpu.make_async_copy(three_s.at[number], three_s.at[number], sems.at[number]).wait()
    g_s[...] = three_s[0].astype(F32) + three_s[1].astype(F32) + three_s[2].astype(F32)

    @pl.when(flags[1] == 1)
    def _():
        for lane in range(order_s.shape[0]):
            lanes = slice(lane * 128, (lane + 1) * 128)
            for number in range(4):
                order_s[lane, pl.ds(number, part, stride=4), :] = g_s[number * part : (number + 1) * part, lanes]
            g_s[:, lanes] = order_s[lane]

    moment, second, delta = inner_update(w_ref[...], g_s[...], state_ref[0, 0], state_ref[0, 1], decay_rate)
    new_ref[0, 0] = moment
    new_ref[0, 1] = second
    low = delta.astype(BF)
    upper_ref[...] = low[: share // 2]
    lower_ref[...] = low[share // 2 :]


def outer(replicas, one_a, one_b, two_a, two_b, w_ref, mom_ref, *refs):
    out_ref = refs[-1]
    share = w_ref.shape[0] // 2
    for half, (one, two) in enumerate(((one_a, two_a), (one_b, two_b))):
        rows = slice(half * share, (half + 1) * share)
        mean = (one[...].astype(F32) + two[...].astype(F32)) / replicas
        momentum = outer_push * mom_ref[rows, :] + mean
        out_ref[0, rows, :] = w_ref[rows, :] - rate_outer * (mean + outer_push * momentum)
        out_ref[1, rows, :] = mean
        out_ref[2, rows, :] = momentum


VM = pl.BlockSpec(memory_space=pltpu.VMEM)
SM = pl.BlockSpec(memory_space=pltpu.SMEM)
HB = pl.BlockSpec(memory_space=pl.ANY)
FAR = pl.BlockSpec(memory_space=pltpu.HBM)


def call(body, name, ins, outs, scratch=(), places=None, grid=(), aliases=None, room=12):
    shapes = tuple(jax.ShapeDtypeStruct(shape, kind) for shape, kind in outs)
    return pl.pallas_call(
        body,
        name=name,
        grid=grid,
        cost_estimate=pl.CostEstimate(flops=0, transcendentals=0, bytes_accessed=0),
        input_output_aliases=aliases or {},
        out_shape=shapes,
        in_specs=ins,
        out_specs=tuple(places or [VM] * len(outs)),
        scratch_shapes=[item if not isinstance(item, tuple) else pltpu.VMEM(*item) for item in scratch],
        compiler_params=pltpu.CompilerParams(vmem_limit_bytes=room << 20),
    )


def inner_update(weight, gradient, moment_one, second, shrink):
    moment_new = beta_first * moment_one + (1.0 - beta_first) * gradient
    second_new = beta_second * second + (1.0 - beta_second) * gradient * gradient
    moment_hat = moment_new / (1.0 - beta_first**STEP)
    second_hat = second_new / (1.0 - beta_second**STEP)
    local_weight = weight - rate_inner * (
        moment_hat / (jnp.sqrt(second_hat) + adam_epsilon) + shrink * weight
    )
    return (moment_new, second_new, weight - local_weight)


def swap(values, axis, bit):
    count = lax.axis_size(axis)
    return lax.ppermute(values, axis, [(i, i ^ bit) for i in range(count)])


def total_over(values, axis):
    count = lax.axis_size(axis)
    if count & (count - 1):
        return lax.psum(values, axis)
    bit = 1
    while bit < count:
        values = values + swap(values, axis, bit)
        bit *= 2
    return values


def hop(values, *moves):
    return lax.ppermute(values, "fsdp", [(2 * one + core, 2 * two + core) for one, two in moves for core in range(2)])


def add_low(one, two):
    return (one.astype(F32) + two.astype(F32)).astype(BF)


def cycle(values, distance):
    count = lax.axis_size("fsdp")
    return lax.ppermute(values, "fsdp", [((to + 2 * distance) % count, to) for to in range(count)])


def around(piece):
    return [piece] + [swap(piece, "rep", distance) for distance in (1, 2, 3)]


def with_other(quarters):
    return quarters + [swap(quarter, "fsdp", 1) for quarter in quarters]


def gather_pieces(piece, vectors, x):
    chip = lax.axis_index("fsdp") // 2
    vectors = vectors + swap(vectors, "fsdp", 1)
    slots = [piece] + [cycle(piece, distance) for distance in (1, 2, 3)]
    vectors = vectors + swap(vectors, "fsdp", 2)
    slots, vectors, x = lax.optimization_barrier((slots, vectors, x))
    pieces = [lax.select_n((block - chip) % 4, *slots) for block in range(4)]
    return pieces, vectors + swap(vectors, "fsdp", 4), x


def per_device(embed, first_tokens, sample_tokens, seq_len, mem_len, memory, cotangent, params, vecs, inner_state, inner_vecs, outer_mom, outer_vecs):
    groups = lax.axis_size("fsdp")
    replicas = lax.axis_size("rep")
    direct = groups == 8 and replicas == 4
    share, width = params.shape
    hidden = 4 * width
    me = lax.axis_index("fsdp")
    chip = me // 2
    own_up = (me >= 2 * hidden // share) & (me < 3 * hidden // share)
    rank = lax.axis_index("rep")
    count, columns = vecs.shape
    vectors = lax.dynamic_update_slice(jnp.zeros((16, width), BF), vecs.astype(BF), (0, me * columns))
    (low,) = call(
        prepare, "prepare", [SM, FAR], [((share // 4 if direct else share, width), BF)],
        [((share, width), F32), ((width // 128, share, 128), F32), pltpu.SemaphoreType.DMA((2,))],
    )(jnp.stack([own_up, rank if direct else 0]).astype(jnp.int32), params)
    x = embed[jnp.concatenate([first_tokens[0], sample_tokens[0]])]
    if direct:
        pieces, vectors, x = gather_pieces(low, vectors, x)
        core = me % 2
        w_self = with_other(around(pieces[0]))
        w_cross = around(pieces[1])
    else:
        w_self = w_cross = w_feed = [lax.all_gather(low, "fsdp", axis=0, tiled=True)]
        vectors = total_over(vectors, "fsdp")
        core = 0
    vectors = vectors.astype(F32)
    lens = jnp.stack([seq_len[0], mem_len[0], core, chip, rank]).astype(jnp.int32)
    many = len(w_self)
    far_w = [FAR if many == 1 else VM] * many
    length = first_tokens.shape[1]
    rows = PASSES * length
    cot = cotangent.reshape(rows, width)
    memory = memory[0]
    slots = memory.shape[0]

    heads_n = ((HEADS, AUG, rows), BF)
    heads_m = ((HEADS, AUG, slots), BF)
    flat_n = ((width, rows), BF)
    flat_m = ((width, slots), BF)
    full = ((rows, width), F32)
    half_g = ((hidden // 2, width), BF)
    block_w = ((hidden, width), BF)
    vec_g = ((16, width), F32)
    peak = ((8, length), F32)
    sems = pltpu.SemaphoreType.DMA((2,))
    qs, ks, vs, o_self, h, weights_self = call(
        functools.partial(self_forward, many), "self_forward", [SM] + far_w + [VM] * 2,
        [heads_n, heads_n, heads_n, flat_n, full, block_w],
        [((length, length), F32)] * 2 + [peak] * 2 + [sems],
    )(lens, *w_self, x, vectors)
    if direct:
        h, w_cross = lax.optimization_barrier((h, w_cross))
        w_cross = with_other(w_cross)
        w_feed = around(jnp.stack(pieces[2:]))
    qc, kc, vc, o_cross, h2, weights_cross = call(
        functools.partial(cross_forward, many), "cross_forward", [SM] + far_w + [VM] * 3,
        [heads_n, heads_m, heads_m, flat_n, full, block_w],
        [((slots, length), F32)] * 2 + [peak] * 2 + [sems],
    )(lens, *w_cross, h, memory, vectors)
    if direct:
        h2, w_feed = lax.optimization_barrier((h2, w_feed))
        w_feed = with_other(w_feed)
    pair_g = ((2, hidden // 2, width), BF)
    y, dh2, feed_near, feed_far, gv3 = call(
        functools.partial(feed, hidden // min(share, hidden), many), "feed", [SM] + far_w + [VM] * 3,
        [((rows, width), BF), full, pair_g, pair_g, vec_g],
        [((4, width, width), BF), ((rows, width), BF), full, full, full, block_w, ((2, 2, hidden // 2, width), BF), sems],
        [VM, VM, HB, HB, VM], room=26,
    )(lens, *w_feed, h2, vectors, cot)
    if direct:
        feed_got = swap(feed_far, "fsdp", 1)
    do_cross, g_out = call(
        cross_start, "cross_start", [VM] * 3, [heads_n, ((width, width), BF)],
    )(weights_cross, dh2, o_cross)
    if direct:
        up_sum, down_sum = add_low(feed_near[0], feed_got[0]), add_low(feed_near[1], feed_got[1])
        do_cross, up_sum, down_sum = lax.optimization_barrier((do_cross, up_sum, down_sum))
        up_got = hop(up_sum, (0, 1), (3, 2))
    dqt, dkt, dvt = call(
        cross_attend, "cross_attend", [VM] * 4, [flat_n, flat_m, flat_m], [((64, slots), F32)] * 2,
    )(qc, kc, vc, do_cross)
    if direct:
        dqt, up_got, down_sum = lax.optimization_barrier((dqt, up_got, down_sum))
        down_got = hop(down_sum, (0, 1), (2, 3))
    cross_near, cross_far, dh, gv2 = call(
        cross_finish, "cross_finish", [SM] + [VM] * 9,
        [half_g, half_g, full, vec_g],
        [pair_g, sems],
        [HB, HB, VM, VM],
    )(lens, weights_cross, dh2, dqt, dkt, dvt, g_out, h, memory, vectors)
    if direct:
        cross_got = swap(cross_far, "fsdp", 1)
    (g_mem,) = call(
        memory_finish, "memory_finish", [VM] * 3, [(memory.shape, F32)],
    )(weights_cross, dkt, dvt)
    chunks = 2
    span = width // chunks
    chunk_g = ((hidden // 2, span), BF)
    if direct:
        up_late = add_low(up_sum, up_got)
        cross_sum = add_low(cross_near, cross_got)
        dh, g_mem, up_late, cross_sum = lax.optimization_barrier((dh, g_mem, up_late, cross_sum))
        cross_hop = hop(cross_sum, (3, 2))
        up_last = hop(up_late, (1, 2))

    def chunk_of(chunk):
        heads = [pl.BlockSpec((HEADS // chunks, AUG, rows), lambda i: (chunk, 0, 0))] * 3
        return call(
            functools.partial(self_backward, chunk, chunks), "self_backward", [SM] + [VM] * 2 + heads + [VM] * 3,
            [chunk_g, chunk_g] + [((span, rows), BF)] * 3,
            [((HEADS // chunks, AUG, rows), BF), ((2, hidden // 2, span), BF), sems],
            [HB, HB, VM, VM, VM], (1,),
        )(lens, weights_self, dh, qs, ks, vs, o_self, x, vectors)

    near_a, far_a, *grads_a = chunk_of(0)
    if direct:
        got_a = swap(far_a, "fsdp", 1)
        dh, grads_a = lax.optimization_barrier((dh, grads_a))
    near_b, far_b, *grads_b = chunk_of(1)
    if direct:
        far_b, up_last, got_a, dh, cross_hop, down_got = lax.optimization_barrier((far_b, up_last, got_a, dh, cross_hop, down_got))
        got_b = swap(far_b, "fsdp", 1)
        sum_a = add_low(near_a, got_a)
        hop_a = hop(sum_a, (1, 0), (3, 2))
        cross_late = add_low(cross_sum, cross_hop)
        cross_last = hop(cross_late, (2, 1))
        cross_side = hop(cross_sum, (0, 1))
        down_late = add_low(down_sum, down_got)
        down_last = hop(down_late, (1, 3))
        sum_b = add_low(near_b, got_b)
        hop_b = hop(sum_b, (1, 0), (3, 2))
        late_a, hop_a, dh = lax.optimization_barrier((add_low(sum_a, hop_a), hop_a, dh))
        last_a = hop(late_a, (2, 0))
    g_in, gv1 = call(
        self_finish, "self_finish", [VM] * 10, [full, vec_g],
    )(weights_self, *grads_a, *grads_b, dh, x, vectors)
    gv = gv1 + gv2 + gv3
    if direct:
        late_b, hop_b, gv, g_in = lax.optimization_barrier((add_low(sum_b, hop_b), hop_b, gv, g_in))
        last_b = hop(late_b, (2, 0))
        gv = gv + swap(gv, "fsdp", 1)
        last_a, gv = lax.optimization_barrier((last_a, gv))
        gv = gv + swap(gv, "fsdp", 2)
        last_b, gv = lax.optimization_barrier((last_b, gv))
        gv = gv + swap(gv, "fsdp", 4)
        grad_v = lax.dynamic_slice(gv, (0, me * columns), (count, columns))
        cross = (cross_sum, cross_side, cross_last)
        feeds = [(up_sum, up_got, up_last), (down_sum, down_got, down_last)]
        parts = [[first, cross, *feeds] for first in ((sum_a, hop_a, last_a), (sum_b, hop_b, last_b))]
        block = chip
    else:
        whole = [jnp.concatenate([near_a, near_b], axis=1), jnp.concatenate([far_a, far_b], axis=1), cross_near, cross_far]
        whole += [feed_near[0], feed_far[0], feed_near[1], feed_far[1]]
        rest = lax.psum_scatter(jnp.concatenate(whole), "fsdp", scatter_dimension=0, tiled=True)
        parts = [[[rest, jnp.zeros_like(rest), jnp.zeros_like(rest)]]] * chunks
        block = 0
        grad_v = lax.dynamic_slice(total_over(gv, "fsdp"), (0, me * columns), (count, columns))
    flags = jnp.stack([block, own_up]).astype(jnp.int32)
    inner_new = param_results = None
    deltas = []
    for chunk in range(chunks):
        lanes = pl.BlockSpec((share, span), lambda i, c=chunk: (0, c))
        taken = [item for three in parts[chunk] for item in three]
        part = pl.BlockSpec((share // 2, span), lambda i: (0, 0))
        state = pl.BlockSpec((1, 2, share, span), lambda i, c=chunk: (0, 0, 0, c))
        inner_new, upper, lower = call(
            functools.partial(adam, chunk, len(parts[chunk])), "adam", [SM] + [FAR] * len(taken) + [lanes, state] + [HB] * min(chunk, 1),
            [(inner_state.shape, F32)] + [((share // 2, span), BF)] * 2,
            [((share, span), F32), ((span // 128, share, 128), F32), ((3, share, span), BF), pltpu.SemaphoreType.DMA((3,))],
            [state, part, part], (1,), {len(taken) + 3: 0} if chunk else None, 16,
        )(flags, *taken, params, inner_state, *([inner_new] if chunk else []))
        deltas.append((upper, lower))
    for chunk, (upper, lower) in enumerate(deltas):
        if replicas == 4:
            upper = add_low(upper, swap(upper, "rep", 1))
            lower = add_low(lower, swap(lower, "rep", 2))
            others = [swap(upper, "rep", 2), swap(lower, "rep", 1)]
        else:
            upper, lower = lax.psum(upper, "rep"), lax.psum(lower, "rep")
            others = [jnp.zeros_like(upper), jnp.zeros_like(lower)]
        lanes = pl.BlockSpec((share, span), lambda i, c=chunk: (0, c))
        part = pl.BlockSpec((share // 2, span), lambda i: (0, 0))
        (param_results,) = call(
            functools.partial(outer, replicas), "outer", [part] * 4 + [lanes, lanes] + [HB] * min(chunk, 1),
            [((3, share, width), F32)], (),
            [pl.BlockSpec((3, share, span), lambda i, c=chunk: (0, 0, c))], (1,), {6: 0} if chunk else None,
        )(upper, lower, *others, params, outer_mom, *([param_results] if chunk else []))
    moment_v, second_v, delta_v = inner_update(vecs, grad_v, inner_vecs[0, 0], inner_vecs[0, 1], 0.0)
    if replicas == 4:
        low_v = delta_v.astype(BF)
        mean_v = sum([swap(low_v, "rep", bit).astype(F32) for bit in (1, 2, 3)], low_v.astype(F32)) / replicas
    else:
        mean_v = lax.psum(delta_v.astype(BF), "rep").astype(F32) / replicas
    momentum_v = outer_push * outer_vecs + mean_v
    new_v = vecs - rate_outer * (mean_v + outer_push * momentum_v)
    return (
        y.reshape(PASSES, 1, length, width),
        g_in.reshape(PASSES, 1, length, width),
        g_mem[None],
        param_results,
        jnp.stack([new_v, mean_v, momentum_v]),
        inner_new,
        jnp.stack([moment_v, second_v])[None],
    )


def solution(mesh):
    both = ("rep", "fsdp")
    return jax.shard_map(
        per_device,
        mesh=mesh,
        in_specs=(
            P(),
            P(both, None),
            P(both, None),
            P(both),
            P(both),
            P(both, None, None),
            P(None, both, None, None),
            P("fsdp", None),
            P(None, "fsdp"),
            P("rep", None, "fsdp", None),
            P("rep", None, None, "fsdp"),
            P("fsdp", None),
            P(None, "fsdp"),
        ),
        out_specs=(
            P(None, both, None, None),
            P(None, both, None, None),
            P(both, None, None),
            P(None, "fsdp", None),
            P(None, None, "fsdp"),
            P("rep", None, "fsdp", None),
            P("rep", None, None, "fsdp"),
        ),
        check_vma=False,
    )
```

```python
import functools
import math

import jax
import jax.numpy as jnp
from jax import lax
from jax.experimental import pallas as pl
from jax.experimental.pallas import tpu as pltpu
from jax.sharding import PartitionSpec as P

HEADS = 8
STEP = 8
PASSES = 2
AUG = 80
norm_epsilon = 1e-05
beta_first = 0.9
beta_second = 0.999
adam_epsilon = 1e-08
rate_inner = 0.1
rate_outer = 0.7
outer_push = 0.9
decay_rate = 0.01

BF = jnp.bfloat16
F32 = jnp.float32
NN = (((1,), (0,)), ((), ()))
NT = (((1,), (1,)), ((), ()))
TN = (((0,), (0,)), ((), ()))
TT = (((0,), (1,)), ((), ()))


def dot(left, right, dims):
    return lax.dot_general(left, right, dims, preferred_element_type=F32)


def normalise(values):
    centre = values - jnp.mean(values, axis=-1, keepdims=True)
    spread = jnp.mean(centre * centre, axis=-1, keepdims=True)
    inverse = lax.rsqrt(spread + norm_epsilon)
    return centre * inverse, inverse


def norm_back(grad_out, gain_row, normal, inverse):
    grad_normal = grad_out * gain_row
    mean_grad = jnp.mean(grad_normal, axis=-1, keepdims=True)
    mean_proj = jnp.mean(grad_normal * normal, axis=-1, keepdims=True)
    grad_in = inverse * (grad_normal - mean_grad - normal * mean_proj)
    return grad_in, jnp.sum(grad_out * normal, axis=0, keepdims=True), jnp.sum(grad_out, axis=0, keepdims=True)


def thirds(row):
    high = row.astype(BF)
    rest = row - high.astype(F32)
    middle = rest.astype(BF)
    low = (rest - middle.astype(F32)).astype(BF)
    return high.astype(F32), middle.astype(F32), low.astype(F32)


def tail_rows(width, rows):
    place = lax.broadcasted_iota(jnp.int32, (AUG - 64, width), 0)
    tail = jnp.zeros((AUG - 64, width), F32)
    for number, row in enumerate(rows):
        tail = jnp.where(place == number, row, tail)
    return tail.astype(BF)


def put_heads(target, matrix_t, scale, tail):
    low = matrix_t.astype(BF)
    if scale != 1.0:
        low = low * BF(scale)
    size = low.shape[0] // HEADS
    for head in range(HEADS):
        target[head, :size, :] = low[head * size : (head + 1) * size]
        target[head, size:, :] = tail


def key_tail(width, count, period):
    spot = lax.broadcasted_iota(jnp.int32, (1, width), 1) % period
    bias = jnp.where(spot < count, 0.0, -1e30)
    return tail_rows(width, [bias, 1.0, 1.0, 1.0])


def attend_forward(units, where_of, block, q_ref, k_ref, v_ref, o_ref, s_a, s_b, m_a, m_b):
    keys = s_a.shape[0]

    def scores(step, store, peak):
        head, first, key_first = where_of(jnp.minimum(step, units - 1))
        value = dot(k_ref[head, :, pl.ds(key_first, keys)], q_ref[head, :, pl.ds(first, block)], TN)
        store[...] = value
        peak[...] = jnp.broadcast_to(jnp.max(value, axis=0, keepdims=True), peak.shape)

    def finish(step, store, peak):
        head, first, key_first = where_of(step)
        top = peak[0:1, :]
        weight = jnp.exp(store[...] - top).astype(BF)
        mixed = dot(v_ref[head, :, pl.ds(key_first, keys)], weight, NN)
        total = mixed[64:65, :]
        o_ref[pl.ds(pl.multiple_of(head * 64, 64), 64), pl.ds(first, block)] = (mixed[:64] * (1.0 / total)).astype(BF)
        high, middle, low = thirds(top + jnp.log(total))
        q_ref[head, 64:, pl.ds(first, block)] = tail_rows(block, [1.0, -high, -middle, -low])

    scores(0, s_a, m_a)

    def body(pair, carry):
        step = 2 * pair
        scores(step + 1, s_b, m_b)
        finish(step, s_a, m_a)
        scores(step + 2, s_a, m_a)
        finish(step + 1, s_b, m_b)
        return carry

    lax.fori_loop(0, units // 2 - 1, body, 0)
    step = units - 2
    scores(step + 1, s_b, m_b)
    finish(step, s_a, m_a)
    finish(step + 1, s_b, m_b)


def attend_backward(head, first, block, key_first, keys, q_ref, k_ref, v_ref, d_ref):
    here = pl.ds(first, block)
    there = pl.ds(key_first, keys)
    grad = d_ref[head, :, here]
    query = q_ref[head, :, here]
    key_t = k_ref[head, :, there]
    weight = jnp.exp(dot(query, key_t, TN))
    grad_scores = (weight * dot(grad, v_ref[head, :, there], TN)).astype(BF)
    grad_value = dot(grad[:64], weight.astype(BF), NN)
    grad_key = dot(query[:64], grad_scores, NN)
    grad_query = dot(key_t[:64], grad_scores, NT) * 0.125
    return grad_query.astype(BF), grad_key, grad_value


def put_grads(d_ref, grad_t, o_ref, skip, heads):
    low = grad_t.astype(BF)
    for head in range(heads):
        part = low[head * 64 : (head + 1) * 64]
        both = part.astype(F32) * o_ref[(skip + head) * 64 : (skip + head + 1) * 64, :].astype(F32)
        high, middle, rest = thirds(jnp.sum(both, axis=0, keepdims=True))
        d_ref[head, :64, :] = part
        d_ref[head, 64:, :] = tail_rows(low.shape[1], [-high, -middle, -rest])


def assemble(lens, weights, block, put, target, sem):
    if len(weights) == 1:
        rows = target.shape[0]
        copy = pltpu.make_async_copy(weights[0].at[pl.ds(block * rows, rows)], target, sem)
        copy.start()
        copy.wait()
        return
    core, rank = lens[2], lens[4]
    for side in range(2):
        for distance in range(4):
            source = weights[4 * side + distance]
            value = source[block % 2] if len(source.shape) == 3 else source[...]
            put(core if side == 0 else 1 - core, rank ^ distance, value)


def rows_of(target):
    quarter = target.shape[0] // 8

    def put(owner, number, value):
        target[pl.ds(pl.multiple_of((4 * owner + number) * quarter, quarter), quarter), :] = value

    return put


def deliver(core, source, near, far, sems):
    first = pltpu.make_async_copy(source.at[core], near, sems.at[0])
    second = pltpu.make_async_copy(source.at[1 - core], far, sems.at[1])
    first.start()
    second.start()
    return first, second


def wait(copies):
    for copy in copies:
        copy.wait()


def self_forward(many, lens, *refs):
    weights, refs = refs[:many], refs[many:]
    x_ref, vec_ref, q_ref, k_ref, v_ref, o_ref, h_ref, w_ref, s_a, s_b, m_a, m_b, sems = refs
    width = x_ref.shape[1]
    rows = x_ref.shape[0]
    length = rows // PASSES
    assemble(lens, weights, 0, rows_of(w_ref), w_ref, sems.at[0])
    x = x_ref[...].astype(F32)
    normal, _ = normalise(x)
    low = (normal * vec_ref[0:1, :] + vec_ref[3:4, :]).astype(BF)
    put_heads(q_ref, dot(w_ref[0:width, :], low, TT), 0.125, tail_rows(rows, [1.0]))
    put_heads(k_ref, dot(w_ref[width : 2 * width, :], low, TT), 1.0, key_tail(rows, lens[0], length))
    put_heads(v_ref, dot(w_ref[2 * width : 3 * width, :], low, TT), 1.0, tail_rows(rows, [1.0, 1.0, 1.0]))

    def where_of(step):
        place = pl.multiple_of((step % PASSES) * length, length)
        return step // PASSES, place, place

    attend_forward(HEADS * PASSES, where_of, length, q_ref, k_ref, v_ref, o_ref, s_a, s_b, m_a, m_b)
    h_ref[...] = x_ref[...].astype(F32) + dot(o_ref[...], w_ref[3 * width : 4 * width, :], TN)


def cross_forward(many, lens, *refs):
    weights, refs = refs[:many], refs[many:]
    h_ref, mem_ref, vec_ref, q_ref, k_ref, v_ref, o_ref, out_ref, w_ref, s_a, s_b, m_a, m_b, sems = refs
    width = h_ref.shape[1]
    rows = h_ref.shape[0]
    slots = mem_ref.shape[0]
    block = s_a.shape[1]
    assemble(lens, weights, 1, rows_of(w_ref), w_ref, sems.at[0])
    normal, _ = normalise(h_ref[...])
    low = (normal * vec_ref[1:2, :] + vec_ref[4:5, :]).astype(BF)
    memory = mem_ref[...]
    put_heads(q_ref, dot(w_ref[0:width, :], low, TT), 0.125, tail_rows(rows, [1.0]))
    put_heads(k_ref, dot(w_ref[width : 2 * width, :], memory, TT), 1.0, key_tail(slots, lens[1], slots))
    put_heads(v_ref, dot(w_ref[2 * width : 3 * width, :], memory, TT), 1.0, tail_rows(slots, [1.0, 1.0, 1.0]))
    pieces = rows // block

    def where_of(step):
        return step // pieces, pl.multiple_of((step % pieces) * block, block), 0

    attend_forward(HEADS * pieces, where_of, block, q_ref, k_ref, v_ref, o_ref, s_a, s_b, m_a, m_b)
    out_ref[...] = h_ref[...] + dot(o_ref[...], w_ref[3 * width : 4 * width, :], TN)


def feed(shards, many, lens, *refs):
    weights, refs = refs[:many], refs[many:]
    h_ref, vec_ref, cot_ref, y_ref, dh_ref, near, far, gv_ref, up_s, e_s, n_s, y_s, de_s, down_ref, g_ref, sems = refs
    width = h_ref.shape[1]
    rows = h_ref.shape[0]
    hidden = down_ref.shape[0]
    half = hidden // 2
    parts = hidden // width
    piece = hidden // shards // parts
    core = lens[2]

    def put_up(owner, number, value):
        size = value.shape[0]
        up_s[number, pl.ds(pl.multiple_of(owner * size, size), size), :] = value

    assemble(lens, weights, 2, put_up, down_ref, sems.at[0])
    if many == 1:
        for shard in range(shards):
            for part in range(parts):
                begin = (shard * parts + part) * piece
                up_s[part, shard * piece : (shard + 1) * piece, :] = down_ref[begin : begin + piece, :]
    assemble(lens, weights, 3, rows_of(down_ref), down_ref, sems.at[1])
    normal, inverse = normalise(h_ref[...])
    n_s[...] = normal
    e_s[...] = (normal * vec_ref[2:3, :] + vec_ref[5:6, :]).astype(BF)
    spot = lax.broadcasted_iota(jnp.int32, (rows, 1), 0) % (rows // PASSES)
    cot = jnp.where(spot < lens[0], cot_ref[...].astype(F32), 0.0)
    df = cot.astype(BF)
    y_s[...] = h_ref[...] + vec_ref[6:7, :]
    de_s[...] = jnp.zeros_like(de_s)
    gv_ref[...] = jnp.zeros_like(gv_ref)

    def body(part, carry):
        place = pl.multiple_of(part * width, width)
        down = down_ref[pl.ds(place, width), :]
        up = up_s[part]
        pre = dot(e_s[...], up, NN) + vec_ref[pl.ds(7 + part, 1), :]
        active = jnp.maximum(pre, 0.0).astype(BF)
        y_s[...] += dot(active, down, NN)
        g_ref[place // half, 1, pl.ds(pl.multiple_of(place % half, width), width), :] = dot(active, df, TN).astype(BF)
        du = jnp.where(pre > 0, dot(df, down, NT), 0.0).astype(BF)
        gv_ref[pl.ds(7 + part, 1), :] = jnp.sum(du.astype(F32), axis=0, keepdims=True)
        gup = dot(e_s[...], du, TN).astype(BF)
        for shard in range(shards):
            begin = (shard * parts + part) * piece
            g_ref[begin // half, 0, pl.ds(pl.multiple_of(begin % half, piece), piece), :] = gup[shard * piece : (shard + 1) * piece, :]
        de_s[...] += dot(du, up, NT)
        return carry

    lax.fori_loop(0, parts, body, 0)
    copies = deliver(core, g_ref, near, far, sems)
    y_ref[...] = y_s[...].astype(BF)
    gv_ref[6:7, :] = jnp.sum(cot, axis=0, keepdims=True)
    back, gain, shift = norm_back(de_s[...], vec_ref[2:3, :], n_s[...], inverse)
    gv_ref[2:3, :] = gain
    gv_ref[5:6, :] = shift
    dh_ref[...] = cot + back
    wait(copies)


def cross_start(w_ref, dh_ref, o_ref, d_ref, g_ref):
    width = dh_ref.shape[1]
    low = dh_ref[...].astype(BF)
    g_ref[...] = dot(o_ref[...], low, NN).astype(BF)
    put_grads(d_ref, dot(w_ref[3 * width :, :], low, NT), o_ref, 0, HEADS)


def cross_attend(q_ref, k_ref, v_ref, d_ref, dq_ref, dk_ref, dv_ref, sk, sv):
    rows = q_ref.shape[2]
    slots = k_ref.shape[2]
    block = rows // 4

    def body(head, carry):
        place = pl.ds(pl.multiple_of(head * 64, 64), 64)
        for piece in range(4):
            dq, dk, dv = attend_backward(head, piece * block, block, 0, slots, q_ref, k_ref, v_ref, d_ref)
            dq_ref[place, piece * block : (piece + 1) * block] = dq
            if piece == 0:
                sk[...] = dk
                sv[...] = dv
            elif piece < 3:
                sk[...] += dk
                sv[...] += dv
            else:
                dk_ref[place, :] = (sk[...] + dk).astype(BF)
                dv_ref[place, :] = (sv[...] + dv).astype(BF)
        return carry

    lax.fori_loop(0, HEADS, body, 0)


def cross_finish(lens, w_ref, dh2_ref, dq_ref, dk_ref, dv_ref, out_ref, h_ref, mem_ref, vec_ref, near, far, dh_ref, gv_ref, g_ref, sems):
    width = h_ref.shape[1]
    core = lens[2]
    memory = mem_ref[...]
    normal, inverse = normalise(h_ref[...])
    low = (normal * vec_ref[1:2, :] + vec_ref[4:5, :]).astype(BF)
    dq = dq_ref[...].T
    g_ref[0, :width, :] = dot(dq_ref[...], low, NN).T.astype(BF)
    g_ref[1, width:, :] = out_ref[...]
    g_ref[0, width:, :] = dot(dk_ref[...], memory, NN).T.astype(BF)
    g_ref[1, :width, :] = dot(dv_ref[...], memory, NN).T.astype(BF)
    copies = deliver(core, g_ref, near, far, sems)
    back, gain, shift = norm_back(dot(dq, w_ref[0:width, :], NT), vec_ref[1:2, :], normal, inverse)
    gv_ref[...] = jnp.zeros_like(gv_ref)
    gv_ref[1:2, :] = gain
    gv_ref[4:5, :] = shift
    dh_ref[...] = dh2_ref[...] + back
    wait(copies)


def self_backward(chunk, chunks, lens, w_ref, dh_ref, q_ref, k_ref, v_ref, o_ref, x_ref, vec_ref, near, far, dq_ref, dk_ref, dv_ref, d_s, g_ref, sems):
    width = x_ref.shape[1]
    rows = x_ref.shape[0]
    length = rows // PASSES
    heads = HEADS // chunks
    span = width // chunks
    lanes = slice(chunk * span, (chunk + 1) * span)
    core = lens[2]
    dz = dh_ref[...].astype(BF)
    g_ref[1, width:, :] = dot(o_ref[...], dz[:, lanes], NN).astype(BF)
    put_grads(d_s, dot(w_ref[3 * width + chunk * span : 3 * width + (chunk + 1) * span, :], dz, NT), o_ref, chunk * heads, heads)

    def body(head, carry):
        place = pl.ds(pl.multiple_of(head * 64, 64), 64)
        for number in range(PASSES):
            begin = number * length
            dq, dk, dv = attend_backward(head, begin, length, begin, length, q_ref, k_ref, v_ref, d_s)
            dq_ref[place, begin : begin + length] = dq
            dk_ref[place, begin : begin + length] = dk.astype(BF)
            dv_ref[place, begin : begin + length] = dv.astype(BF)
        return carry

    lax.fori_loop(0, heads, body, 0)
    normal, _ = normalise(x_ref[...].astype(F32))
    low = (normal * vec_ref[0:1, :] + vec_ref[3:4, :]).astype(BF)
    for number, store in enumerate((dq_ref, dk_ref, dv_ref)):
        g_ref[number // 2, (number % 2) * width : (number % 2 + 1) * width, :] = dot(low, store[...].T, TN).astype(BF)
    wait(deliver(core, g_ref, near, far, sems))


def self_finish(w_ref, *refs):
    parts = refs[:-5]
    dh_ref, x_ref, vec_ref, out_ref, gv_ref = refs[-5:]
    width = x_ref.shape[1]
    normal, inverse = normalise(x_ref[...].astype(F32))
    total = None
    span = parts[0].shape[0]
    for place, part in enumerate(parts):
        chunk, number = place // 3, place % 3
        lanes = slice(chunk * span, (chunk + 1) * span)
        value = dot(part[...].T, w_ref[number * width : (number + 1) * width, lanes], NT)
        total = value if total is None else total + value
    back, gain, shift = norm_back(total, vec_ref[0:1, :], normal, inverse)
    gv_ref[...] = jnp.zeros_like(gv_ref)
    gv_ref[0:1, :] = gain
    gv_ref[3:4, :] = shift
    out_ref[...] = dh_ref[...] + back


def memory_finish(w_ref, dk_ref, dv_ref, out_ref):
    width = dk_ref.shape[0]
    dk, dv = dk_ref[...].T, dv_ref[...].T
    out_ref[...] = dot(dk, w_ref[width : 2 * width, :], NT) + dot(dv, w_ref[2 * width : 3 * width, :], NT)


def prepare(flags, w_ref, low_ref, whole_s, order_s, sems):
    size = low_ref.shape[0]
    share = w_ref.shape[0]
    parts = share // size
    begin = pl.multiple_of(flags[1] * size, size)

    @pl.when(flags[0] == 0)
    def _():
        part = whole_s.at[pl.ds(0, size)]
        copy = pltpu.make_async_copy(w_ref.at[pl.ds(begin, size)], part, sems.at[0])
        copy.start()
        copy.wait()
        low_ref[...] = part[...].astype(BF)

    @pl.when(flags[0] == 1)
    def _():
        copy = pltpu.make_async_copy(w_ref, whole_s, sems.at[1])
        copy.start()
        copy.wait()
        for lane in range(order_s.shape[0]):
            lanes = slice(lane * 128, (lane + 1) * 128)
            order_s[lane] = whole_s[:, lanes]
            if parts == 4:
                low_ref[:, lanes] = order_s[lane, pl.ds(flags[1], size, stride=4), :].astype(BF)
            else:
                for number in range(4):
                    rows = slice(number * share // 4, (number + 1) * share // 4)
                    low_ref[rows, lanes] = order_s[lane, pl.ds(number, share // 4, stride=4), :].astype(BF)


def adam(chunk, blocks, flags, *refs):
    parts = refs[: 3 * blocks]
    w_ref, state_ref = refs[3 * blocks : 3 * blocks + 2]
    new_ref, upper_ref, lower_ref, g_s, order_s, three_s, sems = refs[-7:]
    share, span = w_ref.shape
    part = share // 4
    lanes = pl.ds(chunk * span, span)
    for block in range(blocks):

        @pl.when(flags[0] == block)
        def _(block=block):
            for number in range(3):
                source = parts[3 * block + number]
                source = source if source.shape[1] == span else source.at[:, lanes]
                pltpu.make_async_copy(source, three_s.at[number], sems.at[number]).start()

    for number in range(3):
        pltpu.make_async_copy(three_s.at[number], three_s.at[number], sems.at[number]).wait()
    g_s[...] = three_s[0].astype(F32) + three_s[1].astype(F32) + three_s[2].astype(F32)

    @pl.when(flags[1] == 1)
    def _():
        for lane in range(order_s.shape[0]):
            lanes = slice(lane * 128, (lane + 1) * 128)
            for number in range(4):
                order_s[lane, pl.ds(number, part, stride=4), :] = g_s[number * part : (number + 1) * part, lanes]
            g_s[:, lanes] = order_s[lane]

    moment, second, delta = inner_update(w_ref[...], g_s[...], state_ref[0, 0], state_ref[0, 1], decay_rate)
    new_ref[0, 0] = moment
    new_ref[0, 1] = second
    low = delta.astype(BF)
    upper_ref[...] = low[: share // 2]
    lower_ref[...] = low[share // 2 :]


def outer(replicas, one_a, one_b, two_a, two_b, w_ref, mom_ref, *refs):
    out_ref = refs[-1]
    share = w_ref.shape[0] // 2
    for half, (one, two) in enumerate(((one_a, two_a), (one_b, two_b))):
        rows = slice(half * share, (half + 1) * share)
        mean = (one[...].astype(F32) + two[...].astype(F32)) / replicas
        momentum = outer_push * mom_ref[rows, :] + mean
        out_ref[0, rows, :] = w_ref[rows, :] - rate_outer * (mean + outer_push * momentum)
        out_ref[1, rows, :] = mean
        out_ref[2, rows, :] = momentum


VM = pl.BlockSpec(memory_space=pltpu.VMEM)
SM = pl.BlockSpec(memory_space=pltpu.SMEM)
HB = pl.BlockSpec(memory_space=pl.ANY)
FAR = pl.BlockSpec(memory_space=pltpu.HBM)


def call(body, name, ins, outs, scratch=(), places=None, grid=(), aliases=None, room=12):
    shapes = tuple(jax.ShapeDtypeStruct(shape, kind) for shape, kind in outs)
    return pl.pallas_call(
        body,
        name=name,
        grid=grid,
        cost_estimate=pl.CostEstimate(flops=0, transcendentals=0, bytes_accessed=0),
        input_output_aliases=aliases or {},
        out_shape=shapes,
        in_specs=ins,
        out_specs=tuple(places or [VM] * len(outs)),
        scratch_shapes=[item if not isinstance(item, tuple) else pltpu.VMEM(*item) for item in scratch],
        compiler_params=pltpu.CompilerParams(vmem_limit_bytes=room << 20),
    )


def inner_update(weight, gradient, moment_one, second, shrink):
    moment_new = beta_first * moment_one + (1.0 - beta_first) * gradient
    second_new = beta_second * second + (1.0 - beta_second) * gradient * gradient
    moment_hat = moment_new / (1.0 - beta_first**STEP)
    second_hat = second_new / (1.0 - beta_second**STEP)
    local_weight = weight - rate_inner * (
        moment_hat / (jnp.sqrt(second_hat) + adam_epsilon) + shrink * weight
    )
    return (moment_new, second_new, weight - local_weight)


def swap(values, axis, bit):
    count = lax.axis_size(axis)
    return lax.ppermute(values, axis, [(i, i ^ bit) for i in range(count)])


def total_over(values, axis):
    count = lax.axis_size(axis)
    if count & (count - 1):
        return lax.psum(values, axis)
    bit = 1
    while bit < count:
        values = values + swap(values, axis, bit)
        bit *= 2
    return values


def hop(values, *moves):
    return lax.ppermute(values, "fsdp", [(2 * one + core, 2 * two + core) for one, two in moves for core in range(2)])


def add_low(one, two):
    return (one.astype(F32) + two.astype(F32)).astype(BF)


def cycle(values, distance):
    count = lax.axis_size("fsdp")
    return lax.ppermute(values, "fsdp", [((to + 2 * distance) % count, to) for to in range(count)])


def around(piece):
    return [piece] + [swap(piece, "rep", distance) for distance in (1, 2, 3)]


def with_other(quarters):
    return quarters + [swap(quarter, "fsdp", 1) for quarter in quarters]


def gather_pieces(piece, vectors, x):
    chip = lax.axis_index("fsdp") // 2
    vectors = vectors + swap(vectors, "fsdp", 1)
    slots = [piece] + [cycle(piece, distance) for distance in (1, 2, 3)]
    vectors = vectors + swap(vectors, "fsdp", 2)
    slots, vectors, x = lax.optimization_barrier((slots, vectors, x))
    pieces = [lax.select_n((block - chip) % 4, *slots) for block in range(4)]
    return pieces, vectors + swap(vectors, "fsdp", 4), x


def per_device(embed, first_tokens, sample_tokens, seq_len, mem_len, memory, cotangent, params, vecs, inner_state, inner_vecs, outer_mom, outer_vecs):
    groups = lax.axis_size("fsdp")
    replicas = lax.axis_size("rep")
    direct = groups == 8 and replicas == 4
    share, width = params.shape
    hidden = 4 * width
    me = lax.axis_index("fsdp")
    chip = me // 2
    own_up = (me >= 2 * hidden // share) & (me < 3 * hidden // share)
    rank = lax.axis_index("rep")
    count, columns = vecs.shape
    vectors = lax.dynamic_update_slice(jnp.zeros((16, width), BF), vecs.astype(BF), (0, me * columns))
    (low,) = call(
        prepare, "prepare", [SM, FAR], [((share // 4 if direct else share, width), BF)],
        [((share, width), F32), ((width // 128, share, 128), F32), pltpu.SemaphoreType.DMA((2,))],
    )(jnp.stack([own_up, rank if direct else 0]).astype(jnp.int32), params)
    x = embed[jnp.concatenate([first_tokens[0], sample_tokens[0]])]
    if direct:
        pieces, vectors, x = gather_pieces(low, vectors, x)
        core = me % 2
        w_self = with_other(around(pieces[0]))
        w_cross = around(pieces[1])
    else:
        w_self = w_cross = w_feed = [lax.all_gather(low, "fsdp", axis=0, tiled=True)]
        vectors = total_over(vectors, "fsdp")
        core = 0
    vectors = vectors.astype(F32)
    lens = jnp.stack([seq_len[0], mem_len[0], core, chip, rank]).astype(jnp.int32)
    many = len(w_self)
    far_w = [FAR if many == 1 else VM] * many
    length = first_tokens.shape[1]
    rows = PASSES * length
    cot = cotangent.reshape(rows, width)
    memory = memory[0]
    slots = memory.shape[0]

    heads_n = ((HEADS, AUG, rows), BF)
    heads_m = ((HEADS, AUG, slots), BF)
    flat_n = ((width, rows), BF)
    flat_m = ((width, slots), BF)
    full = ((rows, width), F32)
    half_g = ((hidden // 2, width), BF)
    block_w = ((hidden, width), BF)
    vec_g = ((16, width), F32)
    peak = ((8, length), F32)
    sems = pltpu.SemaphoreType.DMA((2,))
    qs, ks, vs, o_self, h, weights_self = call(
        functools.partial(self_forward, many), "self_forward", [SM] + far_w + [VM] * 2,
        [heads_n, heads_n, heads_n, flat_n, full, block_w],
        [((length, length), F32)] * 2 + [peak] * 2 + [sems],
    )(lens, *w_self, x, vectors)
    if direct:
        h, w_cross = lax.optimization_barrier((h, w_cross))
        w_cross = with_other(w_cross)
        w_feed = around(jnp.stack(pieces[2:]))
    qc, kc, vc, o_cross, h2, weights_cross = call(
        functools.partial(cross_forward, many), "cross_forward", [SM] + far_w + [VM] * 3,
        [heads_n, heads_m, heads_m, flat_n, full, block_w],
        [((slots, length), F32)] * 2 + [peak] * 2 + [sems],
    )(lens, *w_cross, h, memory, vectors)
    if direct:
        h2, w_feed = lax.optimization_barrier((h2, w_feed))
        w_feed = with_other(w_feed)
    pair_g = ((2, hidden // 2, width), BF)
    y, dh2, feed_near, feed_far, gv3 = call(
        functools.partial(feed, hidden // min(share, hidden), many), "feed", [SM] + far_w + [VM] * 3,
        [((rows, width), BF), full, pair_g, pair_g, vec_g],
        [((4, width, width), BF), ((rows, width), BF), full, full, full, block_w, ((2, 2, hidden // 2, width), BF), sems],
        [VM, VM, HB, HB, VM], room=26,
    )(lens, *w_feed, h2, vectors, cot)
    if direct:
        feed_got = swap(feed_far, "fsdp", 1)
    do_cross, g_out = call(
        cross_start, "cross_start", [VM] * 3, [heads_n, ((width, width), BF)],
    )(weights_cross, dh2, o_cross)
    if direct:
        up_sum, down_sum = add_low(feed_near[0], feed_got[0]), add_low(feed_near[1], feed_got[1])
        do_cross, up_sum, down_sum = lax.optimization_barrier((do_cross, up_sum, down_sum))
        up_got = hop(up_sum, (0, 1), (3, 2))
    dqt, dkt, dvt = call(
        cross_attend, "cross_attend", [VM] * 4, [flat_n, flat_m, flat_m], [((64, slots), F32)] * 2,
    )(qc, kc, vc, do_cross)
    if direct:
        dqt, up_got = lax.optimization_barrier((dqt, up_got))
    cross_near, cross_far, dh, gv2 = call(
        cross_finish, "cross_finish", [SM] + [VM] * 9,
        [half_g, half_g, full, vec_g],
        [pair_g, sems],
        [HB, HB, VM, VM],
    )(lens, weights_cross, dh2, dqt, dkt, dvt, g_out, h, memory, vectors)
    if direct:
        cross_got = swap(cross_far, "fsdp", 1)
    (g_mem,) = call(
        memory_finish, "memory_finish", [VM] * 3, [(memory.shape, F32)],
    )(weights_cross, dkt, dvt)
    chunks = 2
    span = width // chunks
    chunk_g = ((hidden // 2, span), BF)
    if direct:
        cross_sum = add_low(cross_near, cross_got)
        dh, g_mem, cross_sum, up_got, down_sum = lax.optimization_barrier((dh, g_mem, cross_sum, up_got, down_sum))
        cross_hop = hop(cross_sum, (3, 2))
        down_got = hop(down_sum, (0, 1), (2, 3))
        up_late = add_low(up_sum, up_got)
        dh, up_late = lax.optimization_barrier((dh, up_late))
        up_last = hop(up_late, (1, 2))

    def chunk_of(chunk):
        heads = [pl.BlockSpec((HEADS // chunks, AUG, rows), lambda i: (chunk, 0, 0))] * 3
        return call(
            functools.partial(self_backward, chunk, chunks), "self_backward", [SM] + [VM] * 2 + heads + [VM] * 3,
            [chunk_g, chunk_g] + [((span, rows), BF)] * 3,
            [((HEADS // chunks, AUG, rows), BF), ((2, hidden // 2, span), BF), sems],
            [HB, HB, VM, VM, VM], (1,),
        )(lens, weights_self, dh, qs, ks, vs, o_self, x, vectors)

    near_a, far_a, *grads_a = chunk_of(0)
    if direct:
        got_a = swap(far_a, "fsdp", 1)
        dh, grads_a = lax.optimization_barrier((dh, grads_a))
    near_b, far_b, *grads_b = chunk_of(1)
    if direct:
        far_b, up_last, got_a, dh, cross_hop, down_got = lax.optimization_barrier((far_b, up_last, got_a, dh, cross_hop, down_got))
        got_b = swap(far_b, "fsdp", 1)
        sum_a = add_low(near_a, got_a)
        hop_a = hop(sum_a, (1, 0), (3, 2))
        cross_late = add_low(cross_sum, cross_hop)
        cross_last = hop(cross_late, (2, 1))
        cross_side = hop(cross_sum, (0, 1))
        down_late = add_low(down_sum, down_got)
        down_last = hop(down_late, (1, 3))
        sum_b = add_low(near_b, got_b)
        hop_b = hop(sum_b, (1, 0), (3, 2))
        late_a, hop_a, dh = lax.optimization_barrier((add_low(sum_a, hop_a), hop_a, dh))
        last_a = hop(late_a, (2, 0))
    g_in, gv1 = call(
        self_finish, "self_finish", [VM] * 10, [full, vec_g],
    )(weights_self, *grads_a, *grads_b, dh, x, vectors)
    gv = gv1 + gv2 + gv3
    if direct:
        late_b, hop_b, gv, g_in = lax.optimization_barrier((add_low(sum_b, hop_b), hop_b, gv, g_in))
        last_b = hop(late_b, (2, 0))
        gv = gv + swap(gv, "fsdp", 1)
        last_a, gv = lax.optimization_barrier((last_a, gv))
        gv = gv + swap(gv, "fsdp", 2)
        last_b, gv = lax.optimization_barrier((last_b, gv))
        gv = gv + swap(gv, "fsdp", 4)
        grad_v = lax.dynamic_slice(gv, (0, me * columns), (count, columns))
        cross = (cross_sum, cross_side, cross_last)
        feeds = [(up_sum, up_got, up_last), (down_sum, down_got, down_last)]
        parts = [[first, cross, *feeds] for first in ((sum_a, hop_a, last_a), (sum_b, hop_b, last_b))]
        block = chip
    else:
        whole = [jnp.concatenate([near_a, near_b], axis=1), jnp.concatenate([far_a, far_b], axis=1), cross_near, cross_far]
        whole += [feed_near[0], feed_far[0], feed_near[1], feed_far[1]]
        rest = lax.psum_scatter(jnp.concatenate(whole), "fsdp", scatter_dimension=0, tiled=True)
        parts = [[[rest, jnp.zeros_like(rest), jnp.zeros_like(rest)]]] * chunks
        block = 0
        grad_v = lax.dynamic_slice(total_over(gv, "fsdp"), (0, me * columns), (count, columns))
    flags = jnp.stack([block, own_up]).astype(jnp.int32)
    inner_new = param_results = None
    deltas = []
    for chunk in range(chunks):
        lanes = pl.BlockSpec((share, span), lambda i, c=chunk: (0, c))
        taken = [item for three in parts[chunk] for item in three]
        part = pl.BlockSpec((share // 2, span), lambda i: (0, 0))
        state = pl.BlockSpec((1, 2, share, span), lambda i, c=chunk: (0, 0, 0, c))
        inner_new, upper, lower = call(
            functools.partial(adam, chunk, len(parts[chunk])), "adam", [SM] + [FAR] * len(taken) + [lanes, state] + [HB] * min(chunk, 1),
            [(inner_state.shape, F32)] + [((share // 2, span), BF)] * 2,
            [((share, span), F32), ((span // 128, share, 128), F32), ((3, share, span), BF), pltpu.SemaphoreType.DMA((3,))],
            [state, part, part], (1,), {len(taken) + 3: 0} if chunk else None, 16,
        )(flags, *taken, params, inner_state, *([inner_new] if chunk else []))
        deltas.append((upper, lower))
    for chunk, (upper, lower) in enumerate(deltas):
        if replicas == 4:
            upper = add_low(upper, swap(upper, "rep", 1))
            lower = add_low(lower, swap(lower, "rep", 2))
            others = [swap(upper, "rep", 2), swap(lower, "rep", 1)]
        else:
            upper, lower = lax.psum(upper, "rep"), lax.psum(lower, "rep")
            others = [jnp.zeros_like(upper), jnp.zeros_like(lower)]
        lanes = pl.BlockSpec((share, span), lambda i, c=chunk: (0, c))
        part = pl.BlockSpec((share // 2, span), lambda i: (0, 0))
        (param_results,) = call(
            functools.partial(outer, replicas), "outer", [part] * 4 + [lanes, lanes] + [HB] * min(chunk, 1),
            [((3, share, width), F32)], (),
            [pl.BlockSpec((3, share, span), lambda i, c=chunk: (0, 0, c))], (1,), {6: 0} if chunk else None,
        )(upper, lower, *others, params, outer_mom, *([param_results] if chunk else []))
    moment_v, second_v, delta_v = inner_update(vecs, grad_v, inner_vecs[0, 0], inner_vecs[0, 1], 0.0)
    if replicas == 4:
        low_v = delta_v.astype(BF)
        mean_v = sum([swap(low_v, "rep", bit).astype(F32) for bit in (1, 2, 3)], low_v.astype(F32)) / replicas
    else:
        mean_v = lax.psum(delta_v.astype(BF), "rep").astype(F32) / replicas
    momentum_v = outer_push * outer_vecs + mean_v
    new_v = vecs - rate_outer * (mean_v + outer_push * momentum_v)
    return (
        y.reshape(PASSES, 1, length, width),
        g_in.reshape(PASSES, 1, length, width),
        g_mem[None],
        param_results,
        jnp.stack([new_v, mean_v, momentum_v]),
        inner_new,
        jnp.stack([moment_v, second_v])[None],
    )


def solution(mesh):
    both = ("rep", "fsdp")
    return jax.shard_map(
        per_device,
        mesh=mesh,
        in_specs=(
            P(),
            P(both, None),
            P(both, None),
            P(both),
            P(both),
            P(both, None, None),
            P(None, both, None, None),
            P("fsdp", None),
            P(None, "fsdp"),
            P("rep", None, "fsdp", None),
            P("rep", None, None, "fsdp"),
            P("fsdp", None),
            P(None, "fsdp"),
        ),
        out_specs=(
            P(None, both, None, None),
            P(None, both, None, None),
            P(both, None, None),
            P(None, "fsdp", None),
            P(None, None, "fsdp"),
            P("rep", None, "fsdp", None),
            P("rep", None, None, "fsdp"),
        ),
        check_vma=False,
    )
```
